32 devices in a mesh: dp: 8 (over z, y), tensor: 4 (over x, core).
Axes of the slice: x: 2, y: 2, z: 4, core: 2. Of those that a mesh axis runs over, the one named last changes fastest.
Arguments:
- inputs: bfloat16 [4096, 768], P(('dp', 'tensor')), may hold values from -6 to 6
- prev_logits: bfloat16 [4096, 12, 4096], P('dp', 'tensor'), may hold values from -6 to 6
- w_query: bfloat16 [768, 768], P('dp', 'tensor'), may hold values from -0.21875 to 0.21875
- w_key: bfloat16 [768, 768], P('dp', 'tensor'), may hold values from -0.21875 to 0.21875
- w_value: bfloat16 [768, 768], P('dp', 'tensor'), may hold values from -0.21875 to 0.21875
- w_attn_out: bfloat16 [768, 768], P('tensor', 'dp'), may hold values from -2.5 to 2.5
- w_ffn_in: bfloat16 [768, 3072], P('dp', 'tensor'), may hold values from -0.21875 to 0.21875
- ffn_bias: bfloat16 [3072], P(('tensor', 'dp')), may hold values from -3 to 3
- w_ffn_out: bfloat16 [3072, 768], P(('tensor', 'dp')), may hold values from -0.109375 to 0.109375
- norm1_gain: float32 [768], replicated, may hold values from 0.5 to 1.5
- norm1_shift: float32 [768], replicated, may hold values from -2 to 2
- norm2_gain: float32 [768], replicated, may hold values from 0.5 to 1.5
- norm2_shift: float32 [768], replicated, may hold values from -2 to 2
- token_segment: int32 [4096], replicated, may hold values from 0 to 12, as said below
- segment_parent: int32 [1, 13], replicated, may hold values from 0 to 4, as said below
- out_grad: bfloat16 [4096, 768], P(('dp', 'tensor')), may hold values from -6 to 6
- logit_grad: bfloat16 [4096, 12, 4096], P('dp', 'tensor'), may hold values from -6 to 6
Outputs:
- output: bfloat16 [4096, 768], P(('dp', 'tensor'))
- logits: bfloat16 [4096, 12, 4096], P('dp', 'tensor')
- input_grad: float32 [4096, 768], P(('dp', 'tensor'))
- prev_grad: bfloat16 [4096, 12, 4096], P('dp', 'tensor')
- w_query_grad: float32 [768, 768], P('dp', 'tensor')
- w_key_grad: float32 [768, 768], P('dp', 'tensor')
- w_value_grad: float32 [768, 768], P('dp', 'tensor')
- w_attn_out_grad: float32 [768, 768], P('tensor', 'dp')
- w_ffn_in_grad: float32 [768, 3072], P('dp', 'tensor')
- ffn_bias_grad: float32 [3072], P(('tensor', 'dp'))
- w_ffn_out_grad: float32 [3072, 768], P(('tensor', 'dp'))
- norm1_gain_grad: float32 [768], replicated
- norm1_shift_grad: float32 [768], replicated
- norm2_gain_grad: float32 [768], replicated
- norm2_shift_grad: float32 [768], replicated
The draws below stay inside these ranges and needn't reach their ends.
Inputs may be any that keep to these rules, and one draw needn't show every extreme that they name: `token_segment`: in each tree the first 2048 tokens are segment 0, the trunk; the other tokens hold the 4 branches (segments 1 to 4, 256 tokens each) and the 8 leaves (segments 5 to 12, 128 tokens each), each segment one contiguous run, in an order that varies from tree to tree. `segment_parent`: row t lists the parents of tree t's segments: 0 for the trunk and every branch, a branch for every leaf, each branch the parent of exactly two leaves.
All inputs are finite; a program needn't handle non-finite values.
Results may differ from the reference program's by a relative error of at most 0.017.
Values may be sent and summed in bfloat16 or wider, within the bound.
No kernel may reach another device: no remote copies, remote signals or barrier semaphores. Data moves between devices by JAX's collectives and lax.ppermute only.
A program may use at most 256 MiB of HBM per device.

```python
import jax
import jax.numpy as jnp
from jax import lax

D = 768
H = 12
E = 64
FF = 3072
TRUNK = 2048
BRANCH = 256
LEAF = 128
NB = 4
TREE = 4096
TOKENS = 4096
TREES = 1


def draw_token_segment(key, part):
    tree_keys = jax.random.split(jax.random.fold_in(key, 11), TREES)

    def one_tree(tree_key):
        segment_order = (jax.random.permutation(tree_key, 3 * NB) + 1).astype(jnp.int32)
        run_lengths = jnp.where(segment_order <= NB, BRANCH, LEAF).astype(jnp.int32)
        run_ends = TRUNK + jnp.cumsum(run_lengths)
        position = jnp.arange(TREE, dtype=jnp.int32)
        run_index = jnp.sum((position[:, None] >= run_ends[None, :]).astype(jnp.int32), axis=1)
        run_picks = (run_index[:, None] == jnp.arange(3 * NB, dtype=jnp.int32)[None, :]).astype(jnp.int32)
        run_label = jnp.sum(run_picks * segment_order[None, :], axis=1)
        return jnp.where(position < TRUNK, 0, run_label).astype(jnp.int32)
    return jax.vmap(one_tree)(tree_keys).reshape(TOKENS)


def draw_segment_parent(key, part):
    tree_keys = jax.random.split(jax.random.fold_in(key, 23), TREES)

    def one_tree(tree_key):
        leaves = jax.random.permutation(tree_key, 2 * NB).astype(jnp.int32)
        fixed_head = jnp.zeros((1 + NB,), jnp.int32)
        return jnp.concatenate([fixed_head, (1 + leaves // 2).astype(jnp.int32)])
    return jax.vmap(one_tree)(tree_keys)


def shard_levels(key, shape, cuts, least, largest):
    level = 1.0
    for dim, shards_of in cuts:
        steps = jax.random.uniform(jax.random.fold_in(jax.random.fold_in(key, 6), dim), (shards_of,), jnp.float32, least / len(cuts), largest / len(cuts))
        level = level * jnp.repeat(jnp.exp(steps), shape[dim] // shards_of).reshape((-1,) + (1,) * (len(shape) - 1 - dim))
    return level


def noise(own_key, dims, scale, most, shards=(), kind=jnp.bfloat16):
    entries = jax.random.normal(own_key, dims, jnp.float32) * scale
    if len(shards) > 0:
        entries = shard_levels(own_key, dims, shards, -0.22, 0.18) * entries
    return jnp.clip(entries, min=-most, max=most).astype(kind)


def setup_inputs(seed: int = 0) -> dict:
    arg_keys = jax.random.split(jax.random.key(seed), 18)
    inputs = noise(arg_keys[0], (TOKENS, D), 1.0, 6.0, ((0, 32),))
    prev_logits = noise(arg_keys[1], (TOKENS, H, TREE), 1.0, 6.0, ((0, 8), (1, 4)))
    w_query = noise(arg_keys[2], (D, D), D ** -0.5, 0.21875, ((0, 8), (1, 4)))
    w_key = noise(arg_keys[3], (D, D), D ** -0.5, 0.21875, ((0, 8), (1, 4)))
    w_value = noise(arg_keys[4], (D, D), D ** -0.5, 0.21875, ((0, 8), (1, 4)))
    w_attn_out = noise(arg_keys[5], (D, D), (D // 128) ** -0.5, 2.5, ((0, 4), (1, 8)))
    w_ffn_in = noise(arg_keys[6], (D, FF), D ** -0.5, 0.21875, ((0, 8), (1, 4)))
    ffn_bias = noise(arg_keys[7], (FF,), 0.5, 3.0, ((0, 32),))
    w_ffn_out = noise(arg_keys[8], (FF, D), FF ** -0.5, 0.109375, ((0, 32),))
    norm1_gain = jnp.clip(1.0 + 0.1 * jax.random.normal(arg_keys[9], (D,), jnp.float32), 0.5, 1.5)
    norm1_shift = noise(arg_keys[10], (D,), 0.3, 2.0, (), jnp.float32)
    norm2_gain = jnp.clip(1.0 + 0.1 * jax.random.normal(arg_keys[11], (D,), jnp.float32), 0.5, 1.5)
    norm2_shift = noise(arg_keys[12], (D,), 0.3, 2.0, (), jnp.float32)
    token_segment = draw_token_segment(jax.random.fold_in(arg_keys[17], 71), 0)
    segment_parent = draw_segment_parent(jax.random.fold_in(arg_keys[17], 71), 0)
    out_grad = noise(arg_keys[15], (TOKENS, D), 1.0, 6.0, ((0, 32),))
    logit_grad = noise(arg_keys[16], (TOKENS, H, TREE), 1.0, 6.0, ((0, 8), (1, 4)))
    return {"inputs": inputs, "prev_logits": prev_logits, "w_query": w_query, "w_key": w_key, "w_value": w_value, "w_attn_out": w_attn_out, "w_ffn_in": w_ffn_in, "ffn_bias": ffn_bias, "w_ffn_out": w_ffn_out, "norm1_gain": norm1_gain, "norm1_shift": norm1_shift, "norm2_gain": norm2_gain, "norm2_shift": norm2_shift, "token_segment": token_segment, "segment_parent": segment_parent, "out_grad": out_grad, "logit_grad": logit_grad}


@jax.custom_vjp
def low(v):
    return lax.optimization_barrier(v.astype(jnp.bfloat16)).astype(jnp.float32)

@jax.custom_vjp
def low_back(v):
    return v

def low_keep(v):
    return (low(v), None)

def low_pass(kept, grad):
    return (grad,)

def back_keep(v):
    return (v, None)

def back_low(kept, grad):
    return (low(grad),)
low.defvjp(low_keep, low_pass)
low_back.defvjp(back_keep, back_low)
HIGH = lax.Precision.HIGHEST
EPSILON = 1e-12

def product(factor_one, factor_two):
    return jnp.dot(factor_one, factor_two, precision=HIGH, preferred_element_type=jnp.float32)

def layer_norm(values, norm_gain, norm_shift):
    center = values - lax.optimization_barrier(jnp.mean(values, axis=-1, keepdims=True))
    spread = lax.optimization_barrier(jnp.mean(center * center, axis=-1, keepdims=True))
    return center * lax.rsqrt(spread + EPSILON) * norm_gain + norm_shift

def path_mask(seg_tree, parents):
    parent_one = parents[seg_tree]
    parent_two = parents[parent_one]
    key_labels = seg_tree[None, :]
    return (key_labels == seg_tree[:, None]) | (key_labels == parent_one[:, None]) | (key_labels == parent_two[:, None])

def tree_attention(query, key_rows, value_rows, previous, seg_tree, parents):
    score_scale = E ** (-0.5)
    query_heads = query.reshape(TREE, H, E)
    key_heads = key_rows.reshape(TREE, H, E)
    value_heads = value_rows.reshape(TREE, H, E)
    scores = jnp.einsum('qhe,khe->qhk', query_heads, key_heads, precision=HIGH) * score_scale + previous
    scores = low_back(scores)
    allowed = path_mask(seg_tree, parents)[:, None, :]
    logits = jnp.where(allowed, scores, 0.0)
    masked = jnp.where(allowed, scores, -jnp.inf)
    row_max = lax.optimization_barrier(jnp.max(masked, axis=-1, keepdims=True))
    exponent = jnp.exp(masked - row_max)
    weights = exponent / lax.optimization_barrier(jnp.sum(exponent, axis=-1, keepdims=True))
    mixed = jnp.einsum('qhk,khe->qhe', low(weights), value_heads, precision=HIGH)
    return (low_back(low(mixed.reshape(TREE, D))), logits)

def tree_block(pieces):
    return tree_attention(pieces[0], pieces[1], pieces[2], pieces[3], pieces[4], pieces[5])

def layer(inputs, previous, w_query, w_key, w_value, w_attn_out, w_ffn_in, ffn_bias, w_ffn_out, norm1_gain, norm1_shift, norm2_gain, norm2_shift, token_segment, segment_parent):
    query = low_back(low(product(inputs, w_query)))
    key_rows = low_back(low(product(inputs, w_key)))
    value_rows = low_back(low(product(inputs, w_value)))
    blocks = (query.reshape(TREES, TREE, D), key_rows.reshape(TREES, TREE, D), value_rows.reshape(TREES, TREE, D), previous.reshape(TREES, TREE, H, TREE), token_segment.reshape(TREES, TREE), segment_parent)
    mixed, logits = lax.map(jax.checkpoint(tree_block), blocks)
    mixed = mixed.reshape(TOKENS, D)
    logits = logits.reshape(TOKENS, H, TREE)
    attended = low_back(product(mixed, w_attn_out))
    hidden = layer_norm(inputs + attended, norm1_gain, norm1_shift)
    inner = low_back(product(low(hidden), w_ffn_in) + ffn_bias)
    active = low_back(low(jax.nn.gelu(inner, approximate=False)))
    ffn_out = low_back(product(active, w_ffn_out))
    result = layer_norm(hidden + ffn_out, norm2_gain, norm2_shift)
    return (result, logits)

def reference(inputs, prev_logits, w_query, w_key, w_value, w_attn_out, w_ffn_in, ffn_bias, w_ffn_out, norm1_gain, norm1_shift, norm2_gain, norm2_shift, token_segment, segment_parent, out_grad, logit_grad):
    floats = tuple((v.astype(jnp.float32) for v in (inputs, prev_logits, w_query, w_key, w_value, w_attn_out, w_ffn_in, ffn_bias, w_ffn_out, norm1_gain, norm1_shift, norm2_gain, norm2_shift)))

    def forward(*values):
        return layer(*values, token_segment, segment_parent)
    (result, logits), pullback = jax.vjp(forward, *floats)
    grads = pullback((out_grad.astype(jnp.float32), logit_grad.astype(jnp.float32)))
    return (result.astype(jnp.bfloat16), logits.astype(jnp.bfloat16), grads[0], grads[1].astype(jnp.bfloat16), grads[2], grads[3], grads[4], grads[5], grads[6], grads[7], grads[8], grads[9], grads[10], grads[11], grads[12])
```

```python
import functools

import jax
import jax.numpy as jnp
from jax import lax
from jax.experimental import pallas as pl
from jax.experimental.pallas import tpu as pltpu
from jax.sharding import PartitionSpec as P

E = 64
TRUNK = 2048
BLOCK = 128
EPSILON = 1e-12
LOW = -1e30

BF = jnp.bfloat16
F32 = jnp.float32


def layer_norm(values, norm_gain, norm_shift):
    center = values - jnp.mean(values, axis=-1, keepdims=True)
    spread = jnp.mean(center * center, axis=-1, keepdims=True)
    return center * lax.rsqrt(spread + EPSILON) * norm_gain + norm_shift


def contract(a, b, da, db):
    return lax.dot_general(a, b, (((da,), (db,)), ((), ())), preferred_element_type=F32)


def forward_kernel(sid_ref, rid_ref, act_ref, q_ref, kv_ref, prev_ref, logit_ref, mix_ref, aux_ref, m_s, l_s, acc_s, q_s):
    j = pl.program_id(1)
    rows = prev_ref.shape[1]
    nb = rows // BLOCK
    chunk = min(256, rows)
    total_blocks = act_ref.shape[0] // nb
    shard = sid_ref[j]

    @pl.when(j == 0)
    def _():
        m_s[...] = jnp.full(m_s.shape, LOW, F32)
        l_s[...] = jnp.zeros(l_s.shape, F32)
        acc_s[...] = jnp.zeros(acc_s.shape, F32)
        q_s[...] = q_ref[...].astype(F32).T.astype(BF)

    def update(r0, count, s, vt):
        rs = pl.ds(r0, count)
        m_old = m_s[rs, :]
        m_new = jnp.maximum(m_old, jnp.max(s, axis=1, keepdims=True))
        p = jnp.exp(s - m_new)
        fix = jnp.exp(m_old - m_new)
        m_s[rs, :] = m_new
        l_s[rs, :] = l_s[rs, :] * fix + jnp.sum(p, axis=1, keepdims=True)
        acc_s[rs, :] = acc_s[rs, :] * fix + contract(p.astype(BF), vt, 1, 1)

    dense = (shard + 1) * rows <= TRUNK

    @pl.when(dense)
    def _():
        for r0 in range(0, rows, chunk):
            s = contract(q_s[r0 : r0 + chunk, :], kv_ref[0, 0], 1, 0)
            s = s + prev_ref[0, r0 : r0 + chunk, :].astype(F32)
            logit_ref[0, r0 : r0 + chunk, :] = s.astype(BF)
            update(r0, chunk, s, kv_ref[0, 1])

    @pl.when(jnp.logical_not(dense))
    def _():
        logit_ref[...] = jnp.zeros(logit_ref.shape, BF)
        for qi in range(nb):
            for ki in range(nb):

                @pl.when(act_ref[qi * total_blocks + shard * nb + ki] == 1)
                def _(qi=qi, ki=ki):
                    r0, c0 = qi * BLOCK, ki * BLOCK
                    s = contract(q_s[r0 : r0 + BLOCK, :], kv_ref[0, 0, :, c0 : c0 + BLOCK], 1, 0)
                    s = s + prev_ref[0, r0 : r0 + BLOCK, c0 : c0 + BLOCK].astype(F32)
                    logit_ref[0, r0 : r0 + BLOCK, c0 : c0 + BLOCK] = s.astype(BF)
                    update(r0, BLOCK, s, kv_ref[0, 1, :, c0 : c0 + BLOCK])

    @pl.when(j == pl.num_programs(1) - 1)
    def _():
        out = acc_s[...] / l_s[...]
        mix_ref[...] = out.T.astype(BF)
        aux_ref[0, :, :E] = out
        aux_ref[0, :, E:] = jnp.broadcast_to(m_s[...] + jnp.log(l_s[...]), (rows, 128 - E))


def attend_forward(sid, rid, act, q_t, kv, prev):
    heads, rows, length = prev.shape
    pieces = kv.shape[0]
    return pl.pallas_call(
        forward_kernel,
        out_shape=(
            jax.ShapeDtypeStruct((heads, rows, length), BF),
            jax.ShapeDtypeStruct((heads * E, rows), BF),
            jax.ShapeDtypeStruct((heads, rows, 128), F32),
        ),
        grid_spec=pltpu.PrefetchScalarGridSpec(
            num_scalar_prefetch=3,
            grid=(heads, pieces),
            in_specs=[
                pl.BlockSpec((E, rows), lambda h, j, s, r, a: (h, 0)),
                pl.BlockSpec((1, 2, E, rows), lambda h, j, s, r, a: (j, 0, h, 0)),
                pl.BlockSpec((1, rows, rows), lambda h, j, s, r, a: (h, 0, r[j])),
            ],
            out_specs=[
                pl.BlockSpec((1, rows, rows), lambda h, j, s, r, a: (h, 0, s[j])),
                pl.BlockSpec((E, rows), lambda h, j, s, r, a: (h, 0)),
                pl.BlockSpec((1, rows, 128), lambda h, j, s, r, a: (h, 0, 0)),
            ],
            scratch_shapes=[
                pltpu.VMEM((rows, 1), F32),
                pltpu.VMEM((rows, 1), F32),
                pltpu.VMEM((rows, E), F32),
                pltpu.VMEM((rows, E), BF),
            ],
        ),
        compiler_params=pltpu.CompilerParams(dimension_semantics=("arbitrary", "arbitrary")),
    )(sid, rid, act, q_t, kv, prev)


def backward_kernel(sid_ref, rid_ref, act_ref, q_ref, kv_ref, prev_ref, up_ref, aux_ref, do_ref, pg_ref, gkv_ref, gq_ref, q_s, do_s, d_s, lse_s, gq_s, p_s):
    j = pl.program_id(1)
    rows = prev_ref.shape[1]
    nb = rows // BLOCK
    chunk = min(256, rows)
    total_blocks = act_ref.shape[0] // nb
    shard = sid_ref[j]

    @pl.when(j == 0)
    def _():
        q_s[...] = q_ref[...].astype(F32).T.astype(BF)
        do = do_ref[...].astype(F32).T
        do_s[...] = do.astype(BF)
        d_s[...] = jnp.sum(do * aux_ref[0, :, :E], axis=1, keepdims=True)
        lse_s[...] = aux_ref[0, :, E : E + 1]
        gq_s[...] = jnp.zeros(gq_s.shape, F32)

    def fill(r0, count, c0, width):
        rs, cs = slice(r0, r0 + count), slice(c0, c0 + width)
        s = contract(q_s[rs, :], kv_ref[0, 0, :, cs], 1, 0) + prev_ref[0, rs, cs].astype(F32)
        p = jnp.exp(s - lse_s[rs, :])
        dp = contract(do_s[rs, :], kv_ref[0, 1, :, cs], 1, 0)
        ds = p * (dp - d_s[rs, :]) + up_ref[0, rs, cs].astype(F32)
        pg_ref[0, rs, cs] = ds.astype(BF)
        p_s[rs, cs] = p.astype(BF)

    def finish():
        gkv_ref[0, 0] = contract(q_ref[...], pg_ref[0], 1, 0).astype(BF)
        gkv_ref[0, 1] = contract(do_ref[...], p_s[...], 1, 0).astype(BF)
        gq_s[...] += contract(pg_ref[0], kv_ref[0, 0], 1, 1)

    dense = (shard + 1) * rows <= TRUNK

    @pl.when(dense)
    def _():
        for r0 in range(0, rows, chunk):
            fill(r0, chunk, 0, rows)
        finish()

    @pl.when(jnp.logical_not(dense))
    def _():
        pg_ref[...] = jnp.zeros(pg_ref.shape, BF)
        some = act_ref[shard * nb]
        for qi in range(nb):
            for ki in range(nb):
                some = jnp.maximum(some, act_ref[qi * total_blocks + shard * nb + ki])

        @pl.when(some == 0)
        def _():
            gkv_ref[...] = jnp.zeros(gkv_ref.shape, BF)

        @pl.when(some == 1)
        def _():
            p_s[...] = jnp.zeros(p_s.shape, BF)
            for qi in range(nb):
                for ki in range(nb):

                    @pl.when(act_ref[qi * total_blocks + shard * nb + ki] == 1)
                    def _(qi=qi, ki=ki):
                        fill(qi * BLOCK, BLOCK, ki * BLOCK, BLOCK)

            finish()

    @pl.when(j == pl.num_programs(1) - 1)
    def _():
        gq_ref[...] = (gq_s[...] * (E ** (-0.5))).T.astype(BF)


def attend_backward(sid, rid, act, q_t, kv, prev, up, aux, do_t):
    heads, rows, length = prev.shape
    pieces = kv.shape[0]
    return pl.pallas_call(
        backward_kernel,
        out_shape=(
            jax.ShapeDtypeStruct((heads, rows, length), BF),
            jax.ShapeDtypeStruct((pieces, 2, heads * E, rows), BF),
            jax.ShapeDtypeStruct((heads * E, rows), BF),
        ),
        grid_spec=pltpu.PrefetchScalarGridSpec(
            num_scalar_prefetch=3,
            grid=(heads, pieces),
            in_specs=[
                pl.BlockSpec((E, rows), lambda h, j, s, r, a: (h, 0)),
                pl.BlockSpec((1, 2, E, rows), lambda h, j, s, r, a: (j, 0, h, 0)),
                pl.BlockSpec((1, rows, rows), lambda h, j, s, r, a: (h, 0, r[j])),
                pl.BlockSpec((1, rows, rows), lambda h, j, s, r, a: (h, 0, r[j])),
                pl.BlockSpec((1, rows, 128), lambda h, j, s, r, a: (h, 0, 0)),
                pl.BlockSpec((E, rows), lambda h, j, s, r, a: (h, 0)),
            ],
            out_specs=[
                pl.BlockSpec((1, rows, rows), lambda h, j, s, r, a: (h, 0, s[j])),
                pl.BlockSpec((1, 2, E, rows), lambda h, j, s, r, a: (j, 0, h, 0)),
                pl.BlockSpec((E, rows), lambda h, j, s, r, a: (h, 0)),
            ],
            scratch_shapes=[
                pltpu.VMEM((rows, E), BF),
                pltpu.VMEM((rows, E), BF),
                pltpu.VMEM((rows, 1), F32),
                pltpu.VMEM((rows, 1), F32),
                pltpu.VMEM((rows, E), F32),
                pltpu.VMEM((rows, rows), BF),
            ],
        ),
        compiler_params=pltpu.CompilerParams(dimension_semantics=("arbitrary", "arbitrary")),
    )(sid, rid, act, q_t, kv, prev, up, aux, do_t)


class Ring:
    def __init__(self, axis, total, size):
        self.axis, self.size = axis, size
        local = list(range(0, size, 2)) + list(range(size - 1 - size % 2, 0, -2))
        self.local = local
        self.up, self.down = [], []
        for base in range(0, total, size):
            for i in range(size):
                a, b = base + local[i], base + local[(i + 1) % size]
                self.up.append((a, b))
                self.down.append((b, a))

    def position(self, index):
        place = [0] * self.size
        for i, v in enumerate(self.local):
            place[v] = i
        return jnp.array(place, jnp.int32)[index % self.size]

    def offsets(self):
        out = [0]
        for k in range(1, self.size // 2):
            out += [-k, k]
        if self.size > 1:
            out.append(-(self.size // 2))
        return out

    def gather(self, x, split):
        pieces = [x]
        up = down = x
        for _ in range(1, self.size // 2):
            up = lax.ppermute(up, self.axis, self.up)
            down = lax.ppermute(down, self.axis, self.down)
            pieces += [up, down]
        if self.size > 1:
            half = x.shape[split] // 2
            a = lax.slice_in_dim(up, 0, half, axis=split)
            b = lax.slice_in_dim(down, half, x.shape[split], axis=split)
            a = lax.ppermute(a, self.axis, self.up)
            b = lax.ppermute(b, self.axis, self.down)
            pieces.append(jnp.concatenate([a, b], axis=split))
        return pieces

    def scatter(self, get):
        n = self.size
        up, down = get(-1 % n, 0), get(1 % n, 1)
        if n == 1:
            return up, down
        for k in range(1, n):
            up = lax.ppermute(up, self.axis, self.up_from())
            down = lax.ppermute(down, self.axis, self.down_from())
            up = (up.astype(F32) + get((-1 - k) % n, 0).astype(F32)).astype(BF)
            down = (down.astype(F32) + get((1 + k) % n, 1).astype(F32)).astype(BF)
        return up, down

    def up_from(self):
        return self.up

    def down_from(self):
        return self.down


def spread_gather(x, axis, n):
    return lax.all_to_all(jnp.broadcast_to(x[None], (n,) + x.shape), axis, 0, 0, tiled=True)


def group_sum(x, axis, n):
    parts = lax.all_to_all(x.reshape(n, x.shape[0] // n, x.shape[1]), axis, 0, 0, tiled=True)
    return jnp.sum(parts.astype(F32), axis=0)


def high_low(x):
    high = x.astype(BF)
    return high, (x - high.astype(F32)).astype(BF)


def shards(
    inputs,
    prev_logits,
    w_query,
    w_key,
    w_value,
    w_attn_out,
    w_ffn_in,
    ffn_bias,
    w_ffn_out,
    norm1_gain,
    norm1_shift,
    norm2_gain,
    norm2_shift,
    token_segment,
    segment_parent,
    out_grad,
    logit_grad,
):
    rows, heads, length = prev_logits.shape
    width = heads * E
    model = inputs.shape[1]
    own = inputs.shape[0]
    spread = length // rows
    nd, nt = lax.axis_size("dp"), lax.axis_size("tensor")
    data_index, tensor_index = lax.axis_index("dp"), lax.axis_index("tensor")
    tree_index, local_index = data_index // spread, data_index % spread
    nb = rows // BLOCK

    pack = jnp.concatenate([w_query, w_key, w_value, w_attn_out.T], axis=1)
    pack = spread_gather(pack, "dp", nd).reshape(model, 4 * width)
    project = pack[:, : 3 * width]
    out_own = pack[:, 3 * width :].T
    out_full = lax.all_gather(out_own, "tensor", axis=0, tiled=True)
    rows_all = lax.all_gather(inputs, "tensor", axis=0, tiled=True)
    w_in = lax.all_gather(w_ffn_in, "dp", axis=0, tiled=True)
    w_out = lax.all_gather(w_ffn_out, "dp", axis=0, tiled=True)
    bias = spread_gather(ffn_bias.reshape(1, -1), "dp", nd).reshape(1, -1).astype(F32)

    seg = lax.dynamic_slice_in_dim(token_segment, tree_index * length, length, 0)[::BLOCK]
    parents = lax.dynamic_slice_in_dim(segment_parent, tree_index, 1, 0)[0]
    seg_rows = lax.dynamic_slice_in_dim(seg, local_index * nb, nb, 0)
    labels = jnp.arange(parents.shape[0], dtype=jnp.int32)
    one = jnp.sum(jnp.where(seg_rows[:, None] == labels[None, :], parents[None, :], 0), axis=1)
    two = jnp.sum(jnp.where(one[:, None] == labels[None, :], parents[None, :], 0), axis=1)
    act = (
        (seg[None, :] == seg_rows[:, None])
        | (seg[None, :] == one[:, None])
        | (seg[None, :] == two[:, None])
    )
    act = act.astype(jnp.int32).reshape(-1)

    projected = contract(project, rows_all, 0, 1)
    q_t = (projected[:width] * (E ** (-0.5))).astype(BF)
    kv_own = projected[width:].astype(BF).reshape(2, width, rows)
    ring = Ring("dp", nd, spread)
    kv = jnp.stack(ring.gather(kv_own, 1), axis=0)
    place = ring.position(local_index)
    offsets = jnp.array(ring.offsets(), jnp.int32)
    local_of = jnp.array(ring.local, jnp.int32)
    sid = local_of[(place + offsets) % spread]

    prev = jnp.transpose(prev_logits, (1, 0, 2))
    up = jnp.transpose(logit_grad, (1, 0, 2))
    logits, mixed, aux = attend_forward(sid, sid, act, q_t, kv, prev)

    mixed_all = lax.all_gather(mixed, "tensor", axis=0, tiled=True)
    attended = contract(mixed_all, out_full, 0, 0)
    first_all = rows_all.astype(F32) + attended
    hidden_all = layer_norm(first_all, norm1_gain, norm1_shift).astype(BF)
    first_sum = lax.dynamic_slice_in_dim(first_all, tensor_index * own, own, 0)
    hidden, norm_one_back = jax.vjp(layer_norm, first_sum, norm1_gain, norm1_shift)

    inner = contract(hidden_all, w_in, 1, 0) + bias
    active, gelu_back = jax.vjp(lambda v: jax.nn.gelu(v, approximate=False), inner)
    active = active.astype(BF)
    ffn_out = group_sum(contract(active, w_out, 1, 0).astype(BF), "tensor", nt)
    result, norm_two_back = jax.vjp(layer_norm, hidden + ffn_out, norm2_gain, norm2_shift)
    grad_second, gain_two, shift_two = norm_two_back(out_grad.astype(F32))
    second_all = lax.all_gather(grad_second.astype(BF), "tensor", axis=0, tiled=True)
    grad_active = contract(second_all, w_out, 1, 1).astype(BF)
    grad_w_out = contract(active, second_all, 0, 0).astype(BF)
    (grad_inner,) = gelu_back(grad_active.astype(F32))
    grad_inner = grad_inner.astype(BF)
    grad_w_in = contract(hidden_all, grad_inner, 0, 0).astype(BF)
    grad_bias = jnp.sum(grad_inner.astype(F32), axis=0)
    grad_hidden = grad_second + group_sum(contract(grad_inner, w_in, 1, 1).astype(BF), "tensor", nt)
    grad_first, gain_one, shift_one = norm_one_back(grad_hidden)
    norms = jnp.stack([gain_one, shift_one, gain_two, shift_two])
    norm_high, norm_low = high_low(norms)
    gathered = lax.all_gather(
        jnp.concatenate([grad_first.astype(BF), norm_high, norm_low], axis=0), "tensor", axis=0
    )
    first_back = gathered[:, :own].reshape(nt * own, model)
    norms = jnp.sum(gathered[:, own:].astype(F32), axis=0)
    norms = norms[:4] + norms[4:]
    grad_mixed = contract(out_own, first_back, 1, 1).astype(BF)
    grad_w_attn = contract(first_back, mixed, 0, 1).astype(BF)
    rest = jnp.concatenate([grad_w_in, grad_w_attn], axis=1)
    rest = lax.psum_scatter(rest, "dp", scatter_dimension=0, tiled=True).astype(F32)
    grad_w_out = lax.psum_scatter(grad_w_out, "dp", scatter_dimension=0, tiled=True).astype(F32)

    prev_grad, grad_kv, grad_query = attend_backward(sid, sid, act, q_t, kv, prev, up, aux, grad_mixed)

    order = {o % spread: i for i, o in enumerate(ring.offsets())}
    half = width // 2

    def part(d, which):
        return grad_kv[order[d], :, which * half : (which + 1) * half]

    top, bottom = ring.scatter(part)
    own_kv = jnp.concatenate([top, bottom], axis=1).reshape(2 * width, rows)
    grad_project = jnp.concatenate([grad_query, own_kv], axis=0)

    input_part = contract(grad_project, project, 0, 1).astype(BF)
    grad_inputs = grad_first + group_sum(input_part, "tensor", nt)
    grad_w_project = contract(rows_all, grad_project, 0, 1).astype(BF)

    share = model // nd
    cols = 3 * width
    norm_high, norm_low = high_low(norms)
    bias_high, bias_low = high_low(grad_bias.reshape(nd, 1, -1))
    extra = -(-model // cols)
    small = jnp.concatenate([norm_high, norm_low], axis=0)
    small = jnp.pad(small, ((0, 0), (0, extra * cols - model))).reshape(8 * extra, cols)
    small = jnp.broadcast_to(small[None], (nd, 8 * extra, cols))
    biases = jnp.concatenate([bias_high, bias_low], axis=2)
    biases = jnp.pad(biases, ((0, 0), (0, 15), (0, cols - biases.shape[2])))
    packed = jnp.concatenate([grad_w_project.reshape(nd, share, cols), small, biases], axis=1)
    packed = lax.all_to_all(packed, "dp", 0, 0, tiled=True)
    packed = jnp.sum(packed.astype(F32), axis=0)
    w_grads = packed[:share]
    norms = packed[share : share + 8 * extra].reshape(8, extra * cols)[:, :model]
    norms = norms[:4] + norms[4:]
    nbias = grad_bias.shape[0] // nd
    biases = packed[share + 8 * extra, : 2 * nbias]
    grad_bias = biases[:nbias] + biases[nbias:]
    return (
        result.astype(BF),
        jnp.transpose(logits, (1, 0, 2)),
        grad_inputs,
        jnp.transpose(prev_grad, (1, 0, 2)),
        w_grads[:, :width],
        w_grads[:, width : 2 * width],
        w_grads[:, 2 * width :],
        rest[:, grad_w_in.shape[1] :].T,
        rest[:, : grad_w_in.shape[1]],
        grad_bias,
        grad_w_out,
        norms[0],
        norms[1],
        norms[2],
        norms[3],
    )


def solution(mesh):
    placed = (
        P(("dp", "tensor"), None),
        P("dp", "tensor", None),
        P("dp", "tensor"),
        P("dp", "tensor"),
        P("dp", "tensor"),
        P("tensor", "dp"),
        P("dp", "tensor"),
        P(("tensor", "dp")),
        P(("tensor", "dp"), None),
        P(),
        P(),
        P(),
        P(),
        P(),
        P(),
        P(("dp", "tensor"), None),
        P("dp", "tensor", None),
    )
    return jax.shard_map(
        shards,
        mesh=mesh,
        in_specs=placed,
        out_specs=(
            P(("dp", "tensor"), None),
            P("dp", "tensor", None),
            P(("dp", "tensor"), None),
            P("dp", "tensor", None),
            P("dp", "tensor"),
            P("dp", "tensor"),
            P("dp", "tensor"),
            P("tensor", "dp"),
            P("dp", "tensor"),
            P(("tensor", "dp")),
            P(("tensor", "dp"), None),
            P(),
            P(),
            P(),
            P(),
        ),
        check_vma=False,
    )
```

```python
import functools

import jax
import jax.numpy as jnp
from jax import lax
from jax.experimental import pallas as pl
from jax.experimental.pallas import tpu as pltpu
from jax.sharding import PartitionSpec as P

E = 64
TRUNK = 2048
BLOCK = 128
EPSILON = 1e-12
LOW = -1e30

BF = jnp.bfloat16
F32 = jnp.float32


def layer_norm(values, norm_gain, norm_shift):
    center = values - jnp.mean(values, axis=-1, keepdims=True)
    spread = jnp.mean(center * center, axis=-1, keepdims=True)
    return center * lax.rsqrt(spread + EPSILON) * norm_gain + norm_shift


def contract(a, b, da, db):
    return lax.dot_general(a, b, (((da,), (db,)), ((), ())), preferred_element_type=F32)


def block_mask(shard, rows, act_ref, q_blocks):
    nb = rows // BLOCK
    total_blocks = act_ref.shape[0] // nb
    parts = []
    for qi in q_blocks:
        flags = [act_ref[qi * total_blocks + shard * nb + ki].astype(F32) for ki in range(nb)]
        line = jnp.concatenate([jnp.full((1, BLOCK), f, F32) for f in flags], axis=1)
        parts.append(jnp.broadcast_to(line, (BLOCK, rows)))
    return jnp.concatenate(parts, axis=0)


def in_use(shard, rows, act_ref):
    nb = rows // BLOCK
    total_blocks = act_ref.shape[0] // nb
    flags = [act_ref[qi * total_blocks + shard * nb + ki] for qi in range(nb) for ki in range(nb)]
    return functools.reduce(jnp.maximum, flags) == 1


def tile_of(ref, head, shard, rows):
    return ref.at[head, :, pl.ds(pl.multiple_of(shard * rows, BLOCK), rows)]


def forward_kernel(first, last, pieces, base, rc, *refs):
    sid_ref, act_ref, q_ref = refs[:3]
    kv_refs = refs[3 : 3 + pieces]
    refs = refs[3 + pieces :]
    prev_ref, refs = refs[0], refs[1:]
    if not first:
        carry_in, refs = refs[1], refs[2:]
    logit_ref, refs = refs[0], refs[1:]
    if last:
        mix_ref, refs = refs[0], refs[1:]
    out_ref, m_s, acc_s, q_s, kv_s, prev_s, logit_s, in_sem, out_sem = refs
    heads, rows, _ = prev_ref.shape
    shards_here = [sid_ref[base + p] for p in range(pieces)]
    uses = [in_use(shard, rows, act_ref) for shard in shards_here]

    def incoming(p, h):
        i = p * heads + h
        return pltpu.make_async_copy(tile_of(prev_ref, h, shards_here[p], rows), prev_s.at[i], in_sem.at[i])

    def outgoing(p, h):
        i = p * heads + h
        return pltpu.make_async_copy(logit_s.at[i], tile_of(logit_ref, h, shards_here[p], rows), out_sem.at[i])

    for p in range(pieces):

        @pl.when(uses[p])
        def _(p=p):
            for h in range(heads):
                incoming(p, h).start()

    for h in range(heads):
        q_s[h] = q_ref[h * E : (h + 1) * E, :].astype(F32).T.astype(BF)
        for p in range(pieces):
            kv_s[p, h, :E, :] = kv_refs[p][1, h * E : (h + 1) * E, :]
            kv_s[p, h, E : 2 * E, :] = jnp.ones((E, rows), BF)
            kv_s[p, h, 2 * E :, :] = kv_refs[p][0, h * E : (h + 1) * E, :]
        if first:
            m_s[h] = jnp.full((rows, 1), LOW, F32)
            acc_s[h] = jnp.zeros((rows, 2 * E), F32)
        else:
            m_s[h] = carry_in[h, :, 96:97]
            acc_s[h] = carry_in[h]

    for p, shard in enumerate(shards_here):

        @pl.when(uses[p])
        def _(p=p, shard=shard):
            @pl.loop(0, heads)
            def _(h):
                i = p * heads + h
                incoming(p, h).wait()
                for r0 in range(0, rows, min(rc, rows)):
                    rs = slice(r0, r0 + min(rc, rows))
                    on = block_mask(shard, rows, act_ref, range(r0 // BLOCK, rs.stop // BLOCK))
                    s = contract(q_s[h, rs, :], kv_s[p, h, 2 * E :, :], 1, 0) + prev_s[i, rs, :].astype(F32)
                    logit_s[i, rs, :] = (s * on).astype(BF)
                    s = s + (on - 1.0) * (-LOW)
                    m_old = m_s[h, rs, :]
                    m_new = jnp.maximum(m_old, jnp.max(s, axis=1, keepdims=True))
                    weight = jnp.exp(s - m_new).astype(BF)
                    fix = jnp.exp(m_old - m_new)
                    m_s[h, rs, :] = m_new
                    acc_s[h, rs, :] = acc_s[h, rs, :] * fix + contract(weight, kv_s[p, h, : 2 * E, :], 1, 1)
                outgoing(p, h).start()

        @pl.when(jnp.logical_not(uses[p]))
        def _(p=p):
            for h in range(heads):
                logit_s[p * heads + h] = jnp.zeros((rows, rows), BF)
                outgoing(p, h).start()

    for h in range(heads):
        if last:
            total = acc_s[h, :, E : E + 1]
            out = acc_s[h, :, :E] / total
            mix_ref[h * E : (h + 1) * E, :] = out.T.astype(BF)
            out_ref[h, :, :E] = out
            out_ref[h, :, E:] = jnp.broadcast_to(m_s[h] + jnp.log(total), (rows, 128 - E))
        else:
            out_ref[h, :, :96] = acc_s[h, :, :96]
            out_ref[h, :, 96:] = jnp.broadcast_to(m_s[h], (rows, 32))
    for p in range(pieces):
        for h in range(heads):
            outgoing(p, h).wait()


def attend_forward(sid, base, act, q_t, kvs, prev, carry, last, rc=256):
    heads, rows, length = prev.shape
    pieces, first = len(kvs), carry is None
    scalars = pl.BlockSpec(memory_space=pltpu.SMEM)
    whole = pl.BlockSpec(memory_space=pltpu.VMEM)
    left = pl.BlockSpec(memory_space=pl.ANY)
    in_specs = [scalars, scalars, whole] + [whole] * pieces + [left]
    args = [sid, act, q_t, *kvs, prev]
    aliases = {}
    if not first:
        aliases = {len(args): 0}
        in_specs += [left, whole]
        args += list(carry)
    out_shape = [jax.ShapeDtypeStruct((heads, rows, length), BF)]
    if last:
        out_shape.append(jax.ShapeDtypeStruct((heads * E, rows), BF))
    out_shape.append(jax.ShapeDtypeStruct((heads, rows, 128), F32))
    work = heads * pieces * rows * rows
    return pl.pallas_call(
        functools.partial(forward_kernel, first, last, pieces, base, rc),
        out_shape=out_shape,
        in_specs=in_specs,
        out_specs=[left] + [whole] * (len(out_shape) - 1),
        scratch_shapes=[
            pltpu.VMEM((heads, rows, 1), F32),
            pltpu.VMEM((heads, rows, 128), F32),
            pltpu.VMEM((heads, rows, E), BF),
            pltpu.VMEM((pieces, heads, 3 * E, rows), BF),
            pltpu.VMEM((pieces * heads, rows, rows), BF),
            pltpu.VMEM((pieces * heads, rows, rows), BF),
            pltpu.SemaphoreType.DMA((pieces * heads,)),
            pltpu.SemaphoreType.DMA((pieces * heads,)),
        ],
        input_output_aliases=aliases,
        cost_estimate=pl.CostEstimate(flops=4 * E * work, transcendentals=work, bytes_accessed=4 * work),
    )(*args)


def backward_kernel(first, last, pieces, base, rc, *refs):
    sid_ref, act_ref, q_ref, do_ref, aux_ref = refs[:5]
    kv_refs = refs[5 : 5 + pieces]
    refs = refs[5 + pieces :]
    prev_ref, up_ref, refs = refs[0], refs[1], refs[2:]
    if not first:
        gq_in, refs = refs[1], refs[2:]
    pg_ref = refs[0]
    gkv_refs = refs[1 : 1 + pieces]
    gq_ref, q_s, do_s, d_s, lse_s, gq_s, p_s, prev_s, up_s, pg_s, prev_sem, up_sem, out_sem = refs[1 + pieces :]
    heads, rows, _ = prev_ref.shape
    shards_here = [sid_ref[base + p] for p in range(pieces)]
    uses = [in_use(shard, rows, act_ref) for shard in shards_here]

    def incoming(p, h):
        i = p * heads + h
        return (
            pltpu.make_async_copy(tile_of(prev_ref, h, shards_here[p], rows), prev_s.at[i], prev_sem.at[i]),
            pltpu.make_async_copy(tile_of(up_ref, h, shards_here[p], rows), up_s.at[i], up_sem.at[i]),
        )

    def outgoing(p, h):
        i = p * heads + h
        return pltpu.make_async_copy(pg_s.at[i], tile_of(pg_ref, h, shards_here[p], rows), out_sem.at[i])

    for p in range(pieces):

        @pl.when(uses[p])
        def _(p=p):
            for h in range(heads):
                for copy in incoming(p, h):
                    copy.start()

    for h in range(heads):
        q_s[h] = q_ref[h * E : (h + 1) * E, :].astype(F32).T.astype(BF)
        do = do_ref[h * E : (h + 1) * E, :].astype(F32).T
        do_s[h] = do.astype(BF)
        d_s[h] = jnp.sum(do * aux_ref[h, :, :E], axis=1, keepdims=True)
        lse_s[h] = aux_ref[h, :, E : E + 1]
        gq_s[h] = jnp.zeros((rows, E), F32) if first else gq_in[h]

    for p, shard in enumerate(shards_here):

        @pl.when(uses[p])
        def _(p=p, shard=shard):
            @pl.loop(0, heads)
            def _(h):
                i = p * heads + h
                feature = pl.ds(pl.multiple_of(h * E, E), E)
                for copy in incoming(p, h):
                    copy.wait()
                for r0 in range(0, rows, min(rc, rows)):
                    rs = slice(r0, r0 + min(rc, rows))
                    on = block_mask(shard, rows, act_ref, range(r0 // BLOCK, rs.stop // BLOCK))
                    s = contract(q_s[h, rs, :], kv_refs[p][0, feature, :], 1, 0) + prev_s[i, rs, :].astype(F32)
                    weight = jnp.exp(s - lse_s[h, rs, :] + (on - 1.0) * (-LOW))
                    dp = contract(do_s[h, rs, :], kv_refs[p][1, feature, :], 1, 0)
                    upper = up_s[i, rs, :].astype(F32) * on
                    pg_s[i, rs, :] = (weight * (dp - d_s[h, rs, :]) + upper).astype(BF)
                    p_s[rs, :] = weight.astype(BF)
                outgoing(p, h).start()
                gkv_refs[p][0, feature, :] = contract(q_ref[feature, :], pg_s[i], 1, 0).astype(BF)
                gkv_refs[p][1, feature, :] = contract(do_ref[feature, :], p_s[...], 1, 0).astype(BF)
                gq_s[h] += contract(pg_s[i], kv_refs[p][0, feature, :], 1, 1)

        @pl.when(jnp.logical_not(uses[p]))
        def _(p=p):
            for h in range(heads):
                pg_s[p * heads + h] = jnp.zeros((rows, rows), BF)
                outgoing(p, h).start()
            gkv_refs[p][...] = jnp.zeros(gkv_refs[p].shape, BF)

    for h in range(heads):
        if last:
            gq_ref[h * E : (h + 1) * E, :] = (gq_s[h] * (E ** (-0.5))).T.astype(BF)
        else:
            gq_ref[h] = gq_s[h]
    for p in range(pieces):
        for h in range(heads):
            outgoing(p, h).wait()


def attend_backward(sid, base, act, q_t, do_t, aux, kvs, prev, up, carry, last, rc=256):
    heads, rows, length = prev.shape
    pieces, first = len(kvs), carry is None
    scalars = pl.BlockSpec(memory_space=pltpu.SMEM)
    whole = pl.BlockSpec(memory_space=pltpu.VMEM)
    left = pl.BlockSpec(memory_space=pl.ANY)
    in_specs = [scalars, scalars, whole, whole, whole] + [whole] * pieces + [left, left]
    args = [sid, act, q_t, do_t, aux, *kvs, prev, up]
    aliases = {}
    if not first:
        aliases = {len(args): 0}
        in_specs += [left, whole]
        args += list(carry)
    out_shape = [jax.ShapeDtypeStruct((heads, rows, length), BF)]
    out_shape += [jax.ShapeDtypeStruct((2, heads * E, rows), BF)] * pieces
    if last:
        out_shape.append(jax.ShapeDtypeStruct((heads * E, rows), BF))
    else:
        out_shape.append(jax.ShapeDtypeStruct((heads, rows, E), F32))
    work = heads * pieces * rows * rows
    return pl.pallas_call(
        functools.partial(backward_kernel, first, last, pieces, base, rc),
        out_shape=out_shape,
        in_specs=in_specs,
        out_specs=[left] + [whole] * (pieces + 1),
        scratch_shapes=[
            pltpu.VMEM((heads, rows, E), BF),
            pltpu.VMEM((heads, rows, E), BF),
            pltpu.VMEM((heads, rows, 1), F32),
            pltpu.VMEM((heads, rows, 1), F32),
            pltpu.VMEM((heads, rows, E), F32),
            pltpu.VMEM((rows, rows), BF),
            pltpu.VMEM((pieces * heads, rows, rows), BF),
            pltpu.VMEM((pieces * heads, rows, rows), BF),
            pltpu.VMEM((pieces * heads, rows, rows), BF),
            pltpu.SemaphoreType.DMA((pieces * heads,)),
            pltpu.SemaphoreType.DMA((pieces * heads,)),
            pltpu.SemaphoreType.DMA((pieces * heads,)),
        ],
        input_output_aliases=aliases,
        cost_estimate=pl.CostEstimate(flops=10 * E * work, transcendentals=work, bytes_accessed=6 * work),
    )(*args)


class Ring:
    def __init__(self, axis, total, size):
        self.axis, self.size = axis, size
        local = list(range(0, size, 2)) + list(range(size - 1 - size % 2, 0, -2))
        self.local = local
        self.up, self.down = [], []
        for base in range(0, total, size):
            for i in range(size):
                a, b = base + local[i], base + local[(i + 1) % size]
                self.up.append((a, b))
                self.down.append((b, a))

    def members(self, index, offsets):
        n = self.size
        mine = jnp.where(index % 2 == 0, index // 2, n - 1 - index // 2)
        place = (mine + jnp.array(offsets, jnp.int32)) % n
        return jnp.where(place < (n + 1) // 2, 2 * place, 2 * (n - 1 - place) + 1)

    def groups(self):
        if self.size == 1:
            return [[0]]
        half = self.size // 2
        return [[0]] + [[-k, k] for k in range(1, half)] + [[half]]

    def send_up(self, x):
        return lax.ppermute(x, self.axis, self.up)

    def send_down(self, x):
        return lax.ppermute(x, self.axis, self.down)


class RingSum:
    def __init__(self, ring, axis):
        self.ring, self.axis = ring, axis
        self.up = self.down = None
        self.half = False

    def first(self, part):
        a, b = halves(part, self.axis)
        self.up, self.down, self.half = self.ring.send_up(a), self.ring.send_down(b), True

    def step(self, behind, ahead):
        if self.half:
            a, b = halves(ahead, self.axis)
            up = jnp.concatenate([add(a, self.up), b], axis=self.axis)
            a, b = halves(behind, self.axis)
            down = jnp.concatenate([a, add(b, self.down)], axis=self.axis)
        else:
            up, down = add(ahead, self.up), add(behind, self.down)
        self.up, self.down, self.half = self.ring.send_up(up), self.ring.send_down(down), False
        return up, down

    def last(self, part):
        total = part.astype(F32)
        if self.up is None:
            return total
        if self.half:
            return total + jnp.concatenate([self.up, self.down], axis=self.axis).astype(F32)
        return total + self.up.astype(F32) + self.down.astype(F32)


def halves(x, axis):
    middle = x.shape[axis] // 2
    return lax.slice_in_dim(x, 0, middle, axis=axis), lax.slice_in_dim(x, middle, x.shape[axis], axis=axis)


def add(a, b):
    return (a.astype(F32) + b.astype(F32)).astype(BF)


def after(x, *earlier):
    return lax.optimization_barrier((x, *earlier))[0]


def spread_gather(x, axis, n):
    return lax.all_to_all(jnp.broadcast_to(x[None], (n,) + x.shape), axis, 0, 0, tiled=True)


def group_sum(x, axis, n):
    parts = lax.all_to_all(x.reshape(n, x.shape[0] // n, x.shape[1]), axis, 0, 0, tiled=True)
    return jnp.sum(parts.astype(F32), axis=0)


def high_low(x):
    high = x.astype(BF)
    return high, (x - high.astype(F32)).astype(BF)


class Quad:
    def __init__(self, axis):
        self.axis = axis
        index = lax.axis_index(axis)
        self.near, self.far = index % 2, index // 2
        self.flip_near = [(i, i ^ 1) for i in range(4)]
        self.flip_far = [(i, i ^ 2) for i in range(4)]

    def send_near(self, x):
        return lax.ppermute(x, self.axis, self.flip_near)

    def send_far(self, x):
        return lax.ppermute(x, self.axis, self.flip_far)

    def rows_of(self, x, near):
        x = x.reshape(2, 2, x.shape[0] // 4, x.shape[1])
        return lax.dynamic_index_in_dim(x, near, 1, keepdims=False)

    def sum_pair(self, left, right):
        r = left.shape[0] // 4

        def product(near):
            rows = self.rows_of(left, near).reshape(2 * r, left.shape[1])
            return contract(rows, right[0], 1, right[1])

        sent = self.send_near(product(1 - self.near).astype(BF))
        mine = add(product(self.near), sent)
        other = self.send_far(mine)
        return (mine.astype(F32) + other.astype(F32)).reshape(2, r, -1)

    def sum_own(self, x):
        sent = self.send_near(self.rows_of(x, 1 - self.near))
        mine = add(self.rows_of(x, self.near), sent)
        sent = self.send_far(lax.dynamic_index_in_dim(mine, 1 - self.far, 0, keepdims=False))
        kept = lax.dynamic_index_in_dim(mine, self.far, 0, keepdims=False)
        return kept.astype(F32) + sent.astype(F32)

    def join(self, mine, other):
        first = jnp.where(self.near == 0, mine, other)
        second = jnp.where(self.near == 0, other, mine)
        both = jnp.stack([first, second], axis=1)
        return both.reshape(-1, mine.shape[-1])


def norm_pull(n, r, gain, cotangent):
    dn = cotangent * gain
    return r * (
        dn - jnp.mean(dn, axis=-1, keepdims=True) - n * jnp.mean(dn * n, axis=-1, keepdims=True)
    )


def norm_parts(values):
    center = values - jnp.mean(values, axis=-1, keepdims=True)
    r = lax.rsqrt(jnp.mean(center * center, axis=-1, keepdims=True) + EPSILON)
    return center * r, r


def shards(
    inputs,
    prev_logits,
    w_query,
    w_key,
    w_value,
    w_attn_out,
    w_ffn_in,
    ffn_bias,
    w_ffn_out,
    norm1_gain,
    norm1_shift,
    norm2_gain,
    norm2_shift,
    token_segment,
    segment_parent,
    out_grad,
    logit_grad,
):
    rows, heads, length = prev_logits.shape
    width = heads * E
    own, model = inputs.shape
    hidden_units = w_ffn_in.shape[1]
    spread = length // rows
    nd, nt = lax.axis_size("dp"), lax.axis_size("tensor")
    data_index, tensor_index = lax.axis_index("dp"), lax.axis_index("tensor")
    tree_index, local_index = data_index // spread, data_index % spread
    nb = rows // BLOCK
    quad = Quad("tensor")
    ring = Ring("dp", nd, spread)

    pack = jnp.concatenate([w_query, w_key, w_value, w_attn_out.T], axis=1)
    pack = spread_gather(pack, "dp", nd).reshape(model, 4 * width)
    project = pack[:, : 3 * width]
    out_own = pack[:, 3 * width :].T
    rows_all = lax.all_gather(inputs, "tensor", axis=0, tiled=True)
    pack = jnp.concatenate([w_ffn_in, ffn_bias[:, None]], axis=1)
    pack_in = lax.all_gather(after(pack, project), "dp", axis=0, tiled=True)
    w_out = lax.all_gather(after(w_ffn_out, project), "dp", axis=0, tiled=True)
    out_grad_pair = quad.send_far(out_grad)

    seg = lax.dynamic_slice_in_dim(token_segment, tree_index * length, length, 0)[::BLOCK]
    parents = lax.dynamic_slice_in_dim(segment_parent, tree_index, 1, 0)[0]
    seg_rows = lax.dynamic_slice_in_dim(seg, local_index * nb, nb, 0)
    labels = jnp.arange(parents.shape[0], dtype=jnp.int32)
    one = jnp.sum(jnp.where(seg_rows[:, None] == labels[None, :], parents[None, :], 0), axis=1)
    two = jnp.sum(jnp.where(one[:, None] == labels[None, :], parents[None, :], 0), axis=1)
    act = (
        (seg[None, :] == seg_rows[:, None])
        | (seg[None, :] == one[:, None])
        | (seg[None, :] == two[:, None])
    )
    act = act.astype(jnp.int32).reshape(-1)

    projected = contract(project, rows_all, 0, 1)
    q_t = (projected[:width] * (E ** (-0.5))).astype(BF)
    kv_own = projected[width:].astype(BF).reshape(2, width, rows)

    prev = jnp.transpose(prev_logits, (1, 0, 2))
    up_grad = jnp.transpose(logit_grad, (1, 0, 2))
    groups = ring.groups()
    held = {0: kv_own}
    going_up = going_down = kv_own
    state = None
    order = [o for group in groups for o in group]
    sid = ring.members(local_index, order)
    for step, group in enumerate(groups):
        if step + 1 < len(groups):
            if state is not None:
                going_up, going_down = lax.optimization_barrier((going_up, going_down, state[1]))[:2]
            if groups[step + 1] == [spread // 2]:
                a = ring.send_up(halves(going_up, 1)[0])
                b = ring.send_down(halves(going_down, 1)[1])
                held[spread // 2] = jnp.concatenate([a, b], axis=1)
            else:
                going_up, going_down = ring.send_up(going_up), ring.send_down(going_down)
                held[groups[step + 1][0]], held[groups[step + 1][1]] = going_up, going_down
        last = step + 1 == len(groups)
        result = attend_forward(
            sid, order.index(group[0]), act, q_t, [held[o] for o in group], prev, state, last, 512
        )
        state = (result[0], result[-1])
        if step == 0:
            near = quad.send_near(out_own)
            pair_own = jnp.where(quad.near == 0, jnp.stack([out_own, near]), jnp.stack([near, out_own]))
            pair_far = quad.send_far(pair_own)
            out_full = jnp.where(
                quad.far == 0, jnp.stack([pair_own, pair_far]), jnp.stack([pair_far, pair_own])
            ).reshape(nt * width, model)
    logits, mixed, aux = result
    pack_in, w_out, out_full = (after(w, mixed) for w in (pack_in, w_out, out_full))
    w_in = pack_in[:, :hidden_units]
    bias = pack_in[:, hidden_units].astype(F32)

    mixed_all = lax.all_gather(mixed, "tensor", axis=0, tiled=True)
    attended = contract(mixed_all, out_full, 0, 0)
    first_n, first_r = norm_parts(rows_all.astype(F32) + attended)
    hidden_all = first_n * norm1_gain + norm1_shift
    hidden_low = hidden_all.astype(BF)
    pair = lambda x: quad.rows_of(x, quad.near)

    inner = contract(hidden_low, w_in, 1, 0) + bias
    active, gelu_back = jax.vjp(lambda v: jax.nn.gelu(v, approximate=False), inner)
    active = active.astype(BF)
    ffn_out = quad.sum_pair(active, (w_out, 0))
    second_n, second_r = norm_parts(pair(hidden_all) + ffn_out)
    mine = lax.dynamic_index_in_dim(second_n, quad.far, 0, keepdims=False)
    output = mine * norm2_gain + norm2_shift
    pair_grad = jnp.where(
        quad.far == 0, jnp.stack([out_grad, out_grad_pair]), jnp.stack([out_grad_pair, out_grad])
    ).astype(F32)
    grad_second = norm_pull(second_n, second_r, norm2_gain, pair_grad)
    gain_two = jnp.sum(pair_grad * second_n, axis=(0, 1))
    shift_two = jnp.sum(pair_grad, axis=(0, 1))
    second_low = grad_second.astype(BF)
    second_all = quad.join(second_low, quad.send_near(second_low))
    grad_active = contract(second_all, w_out, 1, 1).astype(BF)
    grad_w_out = contract(active, second_all, 0, 0).astype(BF)
    (grad_inner,) = gelu_back(grad_active.astype(F32))
    grad_inner = grad_inner.astype(BF)
    grad_w_in = contract(hidden_low, grad_inner, 0, 0).astype(BF)
    grad_bias = jnp.sum(grad_inner.astype(F32), axis=0)
    weights = RingSum(Ring("dp", nd, nd), 0)
    steps = weights.ring.groups()[::-1]
    where = weights.ring.members(data_index, [o for group in steps for o in group])
    share = model // nd

    def weight_parts(step):
        begin = sum(len(group) for group in steps[:step])
        parts = []
        for i in range(len(steps[step])):
            at = where[begin + i] * share
            parts.append(
                jnp.concatenate(
                    [lax.dynamic_slice_in_dim(g, at, share, 0) for g in (grad_w_out, grad_w_in)], axis=1
                )
            )
        return parts

    def weight_step(step, x):
        if step >= len(steps) - 1:
            return x
        parts = weight_parts(step)
        if step == 0:
            weights.first(parts[0])
            return x
        return after(x, *weights.step(*parts))

    weight_step(0, None)
    grad_hidden = grad_second + quad.sum_pair(grad_inner, (w_in, 1))
    grad_hidden = weight_step(1, grad_hidden)
    pair_n, pair_r = pair(first_n), pair(first_r)
    grad_first = norm_pull(pair_n, pair_r, norm1_gain, grad_hidden)
    gain_one = jnp.sum(grad_hidden * pair_n, axis=(0, 1))
    shift_one = jnp.sum(grad_hidden, axis=(0, 1))
    norm_high, norm_low = high_low(jnp.stack([gain_one, shift_one, gain_two, shift_two]))
    sent = jnp.concatenate([grad_first.astype(BF).reshape(2 * own, model), norm_high, norm_low], axis=0)
    received = quad.send_near(sent)
    first_back = quad.join(
        sent[: 2 * own].reshape(2, own, model), received[: 2 * own].reshape(2, own, model)
    )
    norms = sent[2 * own :].astype(F32) + received[2 * own :].astype(F32)
    norms = norms[:4] + norms[4:]
    grad_first = lax.dynamic_index_in_dim(grad_first, quad.far, 0, keepdims=False)
    grad_mixed = contract(out_own, first_back, 1, 1).astype(BF)
    grad_w_attn = contract(first_back, mixed, 0, 1).astype(BF).reshape(nd, share, width)

    norm_high, norm_low = high_low(norms)
    small = jnp.concatenate([norm_high, norm_low], axis=0).reshape(8 * model // width, width)
    small = jnp.broadcast_to(small[None], (nd,) + small.shape)
    bias_high, bias_low = high_low(grad_bias.reshape(nd, 1, -1))
    biases = jnp.pad(
        jnp.concatenate([bias_high, bias_low], axis=1), ((0, 0), (0, 14), (0, width - hidden_units // nd))
    )
    packed = jnp.concatenate([grad_w_attn, small, biases], axis=1)
    packed = lax.all_to_all(packed, "dp", 0, 0, tiled=True)
    grad_mixed = weight_step(2, grad_mixed)

    state = None
    total_kv = RingSum(ring, 1)
    for step, group in enumerate(reversed(groups)):
        last = step + 1 == len(groups)
        result = attend_backward(
            sid,
            order.index(group[0]),
            act,
            q_t,
            grad_mixed,
            aux,
            [held[o] for o in group],
            prev,
            up_grad,
            state,
            last,
            256,
        )
        state = (result[0], result[-1])
        parts = result[1:-1]
        if not last:
            state = (state[0], weight_step(3 + step, state[1]))
        if last:
            own_kv = total_kv.last(parts[0]).astype(BF).reshape(2 * width, rows)
        elif step == 0:
            total_kv.first(parts[0])
        else:
            total_kv.step(*parts)
    prev_grad, grad_query = result[0], result[-1]
    for step in range(2 + len(groups), len(steps) - 1):
        weight_step(step, grad_query)
    weight_grads = weights.last(weight_parts(len(steps) - 1)[0])

    grad_project = jnp.concatenate([grad_query, own_kv], axis=0)
    grad_w_project = contract(rows_all, grad_project, 0, 1).astype(BF)
    grad_w_project = lax.all_to_all(grad_w_project.reshape(nd, share, 3 * width), "dp", 0, 0, tiled=True)
    input_part = contract(grad_project, project, 0, 1).astype(BF)
    grad_inputs = grad_first + quad.sum_own(input_part)
    grad_w_project = jnp.sum(grad_w_project.astype(F32), axis=0)
    packed = jnp.sum(packed.astype(F32), axis=0)
    norms = packed[share : share + small.shape[1]].reshape(8, model)
    norms = norms[:4] + norms[4:]
    biases = packed[share + small.shape[1] :, : hidden_units // nd]
    grad_bias = biases[0] + biases[1]
    return (
        output.astype(BF),
        jnp.transpose(logits, (1, 0, 2)),
        grad_inputs,
        jnp.transpose(prev_grad, (1, 0, 2)),
        grad_w_project[:, :width],
        grad_w_project[:, width : 2 * width],
        grad_w_project[:, 2 * width :],
        packed[:share].T,
        weight_grads[:, model:],
        grad_bias,
        weight_grads[:, :model],
        norms[0],
        norms[1],
        norms[2],
        norms[3],
    )


def solution(mesh):
    placed = (
        P(("dp", "tensor"), None),
        P("dp", "tensor", None),
        P("dp", "tensor"),
        P("dp", "tensor"),
        P("dp", "tensor"),
        P("tensor", "dp"),
        P("dp", "tensor"),
        P(("tensor", "dp")),
        P(("tensor", "dp"), None),
        P(),
        P(),
        P(),
        P(),
        P(),
        P(),
        P(("dp", "tensor"), None),
        P("dp", "tensor", None),
    )
    return jax.shard_map(
        shards,
        mesh=mesh,
        in_specs=placed,
        out_specs=(
            P(("dp", "tensor"), None),
            P("dp", "tensor", None),
            P(("dp", "tensor"), None),
            P("dp", "tensor", None),
            P("dp", "tensor"),
            P("dp", "tensor"),
            P("dp", "tensor"),
            P("tensor", "dp"),
            P("dp", "tensor"),
            P(("tensor", "dp")),
            P(("tensor", "dp"), None),
            P(),
            P(),
            P(),
            P(),
        ),
        check_vma=False,
    )
```

```python
import functools
import math

import jax
import jax.numpy as jnp
from jax import lax
from jax.experimental import pallas as pl
from jax.experimental.pallas import tpu as pltpu
from jax.sharding import PartitionSpec as P

E = 64
SPARE = 8 << 20
TRUNK = 2048
BLOCK = 128
EPSILON = 1e-12
LOW = -1e30

BF = jnp.bfloat16
F32 = jnp.float32


def layer_norm(values, norm_gain, norm_shift):
    center = values - jnp.mean(values, axis=-1, keepdims=True)
    spread = jnp.mean(center * center, axis=-1, keepdims=True)
    return center * lax.rsqrt(spread + EPSILON) * norm_gain + norm_shift


def size_of(*arrays):
    return sum(math.prod(a.shape) * jnp.dtype(a.dtype).itemsize for a in arrays)


def apart(x):
    return pltpu.with_memory_space_constraint(x, pltpu.HBM)


def contract(a, b, da, db):
    return lax.dot_general(a, b, (((da,), (db,)), ((), ())), preferred_element_type=F32)


def block_mask(shard, rows, act_ref, q_blocks):
    nb = rows // BLOCK
    total_blocks = act_ref.shape[0] // nb
    parts = []
    for qi in q_blocks:
        flags = [act_ref[qi * total_blocks + shard * nb + ki].astype(F32) for ki in range(nb)]
        line = jnp.concatenate([jnp.full((1, BLOCK), f, F32) for f in flags], axis=1)
        parts.append(jnp.broadcast_to(line, (BLOCK, rows)))
    return jnp.concatenate(parts, axis=0)


def in_use(shard, rows, act_ref):
    nb = rows // BLOCK
    total_blocks = act_ref.shape[0] // nb
    flags = [act_ref[qi * total_blocks + shard * nb + ki] for qi in range(nb) for ki in range(nb)]
    return functools.reduce(jnp.maximum, flags) == 1


def tile_of(ref, head, shard, rows):
    return ref.at[head, :, pl.ds(pl.multiple_of(shard * rows, BLOCK), rows)]


def read_pieces(pieces, parted, refs):
    if parted:
        return [(lambda rs: refs[0][0, rs, :], lambda rs: refs[1][0, rs, :])], refs[2:]
    return [
        (lambda rs, ref=ref: ref[0, rs, :], lambda rs, ref=ref: ref[1, rs, :]) for ref in refs[:pieces]
    ], refs[pieces:]


def forward_kernel(first, last, pieces, parted, base, rc, *refs):
    sid_ref, act_ref, q_ref = refs[:3]
    readers, refs = read_pieces(pieces, parted, refs[3:])
    prev_ref, refs = refs[0], refs[1:]
    if not first:
        carry_in, refs = refs[1], refs[2:]
    logit_ref, refs = refs[0], refs[1:]
    if last:
        mix_ref, refs = refs[0], refs[1:]
    out_ref, m_s, acc_s, q_s, kv_s, prev_s, logit_s, in_sem, out_sem = refs
    heads, rows, _ = prev_ref.shape
    count = pieces * heads

    def incoming(i):
        tile = tile_of(prev_ref, i % heads, sid_ref[base + i // heads], rows)
        return pltpu.make_async_copy(tile, prev_s.at[i], in_sem.at[i])

    def outgoing(i):
        tile = tile_of(logit_ref, i % heads, sid_ref[base + i // heads], rows)
        return pltpu.make_async_copy(logit_s.at[i], tile, out_sem.at[i])

    def used(i):
        return in_use(sid_ref[base + i // heads], rows, act_ref)

    @pl.loop(0, count)
    def _(i):
        @pl.when(used(i))
        def _():
            incoming(i).start()

    for h in range(heads):
        feature = slice(h * E, (h + 1) * E)
        q_s[h] = q_ref[feature, :].astype(F32).T.astype(BF)
        for p, (keys, values) in enumerate(readers):
            kv_s[p * heads + h, :E, :] = values(feature)
            kv_s[p * heads + h, E : 2 * E, :] = jnp.ones((E, rows), BF)
            kv_s[p * heads + h, 2 * E :, :] = keys(feature)
        if first:
            m_s[h] = jnp.full((rows, 1), LOW, F32)
            acc_s[h] = jnp.zeros((rows, 2 * E), F32)
        else:
            m_s[h] = carry_in[h, :, 96:97]
            acc_s[h] = carry_in[h]

    @pl.loop(0, count)
    def _(i):
        shard, h, here = sid_ref[base + i // heads], i % heads, used(i)

        @pl.when(here)
        def _():
            incoming(i).wait()

            for r0 in range(0, rows, min(rc, rows)):
                rs = slice(r0, r0 + min(rc, rows))
                on = block_mask(shard, rows, act_ref, range(r0 // BLOCK, rs.stop // BLOCK))
                s = contract(q_s[h, rs, :], kv_s[i, 2 * E :, :], 1, 0) + prev_s[i, rs, :].astype(F32)
                logit_s[i, rs, :] = (s * on).astype(BF)
                s = s + (on - 1.0) * (-LOW)
                m_old = m_s[h, rs, :]
                m_new = jnp.maximum(m_old, jnp.max(s, axis=1, keepdims=True))
                weight = jnp.exp(s - m_new).astype(BF)
                fix = jnp.exp(m_old - m_new)
                m_s[h, rs, :] = m_new
                acc_s[h, rs, :] = acc_s[h, rs, :] * fix + contract(weight, kv_s[i, : 2 * E, :], 1, 1)

        @pl.when(jnp.logical_not(here))
        def _():
            logit_s[i] = jnp.zeros((rows, rows), BF)

        outgoing(i).start()

    for h in range(heads):
        if last:
            total = acc_s[h, :, E : E + 1]
            out = acc_s[h, :, :E] / total
            mix_ref[h * E : (h + 1) * E, :] = out.T.astype(BF)
            out_ref[h, :, :E] = out
            out_ref[h, :, E:] = jnp.broadcast_to(m_s[h] + jnp.log(total), (rows, 128 - E))
        else:
            out_ref[h, :, :96] = acc_s[h, :, :96]
            out_ref[h, :, 96:] = jnp.broadcast_to(m_s[h], (rows, 32))

    @pl.loop(0, count)
    def _(i):
        outgoing(i).wait()


def attend_forward(sid, base, act, q_t, kvs, prev, carry, last, rc=256):
    heads, rows, length = prev.shape
    first, parted = carry is None, kvs[0].shape[0] == 1
    pieces = 1 if parted else len(kvs)
    scalars = pl.BlockSpec(memory_space=pltpu.SMEM)
    whole = pl.BlockSpec(memory_space=pltpu.VMEM)
    left = pl.BlockSpec(memory_space=pltpu.HBM)
    in_specs = [scalars, scalars, whole] + [whole] * len(kvs) + [left]
    args = [sid, act, q_t, *kvs, prev]
    aliases = {}
    if not first:
        aliases = {len(args): 0}
        in_specs += [left, whole]
        args += list(carry)
    out_shape = [jax.ShapeDtypeStruct((heads, rows, length), BF)]
    if last:
        out_shape.append(jax.ShapeDtypeStruct((heads * E, rows), BF))
    out_shape.append(jax.ShapeDtypeStruct((heads, rows, 128), F32))
    work = heads * pieces * rows * rows
    return pl.pallas_call(
        functools.partial(forward_kernel, first, last, pieces, parted, base, rc),
        out_shape=out_shape,
        in_specs=in_specs,
        out_specs=[left] + [whole] * (len(out_shape) - 1),
        scratch_shapes=[
            pltpu.VMEM((heads, rows, 1), F32),
            pltpu.VMEM((heads, rows, 128), F32),
            pltpu.VMEM((heads, rows, E), BF),
            pltpu.VMEM((pieces * heads, 3 * E, rows), BF),
            pltpu.VMEM((pieces * heads, rows, rows), BF),
            pltpu.VMEM((pieces * heads, rows, rows), BF),
            pltpu.SemaphoreType.DMA((pieces * heads,)),
            pltpu.SemaphoreType.DMA((pieces * heads,)),
        ],
        input_output_aliases=aliases,
        cost_estimate=pl.CostEstimate(flops=4 * E * work, transcendentals=work, bytes_accessed=4 * work),
        compiler_params=pltpu.CompilerParams(
            vmem_limit_bytes=6 * work + 16 * heads * rows * 128 * 4 + SPARE
        ),
    )(*args)


def backward_kernel(first, last, pieces, parted, base, rc, *refs):
    sid_ref, act_ref, q_ref, do_ref, aux_ref = refs[:5]
    readers, refs = read_pieces(pieces, parted, refs[5:])
    prev_ref, up_ref, refs = refs[0], refs[1], refs[2:]
    if not first:
        gq_in, refs = refs[1], refs[2:]
    outputs = 2 if parted else pieces
    pg_ref, gkv_refs = refs[0], refs[1 : 1 + outputs]
    gq_ref, q_s, do_s, d_s, lse_s, gq_s, p_s, kv_s, gkv_s, prev_s, up_s, pg_s, prev_sem, up_sem, out_sem = refs[1 + outputs :]
    heads, rows, _ = prev_ref.shape
    count = pieces * heads

    def incoming(i):
        at = i % heads, sid_ref[base + i // heads], rows
        return (
            pltpu.make_async_copy(tile_of(prev_ref, *at), prev_s.at[i], prev_sem.at[i]),
            pltpu.make_async_copy(tile_of(up_ref, *at), up_s.at[i], up_sem.at[i]),
        )

    def outgoing(i):
        tile = tile_of(pg_ref, i % heads, sid_ref[base + i // heads], rows)
        return pltpu.make_async_copy(pg_s.at[i], tile, out_sem.at[i])

    def used(i):
        return in_use(sid_ref[base + i // heads], rows, act_ref)

    @pl.loop(0, count)
    def _(i):
        @pl.when(used(i))
        def _():
            for copy in incoming(i):
                copy.start()

    for h in range(heads):
        feature = slice(h * E, (h + 1) * E)
        q_s[h] = q_ref[feature, :].astype(F32).T.astype(BF)
        do = do_ref[feature, :].astype(F32).T
        do_s[h] = do.astype(BF)
        d_s[h] = jnp.sum(do * aux_ref[h, :, :E], axis=1, keepdims=True)
        lse_s[h] = aux_ref[h, :, E : E + 1]
        gq_s[h] = jnp.zeros((rows, E), F32) if first else gq_in[h]
        for p, (keys, values) in enumerate(readers):
            kv_s[p * heads + h, :E, :] = keys(feature)
            kv_s[p * heads + h, E:, :] = values(feature)

    @pl.loop(0, count)
    def _(i):
        shard, h, here = sid_ref[base + i // heads], i % heads, used(i)
        feature = pl.ds(pl.multiple_of(h * E, E), E)

        @pl.when(here)
        def _():
            for copy in incoming(i):
                copy.wait()
            for r0 in range(0, rows, min(rc, rows)):
                rs = slice(r0, r0 + min(rc, rows))
                on = block_mask(shard, rows, act_ref, range(r0 // BLOCK, rs.stop // BLOCK))
                s = contract(q_s[h, rs, :], kv_s[i, :E, :], 1, 0) + prev_s[i, rs, :].astype(F32)
                weight = jnp.exp(s - lse_s[h, rs, :] + (on - 1.0) * (-LOW))
                dp = contract(do_s[h, rs, :], kv_s[i, E:, :], 1, 0)
                upper = up_s[i, rs, :].astype(F32) * on
                pg_s[i, rs, :] = (weight * (dp - d_s[h, rs, :]) + upper).astype(BF)
                p_s[rs, :] = weight.astype(BF)
            gkv_s[i, :E, :] = contract(q_ref[feature, :], pg_s[i], 1, 0).astype(BF)
            gkv_s[i, E:, :] = contract(do_ref[feature, :], p_s[...], 1, 0).astype(BF)
            gq_s[h] += contract(pg_s[i], kv_s[i, :E, :], 1, 1)

        @pl.when(jnp.logical_not(here))
        def _():
            pg_s[i] = jnp.zeros((rows, rows), BF)
            gkv_s[i] = jnp.zeros((2 * E, rows), BF)

        outgoing(i).start()

    for h in range(heads):
        feature = slice(h * E, (h + 1) * E)
        for p in range(pieces):
            for w in range(2):
                part = gkv_s[p * heads + h, w * E : (w + 1) * E, :]
                if parted:
                    gkv_refs[w][0, feature, :] = part
                else:
                    gkv_refs[p][w, feature, :] = part
        if last:
            gq_ref[feature, :] = (gq_s[h] * (E ** (-0.5))).T.astype(BF)
        else:
            gq_ref[h] = gq_s[h]

    @pl.loop(0, count)
    def _(i):
        outgoing(i).wait()


def attend_backward(sid, base, act, q_t, do_t, aux, kvs, prev, up, carry, last, rc=256):
    heads, rows, length = prev.shape
    first, parted = carry is None, kvs[0].shape[0] == 1
    pieces = 1 if parted else len(kvs)
    scalars = pl.BlockSpec(memory_space=pltpu.SMEM)
    whole = pl.BlockSpec(memory_space=pltpu.VMEM)
    left = pl.BlockSpec(memory_space=pltpu.HBM)
    in_specs = [scalars, scalars, whole, whole, whole] + [whole] * len(kvs) + [left, left]
    args = [sid, act, q_t, do_t, aux, *kvs, prev, up]
    aliases = {}
    if not first:
        aliases = {len(args): 0}
        in_specs += [left, whole]
        args += list(carry)
    out_shape = [jax.ShapeDtypeStruct((heads, rows, length), BF)]
    out_shape += [jax.ShapeDtypeStruct(kv.shape, BF) for kv in kvs]
    if last:
        out_shape.append(jax.ShapeDtypeStruct((heads * E, rows), BF))
    else:
        out_shape.append(jax.ShapeDtypeStruct((heads, rows, E), F32))
    work = heads * pieces * rows * rows
    return pl.pallas_call(
        functools.partial(backward_kernel, first, last, pieces, parted, base, rc),
        out_shape=out_shape,
        in_specs=in_specs,
        out_specs=[left] + [whole] * (len(kvs) + 1),
        scratch_shapes=[
            pltpu.VMEM((heads, rows, E), BF),
            pltpu.VMEM((heads, rows, E), BF),
            pltpu.VMEM((heads, rows, 1), F32),
            pltpu.VMEM((heads, rows, 1), F32),
            pltpu.VMEM((heads, rows, E), F32),
            pltpu.VMEM((rows, rows), BF),
            pltpu.VMEM((pieces * heads, 2 * E, rows), BF),
            pltpu.VMEM((pieces * heads, 2 * E, rows), BF),
            pltpu.VMEM((pieces * heads, rows, rows), BF),
            pltpu.VMEM((pieces * heads, rows, rows), BF),
            pltpu.VMEM((pieces * heads, rows, rows), BF),
            pltpu.SemaphoreType.DMA((pieces * heads,)),
            pltpu.SemaphoreType.DMA((pieces * heads,)),
            pltpu.SemaphoreType.DMA((pieces * heads,)),
        ],
        input_output_aliases=aliases,
        cost_estimate=pl.CostEstimate(flops=10 * E * work, transcendentals=work, bytes_accessed=6 * work),
        compiler_params=pltpu.CompilerParams(
            vmem_limit_bytes=8 * work + 16 * heads * rows * 128 * 4 + SPARE
        ),
    )(*args)


def fused(body, shapes, scalars, *arrays, scratch=(), flops=0):
    shapes = [jax.ShapeDtypeStruct(shape, kind) for shape, kind in shapes]
    scratch = [pltpu.VMEM(shape, kind) for shape, kind in scratch]
    return pl.pallas_call(
        body,
        out_shape=shapes,
        in_specs=[pl.BlockSpec(memory_space=pltpu.SMEM)]
        + [pl.BlockSpec(memory_space=pltpu.VMEM)] * len(arrays),
        out_specs=[pl.BlockSpec(memory_space=pltpu.VMEM)] * len(shapes),
        scratch_shapes=scratch,
        cost_estimate=pl.CostEstimate(flops=flops, transcendentals=0, bytes_accessed=1 << 20),
        compiler_params=pltpu.CompilerParams(vmem_limit_bytes=size_of(*arrays, *shapes, *scratch) + SPARE),
    )(scalars, *arrays)


def rows_at(index, count):
    return pl.ds(pl.multiple_of(index * count, count), count)


def normalize(values):
    center = values - jnp.mean(values, axis=-1, keepdims=True)
    r = lax.rsqrt(jnp.mean(center * center, axis=-1, keepdims=True) + EPSILON)
    return center * r, r


def pull_norm(n, r, gain, cotangent):
    dn = cotangent * gain
    return r * (dn - jnp.mean(dn, axis=-1, keepdims=True) - n * jnp.mean(dn * n, axis=-1, keepdims=True))


def project_kernel(pieces, s_ref, *refs):
    w_refs, x_refs = refs[: pieces + 1], refs[pieces + 1 : pieces + 5]
    rows_ref, turned_ref, q_ref, kv_ref, w_s = refs[pieces + 5 :]
    share, own = w_refs[0].shape[0], x_refs[0].shape[0]
    width = q_ref.shape[0]
    if pieces == 1:
        share *= 2
    for i in range(pieces - 1):
        w_s[rows_at(s_ref[1 + i], share), :] = w_refs[i][...]
    last = s_ref[pieces] * share
    half = share // 2
    w_s[pl.ds(pl.multiple_of(last, half), half), :] = w_refs[pieces - 1][...]
    w_s[pl.ds(pl.multiple_of(last + half, half), half), :] = w_refs[pieces][...]
    for i in range(4):
        rows_ref[rows_at(s_ref[0] ^ i, own), :] = x_refs[i][...]
    turned_ref[...] = w_s[...].astype(F32).T.astype(BF)
    projected = contract(turned_ref[: 3 * width, :], rows_ref[...], 1, 1)
    q_ref[...] = (projected[:width] * (E ** (-0.5))).astype(BF)
    kv_ref[0] = projected[width : 2 * width].astype(BF)
    kv_ref[1] = projected[2 * width :].astype(BF)


def feed_kernel(s_ref, mixed_ref, x_ref, o0, o1, o2, o3, pack_ref, out_ref, gains_ref, low_ref, active_ref, slope_ref, n_ref, r_ref, mine_ref, other_ref, o_s, part_s, n_s, r_s):
    index = s_ref[0]
    near = index % 2
    rows, model = x_ref.shape
    own, width = rows // 4, o0.shape[0]
    for i, ref in enumerate((o0, o1, o2, o3)):
        o_s[rows_at(index ^ i, width), :] = ref[...]
    bias = pack_ref[:, model:].astype(F32).T
    chunk = min(256, rows)
    for r0 in range(0, rows, chunk):
        rs = slice(r0, r0 + chunk)
        attended = contract(mixed_ref[:, rs].astype(F32).T.astype(BF), o_s[...], 1, 0)
        n, r = normalize(x_ref[rs, :].astype(F32) + attended)
        n_s[rs, :] = n
        r_s[rs, :] = jnp.broadcast_to(r, (chunk, 128))
        low = (n * gains_ref[0:1, :] + gains_ref[1:2, :]).astype(BF)
        low_ref[rs, :] = low
        inner = contract(low, pack_ref[:, :model], 1, 0) + bias
        below = 0.5 + 0.5 * lax.erf(inner * (0.5**0.5))
        density = jnp.exp(-0.5 * inner * inner) * 0.3989422804014327
        slope_ref[rs, :] = below + inner * density
        active = (inner * below).astype(BF)
        active_ref[rs, :] = active
        part_s[rs, :] = contract(active, out_ref[...], 1, 0)
    for f in range(2):
        here = slice(f * own, (f + 1) * own)
        n_ref[here, :] = n_s[rows_at(2 * f + near, own), :]
        r_ref[here, :] = r_s[rows_at(2 * f + near, own), :]
        mine_ref[here, :] = part_s[rows_at(2 * f + near, own), :].astype(BF)
        other_ref[here, :] = part_s[rows_at(2 * f + 1 - near, own), :].astype(BF)


def second_kernel(s_ref, a_ref, b_ref, n_ref, cot_own, cot_far, gains_ref, result_ref, second_ref, low_ref, sums_ref):
    far = s_ref[0] // 2
    own = cot_own.shape[0]
    gain1, shift1, gain2, shift2 = (gains_ref[i : i + 1, :] for i in range(4))
    sums = [jnp.zeros(gain2.shape, F32), jnp.zeros(gain2.shape, F32)]
    for f in range(2):
        here = slice(f * own, (f + 1) * own)
        hidden = n_ref[here, :] * gain1 + shift1
        n, r = normalize(hidden + (a_ref[here, :].astype(F32) + b_ref[here, :].astype(F32)))
        cot = jnp.where(far == f, cot_own[...].astype(F32), cot_far[...].astype(F32))

        @pl.when(far == f)
        def _():
            result_ref[...] = (n * gain2 + shift2).astype(BF)

        second = pull_norm(n, r, gain2, cot)
        second_ref[here, :] = second
        low_ref[here, :] = second.astype(BF)
        sums[0] += jnp.sum(cot * n, axis=0, keepdims=True)
        sums[1] += jnp.sum(cot, axis=0, keepdims=True)
    sums_ref[0:1, :] = sums[0]
    sums_ref[1:2, :] = sums[1]


def back_kernel(s_ref, low_ref, near_ref, slope_ref, pack_ref, out_ref, all_ref, inner_ref, bias_ref, mine_ref, other_ref, part_s):
    near = s_ref[0] % 2
    rows, model = slope_ref.shape
    own = rows // 4
    for f in range(2):
        here = slice(f * own, (f + 1) * own)
        all_ref[rows_at(2 * f + near, own), :] = low_ref[here, :]
        all_ref[rows_at(2 * f + 1 - near, own), :] = near_ref[here, :]
    chunk = min(256, rows)
    bias = jnp.zeros((1, model), F32)
    for r0 in range(0, rows, chunk):
        rs = slice(r0, r0 + chunk)
        grad = contract(all_ref[rs, :], out_ref[...], 1, 1).astype(BF).astype(F32)
        inner = (grad * slope_ref[rs, :]).astype(BF)
        inner_ref[rs, :] = inner
        bias += jnp.sum(inner.astype(F32), axis=0, keepdims=True)
        part_s[rs, :] = contract(inner, pack_ref[:, :model], 1, 1)
    bias_ref[...] = bias
    for f in range(2):
        here = slice(f * own, (f + 1) * own)
        mine_ref[here, :] = part_s[rows_at(2 * f + near, own), :].astype(BF)
        other_ref[here, :] = part_s[rows_at(2 * f + 1 - near, own), :].astype(BF)


def first_kernel(s_ref, a_ref, b_ref, second_ref, n_ref, r_ref, sums_ref, gains_ref, sent_ref, grad_ref):
    far = s_ref[0] // 2
    own = grad_ref.shape[0]
    gain = gains_ref[0:1, :]
    sums = [jnp.zeros(gain.shape, F32), jnp.zeros(gain.shape, F32)]
    for f in range(2):
        here = slice(f * own, (f + 1) * own)
        cot = second_ref[here, :] + (a_ref[here, :].astype(F32) + b_ref[here, :].astype(F32))
        n = n_ref[here, :]
        grad = pull_norm(n, r_ref[here, :1], gain, cot)

        @pl.when(far == f)
        def _():
            grad_ref[...] = grad

        sent_ref[here, :] = grad.astype(BF)
        sums[0] += jnp.sum(cot * n, axis=0, keepdims=True)
        sums[1] += jnp.sum(cot, axis=0, keepdims=True)
    sums = jnp.concatenate(sums + [sums_ref[...]], axis=0)
    high = sums.astype(BF).astype(F32)
    tail = jnp.concatenate([high, sums - high, jnp.zeros((8, sums.shape[1]), F32)], axis=0)
    sent_ref[2 * own :, :] = tail.astype(BF)


def mixed_kernel(s_ref, sent_ref, near_ref, mixed_ref, o_ref, do_ref, grad_w_ref, sums_ref, all_s):
    near = s_ref[0] % 2
    rows = all_s.shape[0]
    own = rows // 4
    for f in range(2):
        here = slice(f * own, (f + 1) * own)
        all_s[rows_at(2 * f + near, own), :] = sent_ref[here, :]
        all_s[rows_at(2 * f + 1 - near, own), :] = near_ref[here, :]
    do_ref[...] = contract(o_ref[...], all_s[...], 1, 1).astype(BF)
    grad_w_ref[...] = contract(mixed_ref[...], all_s[...], 1, 0)
    tail = sent_ref[2 * own :, :].astype(F32) + near_ref[2 * own :, :].astype(F32)
    sums = tail[:4] + tail[4:8]
    high = sums.astype(BF).astype(F32)
    sums_ref[...] = jnp.concatenate([high, sums - high, jnp.zeros((8, sums.shape[1]), F32)], axis=0).astype(BF)


def weight_kernel(s_ref, active_ref, second_ref, low_ref, inner_ref, out_ref):
    model = low_ref.shape[1]
    out_ref[:, :model] = contract(active_ref[...].astype(F32).T.astype(BF), second_ref[...], 1, 0).astype(BF)
    out_ref[:, model:] = contract(low_ref[...].astype(F32).T.astype(BF), inner_ref[...], 1, 0).astype(BF)


def join_kernel(half, s_ref, behind_ref, ahead_ref, up_ref, down_ref, up_out, down_out):
    if half:
        middle = up_ref.shape[0]
        up_out[:middle] = add(ahead_ref[:middle], up_ref[...])
        up_out[middle:] = ahead_ref[middle:]
        down_out[:middle] = behind_ref[:middle]
        down_out[middle:] = add(behind_ref[middle:], down_ref[...])
    else:
        up_out[...] = add(ahead_ref[...], up_ref[...])
        down_out[...] = add(behind_ref[...], down_ref[...])


def close_kernel(s_ref, part_ref, up_ref, down_ref, gq_ref, rows_ref, attn_ref, sums_ref, bias_ref, packed_ref, project_ref):
    members, block, _ = packed_ref.shape
    width, model = attn_ref.shape
    share, units = model // members, bias_ref.shape[1] // members
    project_ref[:width] = gq_ref[...]
    for w in range(2):
        total = part_ref[w].astype(F32) + up_ref[w].astype(F32) + down_ref[w].astype(F32)
        project_ref[(1 + w) * width : (2 + w) * width] = total.astype(BF)
    grads = jnp.concatenate([contract(project_ref[...], rows_ref[...], 1, 0), attn_ref[...]], axis=0).T
    high = bias_ref[...].astype(BF).astype(F32)
    low = bias_ref[...] - high
    for i in range(members):
        packed_ref[i, :share] = grads[i * share : (i + 1) * share].astype(BF)
        at = slice(i * units, (i + 1) * units)
        line = jnp.concatenate([high[:, at], low[:, at], jnp.zeros((1, model - 2 * units), F32)], axis=1)
        tail = [sums_ref[:8].astype(F32), line, jnp.zeros((block - share - 9, model), F32)]
        packed_ref[i, share:] = jnp.concatenate(tail, axis=0).astype(BF)


def input_kernel(s_ref, project_ref, turned_ref, mine_ref, other_ref, part_s):
    near = s_ref[0] % 2
    rows = part_s.shape[0]
    own = rows // 4
    cols = project_ref.shape[0]
    part_s[...] = contract(project_ref[...].astype(F32).T.astype(BF), turned_ref[:cols], 1, 0)
    for f in range(2):
        here = slice(f * own, (f + 1) * own)
        mine_ref[here, :] = part_s[rows_at(2 * f + near, own), :].astype(BF)
        other_ref[here, :] = part_s[rows_at(2 * f + 1 - near, own), :].astype(BF)


class Ring:
    def __init__(self, axis, total, size):
        self.axis, self.size = axis, size
        local = list(range(0, size, 2)) + list(range(size - 1 - size % 2, 0, -2))
        self.local = local
        self.up, self.down = [], []
        for base in range(0, total, size):
            for i in range(size):
                a, b = base + local[i], base + local[(i + 1) % size]
                self.up.append((a, b))
                self.down.append((b, a))

    def members(self, index, offsets):
        n = self.size
        mine = jnp.where(index % 2 == 0, index // 2, n - 1 - index // 2)
        place = (mine + jnp.array(offsets, jnp.int32)) % n
        return jnp.where(place < (n + 1) // 2, 2 * place, 2 * (n - 1 - place) + 1)

    def groups(self):
        if self.size == 1:
            return [[0]]
        half = self.size // 2
        return [[0]] + [[-k, k] for k in range(1, half)] + [[half]]

    def gather(self, x):
        pieces = [x]
        up = down = x
        for group in self.groups()[1:-1]:
            up, down = self.send_up(up), self.send_down(down)
            pieces += [up, down]
        return pieces + [self.send_up(halves(up, 0)[0]), self.send_down(halves(down, 0)[1])]

    def send_up(self, x):
        return lax.ppermute(x, self.axis, self.up)

    def send_down(self, x):
        return lax.ppermute(x, self.axis, self.down)


class RingSum:
    def __init__(self, ring):
        self.ring = ring

    def first(self, a, b):
        self.up, self.down, self.half = self.ring.send_up(a), self.ring.send_down(b), True

    def step(self, scalars, behind, ahead):
        kind = (behind.shape, BF)
        up, down = fused(
            functools.partial(join_kernel, self.half), [kind, kind], scalars, behind, ahead, self.up, self.down
        )
        self.up, self.down, self.half = self.ring.send_up(up), self.ring.send_down(down), False
        return up


def halves(x, axis):
    middle = x.shape[axis] // 2
    return lax.slice_in_dim(x, 0, middle, axis=axis), lax.slice_in_dim(x, middle, x.shape[axis], axis=axis)


def add(a, b):
    return (a.astype(F32) + b.astype(F32)).astype(BF)


def after(x, *earlier):
    return lax.optimization_barrier((x, *earlier))[0]


def spread_gather(x, axis, n):
    return lax.all_to_all(jnp.broadcast_to(x[None], (n,) + x.shape), axis, 0, 0, tiled=True)


def group_sum(x, axis, n):
    parts = lax.all_to_all(x.reshape(n, x.shape[0] // n, x.shape[1]), axis, 0, 0, tiled=True)
    return jnp.sum(parts.astype(F32), axis=0)


def high_low(x):
    high = x.astype(BF)
    return high, (x - high.astype(F32)).astype(BF)


class Quad:
    def __init__(self, axis):
        self.axis = axis
        index = lax.axis_index(axis)
        self.near, self.far = index % 2, index // 2
        self.flip_near = [(i, i ^ 1) for i in range(4)]
        self.flip_far = [(i, i ^ 2) for i in range(4)]

    def send_near(self, x):
        return lax.ppermute(x, self.axis, self.flip_near)

    def send_far(self, x):
        return lax.ppermute(x, self.axis, self.flip_far)


def shards(
    inputs,
    prev_logits,
    w_query,
    w_key,
    w_value,
    w_attn_out,
    w_ffn_in,
    ffn_bias,
    w_ffn_out,
    norm1_gain,
    norm1_shift,
    norm2_gain,
    norm2_shift,
    token_segment,
    segment_parent,
    out_grad,
    logit_grad,
):
    rows, heads, length = prev_logits.shape
    width = heads * E
    own, model = inputs.shape
    spread = length // rows
    nd = lax.axis_size("dp")
    share = model // nd
    data_index, tensor_index = lax.axis_index("dp"), lax.axis_index("tensor")
    tree_index, local_index = data_index // spread, data_index % spread
    nb = rows // BLOCK
    quad = Quad("tensor")
    ring, all_ring = Ring("dp", nd, spread), Ring("dp", nd, nd)
    by_ring = share % 32 == 0
    place = tensor_index.astype(jnp.int32).reshape(1)
    gains = jnp.stack([norm1_gain, norm1_shift, norm2_gain, norm2_shift])

    pack_in = jnp.concatenate([w_ffn_in, ffn_bias[:, None]], axis=1)
    pack = jnp.concatenate([w_query, w_key, w_value, w_attn_out.T], axis=1)
    pack, pack_in, gains = lax.optimization_barrier((pack, pack_in, gains))
    pack_in = lax.all_gather(pack_in, "dp", axis=0, tiled=True)
    w_out = lax.all_gather(w_ffn_out, "dp", axis=0, tiled=True)
    if by_ring:
        pieces = all_ring.gather(pack)
        owners = [o for group in all_ring.groups() for o in group]
        owners = all_ring.members(data_index, owners)
    else:
        pieces = list(spread_gather(pack, "dp", nd).reshape(2, model // 2, 4 * width))
        owners = jnp.zeros((1,), jnp.int32)
    place = jnp.concatenate([place, owners])
    near = quad.send_near(inputs)
    rows_of_four = [inputs, near, quad.send_far(inputs), quad.send_far(near)]
    rows_all, turned, q_t, kv_own = fused(
        functools.partial(project_kernel, len(pieces) - 1),
        [((rows, model), BF), ((4 * width, model), BF), ((width, rows), BF), ((2, width, rows), BF)],
        place,
        *map(apart, pieces),
        *map(apart, rows_of_four),
        scratch=[((model, 4 * width), BF)],
    )
    out_own = turned[3 * width :]

    seg = lax.dynamic_slice_in_dim(token_segment, tree_index * length, length, 0)[::BLOCK]
    parents = lax.dynamic_slice_in_dim(segment_parent, tree_index, 1, 0)[0]
    seg_rows = lax.dynamic_slice_in_dim(seg, local_index * nb, nb, 0)
    labels = jnp.arange(parents.shape[0], dtype=jnp.int32)
    one = jnp.sum(jnp.where(seg_rows[:, None] == labels[None, :], parents[None, :], 0), axis=1)
    two = jnp.sum(jnp.where(one[:, None] == labels[None, :], parents[None, :], 0), axis=1)
    act = (
        (seg[None, :] == seg_rows[:, None])
        | (seg[None, :] == one[:, None])
        | (seg[None, :] == two[:, None])
    )
    act = act.astype(jnp.int32).reshape(-1)

    prev = apart(jnp.transpose(prev_logits, (1, 0, 2)))
    up_grad = apart(jnp.transpose(logit_grad, (1, 0, 2)))
    groups = ring.groups()
    order = [o for group in groups for o in group]
    sid = ring.members(local_index, order)
    held = [[kv_own]]
    going_up = going_down = kv_own
    state = None
    for step, group in enumerate(groups):
        last = step + 1 == len(groups)
        if not last:
            if state is not None:
                going_up, going_down = lax.optimization_barrier((going_up, going_down, state[1]))[:2]
            if step + 2 == len(groups):
                held.append([ring.send_up(going_up[:1]), ring.send_down(going_down[1:])])
            else:
                going_up, going_down = ring.send_up(going_up), ring.send_down(going_down)
                held.append([going_up, going_down])
        result = attend_forward(
            sid, order.index(group[0]), act, q_t, held[step], prev, state, last, 512
        )
        state = (result[0], result[-1])
        if step == 0:
            out_grad_far = quad.send_far(after(out_grad, q_t))
            state = (state[0], after(state[1], out_grad_far))
            near = quad.send_near(out_own)
            outs = [out_own, near, quad.send_far(out_own), quad.send_far(near)]
    logits, mixed, aux = result
    pack_in, w_out, *outs = (apart(after(w, mixed)) for w in (pack_in, w_out, *outs))

    pair = (2 * own, model)
    mixed_all = lax.all_gather(mixed, "tensor", axis=0, tiled=True)
    low, active, slope, first_n, first_r, mine, other = fused(
        feed_kernel,
        [((rows, model), BF), ((rows, model), BF), ((rows, model), F32), (pair, F32), ((2 * own, 128), F32)]
        + [(pair, BF)] * 2,
        place,
        mixed_all,
        rows_all,
        *outs,
        pack_in,
        w_out,
        gains,
        scratch=[((4 * width, model), BF), ((rows, model), F32), ((rows, model), F32), ((rows, 128), F32)],
    )
    mine = add(mine, quad.send_near(other))
    output, second, second_low, sums = fused(
        second_kernel,
        [((own, model), BF), (pair, F32), (pair, BF), ((2, model), F32)],
        place,
        mine,
        quad.send_far(mine),
        first_n,
        apart(out_grad),
        apart(out_grad_far),
        gains,
    )
    second_all, inner, grad_bias, mine, other = fused(
        back_kernel,
        [((rows, model), BF), ((rows, model), BF), ((1, model), F32), (pair, BF), (pair, BF)],
        place,
        second_low,
        quad.send_near(second_low),
        slope,
        pack_in,
        w_out,
        scratch=[((rows, model), F32)],
    )
    mine = add(mine, quad.send_near(other))
    far = quad.send_far(mine)
    (weight_grads,) = fused(
        weight_kernel,
        [((model, 2 * model), BF)],
        place,
        active,
        second_all,
        low,
        after(inner, mine),
    )
    far = after(far, weight_grads)
    weight_grads = lax.psum_scatter(weight_grads, "dp", scatter_dimension=0, tiled=True)

    sent, grad_first = fused(
        first_kernel,
        [((2 * own + 16, model), BF), ((own, model), F32)],
        place,
        mine,
        far,
        second,
        first_n,
        first_r,
        sums,
        gains,
    )
    received = quad.send_near(sent)
    grad_mixed, grad_w_attn, sums = fused(
        mixed_kernel,
        [((width, rows), BF), ((width, model), F32), ((16, model), BF)],
        place,
        sent,
        received,
        mixed,
        out_own,
        scratch=[((rows, model), BF)],
    )

    state = None
    total_kv = RingSum(ring)
    for step, group in reversed(list(enumerate(groups))):
        result = attend_backward(
            sid,
            order.index(group[0]),
            act,
            q_t,
            grad_mixed,
            aux,
            [apart(kv) for kv in held[step]],
            prev,
            up_grad,
            state,
            step == 0,
            256,
        )
        state = (result[0], result[-1])
        if step + 1 == len(groups):
            total_kv.first(*result[1:-1])
        elif step > 0:
            total_kv.step(place, *result[1:-1])
    prev_grad, part, grad_query = result

    packed, grad_project = fused(
        close_kernel,
        [((nd, share + 16, model), BF), ((3 * width, rows), BF)],
        place,
        part,
        total_kv.up,
        total_kv.down,
        grad_query,
        rows_all,
        grad_w_attn,
        sums,
        grad_bias,
    )
    mine, other = fused(
        input_kernel,
        [(pair, BF), (pair, BF)],
        place,
        grad_project,
        apart(turned),
        scratch=[((rows, model), F32)],
    )
    mine, packed = lax.optimization_barrier((add(mine, quad.send_near(other)).reshape(2, own, model), packed))
    far = quad.send_far(lax.dynamic_index_in_dim(mine, 1 - quad.far, 0, keepdims=False))
    kept = lax.dynamic_index_in_dim(mine, quad.far, 0, keepdims=False)
    packed = lax.all_to_all(after(packed, far), "dp", 0, 0, tiled=True)
    grad_inputs = grad_first + (kept.astype(F32) + far.astype(F32))
    weight_grads = weight_grads.astype(F32)
    packed = jnp.sum(packed.astype(F32), axis=0)
    norms = packed[share : share + 4] + packed[share + 4 : share + 8]
    units = grad_bias.shape[1] // nd
    grad_bias = packed[share + 8, :units] + packed[share + 8, units : 2 * units]
    return (
        output,
        jnp.transpose(logits, (1, 0, 2)),
        grad_inputs,
        jnp.transpose(prev_grad, (1, 0, 2)),
        packed[:share, :width],
        packed[:share, width : 2 * width],
        packed[:share, 2 * width : 3 * width],
        packed[:share, 3 * width :].T,
        weight_grads[:, model:],
        grad_bias,
        weight_grads[:, :model],
        norms[0],
        norms[1],
        norms[2],
        norms[3],
    )


def solution(mesh):
    placed = (
        P(("dp", "tensor"), None),
        P("dp", "tensor", None),
        P("dp", "tensor"),
        P("dp", "tensor"),
        P("dp", "tensor"),
        P("tensor", "dp"),
        P("dp", "tensor"),
        P(("tensor", "dp")),
        P(("tensor", "dp"), None),
        P(),
        P(),
        P(),
        P(),
        P(),
        P(),
        P(("dp", "tensor"), None),
        P("dp", "tensor", None),
    )
    return jax.shard_map(
        shards,
        mesh=mesh,
        in_specs=placed,
        out_specs=(
            P(("dp", "tensor"), None),
            P("dp", "tensor", None),
            P(("dp", "tensor"), None),
            P("dp", "tensor", None),
            P("dp", "tensor"),
            P("dp", "tensor"),
            P("dp", "tensor"),
            P("tensor", "dp"),
            P("dp", "tensor"),
            P(("tensor", "dp")),
            P(("tensor", "dp"), None),
            P(),
            P(),
            P(),
            P(),
        ),
        check_vma=False,
    )
```

```python
import functools
import math

import jax
import jax.numpy as jnp
from jax import lax
from jax.experimental import pallas as pl
from jax.experimental.pallas import tpu as pltpu
from jax.sharding import PartitionSpec as P

E = 64
SPARE = 6 << 20
TRUNK = 2048
BLOCK = 128
EPSILON = 1e-12
LOW = -1e30

BF = jnp.bfloat16
F32 = jnp.float32


def layer_norm(values, norm_gain, norm_shift):
    center = values - jnp.mean(values, axis=-1, keepdims=True)
    spread = jnp.mean(center * center, axis=-1, keepdims=True)
    return center * lax.rsqrt(spread + EPSILON) * norm_gain + norm_shift


def size_of(*arrays):
    return sum(math.prod(a.shape) * jnp.dtype(a.dtype).itemsize for a in arrays)


def apart(x):
    return pltpu.with_memory_space_constraint(x, pltpu.HBM)


def contract(a, b, da, db):
    return lax.dot_general(a, b, (((da,), (db,)), ((), ())), preferred_element_type=F32)


def block_mask(shard, rows, act_ref, q_blocks):
    nb = rows // BLOCK
    total_blocks = act_ref.shape[0] // nb
    parts = []
    for qi in q_blocks:
        flags = [act_ref[qi * total_blocks + shard * nb + ki].astype(F32) for ki in range(nb)]
        line = jnp.concatenate([jnp.full((1, BLOCK), f, F32) for f in flags], axis=1)
        parts.append(jnp.broadcast_to(line, (BLOCK, rows)))
    return jnp.concatenate(parts, axis=0)


def in_use(shard, rows, act_ref):
    nb = rows // BLOCK
    total_blocks = act_ref.shape[0] // nb
    flags = [act_ref[qi * total_blocks + shard * nb + ki] for qi in range(nb) for ki in range(nb)]
    return functools.reduce(jnp.maximum, flags) == 1


def tile_of(ref, head, shard, rows):
    return ref.at[head, :, pl.ds(pl.multiple_of(shard * rows, BLOCK), rows)]


def read_pieces(pieces, parted, refs):
    if parted:
        return [(lambda rs: refs[0][0, rs, :], lambda rs: refs[1][0, rs, :])], refs[2:]
    return [
        (lambda rs, ref=ref: ref[0, rs, :], lambda rs, ref=ref: ref[1, rs, :]) for ref in refs[:pieces]
    ], refs[pieces:]


def forward_kernel(first, last, pieces, parted, base, rc, *refs):
    sid_ref, act_ref, q_ref = refs[:3]
    readers, refs = read_pieces(pieces, parted, refs[3:])
    prev_ref, refs = refs[0], refs[1:]
    if not first:
        carry_in, refs = refs[1], refs[2:]
    logit_ref, refs = refs[0], refs[1:]
    if last:
        mix_ref, refs = refs[0], refs[1:]
    out_ref, m_s, acc_s, kv_s, prev_s, logit_s, in_sem, out_sem = refs
    heads, rows, _ = prev_ref.shape
    count = pieces * heads

    def incoming(i):
        tile = tile_of(prev_ref, i % heads, sid_ref[base + i // heads], rows)
        return pltpu.make_async_copy(tile, prev_s.at[i], in_sem.at[i])

    def outgoing(i):
        tile = tile_of(logit_ref, i % heads, sid_ref[base + i // heads], rows)
        return pltpu.make_async_copy(logit_s.at[i], tile, out_sem.at[i])

    def used(i):
        return in_use(sid_ref[base + i // heads], rows, act_ref)

    @pl.loop(0, count)
    def _(i):
        @pl.when(used(i))
        def _():
            incoming(i).start()

    for h in range(heads):
        feature = slice(h * E, (h + 1) * E)
        for p, (keys, values) in enumerate(readers):
            kv_s[p * heads + h, :E, :] = values(feature)
            kv_s[p * heads + h, E : 2 * E, :] = jnp.ones((E, rows), BF)
            kv_s[p * heads + h, 2 * E :, :] = keys(feature)
        if first:
            m_s[h] = jnp.full((rows, 1), LOW, F32)
            acc_s[h] = jnp.zeros((rows, 2 * E), F32)
        else:
            m_s[h] = carry_in[h, :, 96:97]
            acc_s[h] = carry_in[h]

    @pl.loop(0, count)
    def _(i):
        shard, h, here = sid_ref[base + i // heads], i % heads, used(i)

        @pl.when(here)
        def _():
            incoming(i).wait()

            for r0 in range(0, rows, min(rc, rows)):
                rs = slice(r0, r0 + min(rc, rows))
                on = block_mask(shard, rows, act_ref, range(r0 // BLOCK, rs.stop // BLOCK))
                s = contract(q_ref[h, rs, :], kv_s[i, 2 * E :, :], 1, 0) + prev_s[i, rs, :].astype(F32)
                logit_s[i, rs, :] = (s * on).astype(BF)
                s = s + (on - 1.0) * (-LOW)
                m_old = m_s[h, rs, :]
                m_new = jnp.maximum(m_old, jnp.max(s, axis=1, keepdims=True))
                weight = jnp.exp(s - m_new).astype(BF)
                fix = jnp.exp(m_old - m_new)
                m_s[h, rs, :] = m_new
                acc_s[h, rs, :] = acc_s[h, rs, :] * fix + contract(weight, kv_s[i, : 2 * E, :], 1, 1)

        @pl.when(jnp.logical_not(here))
        def _():
            logit_s[i] = jnp.zeros((rows, rows), BF)

        outgoing(i).start()

    for h in range(heads):
        if last:
            total = acc_s[h, :, E : E + 1]
            out = acc_s[h, :, :E] / total
            mix_ref[h * E : (h + 1) * E, :] = out.T.astype(BF)
            out_ref[h, :, :E] = out
            out_ref[h, :, E:] = jnp.broadcast_to(m_s[h] + jnp.log(total), (rows, 128 - E))
        else:
            out_ref[h, :, :96] = acc_s[h, :, :96]
            out_ref[h, :, 96:] = jnp.broadcast_to(m_s[h], (rows, 32))

    @pl.loop(0, count)
    def _(i):
        outgoing(i).wait()


def attend_forward(sid, base, act, q_n, kvs, prev, carry, last, rc=256):
    heads, rows, length = prev.shape
    first, parted = carry is None, kvs[0].shape[0] == 1
    pieces = 1 if parted else len(kvs)
    scalars = pl.BlockSpec(memory_space=pltpu.SMEM)
    whole = pl.BlockSpec(memory_space=pltpu.VMEM)
    left = pl.BlockSpec(memory_space=pltpu.HBM)
    in_specs = [scalars, scalars, whole] + [whole] * len(kvs) + [left]
    args = [sid, act, q_n, *kvs, prev]
    aliases = {}
    if not first:
        aliases = {len(args): 0}
        in_specs += [left, whole]
        args += list(carry)
    out_shape = [jax.ShapeDtypeStruct((heads, rows, length), BF)]
    if last:
        out_shape.append(jax.ShapeDtypeStruct((heads * E, rows), BF))
    out_shape.append(jax.ShapeDtypeStruct((heads, rows, 128), F32))
    work = heads * pieces * rows * rows
    return pl.pallas_call(
        functools.partial(forward_kernel, first, last, pieces, parted, base, rc),
        out_shape=out_shape,
        in_specs=in_specs,
        out_specs=[left] + [whole] * (len(out_shape) - 1),
        scratch_shapes=[
            pltpu.VMEM((heads, rows, 1), F32),
            pltpu.VMEM((heads, rows, 128), F32),
            pltpu.VMEM((pieces * heads, 3 * E, rows), BF),
            pltpu.VMEM((pieces * heads, rows, rows), BF),
            pltpu.VMEM((pieces * heads, rows, rows), BF),
            pltpu.SemaphoreType.DMA((pieces * heads,)),
            pltpu.SemaphoreType.DMA((pieces * heads,)),
        ],
        input_output_aliases=aliases,
        cost_estimate=pl.CostEstimate(flops=4 * E * work, transcendentals=work, bytes_accessed=4 * work),
        compiler_params=pltpu.CompilerParams(
            vmem_limit_bytes=6 * work + 16 * heads * rows * 128 * 4 + SPARE
        ),
    )(*args)


def backward_kernel(first, last, pieces, parted, base, rc, *refs):
    sid_ref, act_ref, q_ref, do_ref, q_s, do_s, aux_ref = refs[:7]
    readers, refs = read_pieces(pieces, parted, refs[7:])
    prev_ref, up_ref, refs = refs[0], refs[1], refs[2:]
    if not first:
        gq_in, refs = refs[1], refs[2:]
    outputs = 2 if parted else pieces
    pg_ref, gkv_refs = refs[0], refs[1 : 1 + outputs]
    gq_ref, gq_s, p_s, kv_s, gkv_s, prev_s, up_s, pg_s, prev_sem, up_sem, out_sem = refs[1 + outputs :]
    heads, rows, _ = prev_ref.shape
    count = pieces * heads

    def incoming(i):
        at = i % heads, sid_ref[base + i // heads], rows
        return (
            pltpu.make_async_copy(tile_of(prev_ref, *at), prev_s.at[i], prev_sem.at[i]),
            pltpu.make_async_copy(tile_of(up_ref, *at), up_s.at[i], up_sem.at[i]),
        )

    def outgoing(i):
        tile = tile_of(pg_ref, i % heads, sid_ref[base + i // heads], rows)
        return pltpu.make_async_copy(pg_s.at[i], tile, out_sem.at[i])

    def used(i):
        return in_use(sid_ref[base + i // heads], rows, act_ref)

    @pl.loop(0, count)
    def _(i):
        @pl.when(used(i))
        def _():
            for copy in incoming(i):
                copy.start()

    for h in range(heads):
        feature = slice(h * E, (h + 1) * E)
        gq_s[h] = jnp.zeros((rows, E), F32) if first else gq_in[h]
        for p, (keys, values) in enumerate(readers):
            kv_s[p * heads + h, :E, :] = keys(feature)
            kv_s[p * heads + h, E:, :] = values(feature)

    @pl.loop(0, count)
    def _(i):
        shard, h, here = sid_ref[base + i // heads], i % heads, used(i)
        feature = pl.ds(pl.multiple_of(h * E, E), E)

        @pl.when(here)
        def _():
            for copy in incoming(i):
                copy.wait()
            chunk = min(rc, rows)

            @pl.loop(0, rows // chunk)
            def _(r):
                rs = pl.ds(pl.multiple_of(r * chunk, chunk), chunk)
                blocks = chunk // BLOCK
                on = block_mask(shard, rows, act_ref, [r * blocks + b for b in range(blocks)])
                s = contract(q_s[h, rs, :], kv_s[i, :E, :], 1, 0) + prev_s[i, rs, :].astype(F32)
                weight = jnp.exp(s - aux_ref[h, rs, E : E + 1] + (on - 1.0) * (-LOW))
                dp = contract(do_s[h, rs, :], kv_s[i, E:, :], 1, 0)
                upper = up_s[i, rs, :].astype(F32) * on
                pg_s[i, rs, :] = (weight * (dp - aux_ref[h, rs, :1]) + upper).astype(BF)
                p_s[rs, :] = weight.astype(BF)

            gkv_s[i, :E, :] = contract(q_ref[feature, :], pg_s[i], 1, 0).astype(BF)
            gkv_s[i, E:, :] = contract(do_ref[feature, :], p_s[...], 1, 0).astype(BF)
            gq_s[h] += contract(pg_s[i], kv_s[i, :E, :], 1, 1)

        @pl.when(jnp.logical_not(here))
        def _():
            pg_s[i] = jnp.zeros((rows, rows), BF)
            gkv_s[i] = jnp.zeros((2 * E, rows), BF)

        outgoing(i).start()

    for h in range(heads):
        feature = slice(h * E, (h + 1) * E)
        for p in range(pieces):
            for w in range(2):
                part = gkv_s[p * heads + h, w * E : (w + 1) * E, :]
                if parted:
                    gkv_refs[w][0, feature, :] = part
                else:
                    gkv_refs[p][w, feature, :] = part
        if last:
            gq_ref[feature, :] = (gq_s[h] * (E ** (-0.5))).T.astype(BF)
        else:
            gq_ref[h] = gq_s[h]

    @pl.loop(0, count)
    def _(i):
        outgoing(i).wait()


def attend_backward(sid, base, act, q_t, do_t, q_n, do_n, aux, kvs, prev, up, carry, last, rc=256):
    heads, rows, length = prev.shape
    first, parted = carry is None, kvs[0].shape[0] == 1
    pieces = 1 if parted else len(kvs)
    scalars = pl.BlockSpec(memory_space=pltpu.SMEM)
    whole = pl.BlockSpec(memory_space=pltpu.VMEM)
    left = pl.BlockSpec(memory_space=pltpu.HBM)
    in_specs = [scalars, scalars] + [whole] * (5 + len(kvs)) + [left, left]
    args = [sid, act, q_t, do_t, q_n, do_n, aux, *kvs, prev, up]
    aliases = {}
    if not first:
        aliases = {len(args): 0}
        in_specs += [left, whole]
        args += list(carry)
    out_shape = [jax.ShapeDtypeStruct((heads, rows, length), BF)]
    out_shape += [jax.ShapeDtypeStruct(kv.shape, BF) for kv in kvs]
    if last:
        out_shape.append(jax.ShapeDtypeStruct((heads * E, rows), BF))
    else:
        out_shape.append(jax.ShapeDtypeStruct((heads, rows, E), F32))
    work = heads * pieces * rows * rows
    return pl.pallas_call(
        functools.partial(backward_kernel, first, last, pieces, parted, base, rc),
        out_shape=out_shape,
        in_specs=in_specs,
        out_specs=[left] + [whole] * (len(kvs) + 1),
        scratch_shapes=[
            pltpu.VMEM((heads, rows, E), F32),
            pltpu.VMEM((rows, rows), BF),
            pltpu.VMEM((pieces * heads, 2 * E, rows), BF),
            pltpu.VMEM((pieces * heads, 2 * E, rows), BF),
            pltpu.VMEM((pieces * heads, rows, rows), BF),
            pltpu.VMEM((pieces * heads, rows, rows), BF),
            pltpu.VMEM((pieces * heads, rows, rows), BF),
            pltpu.SemaphoreType.DMA((pieces * heads,)),
            pltpu.SemaphoreType.DMA((pieces * heads,)),
            pltpu.SemaphoreType.DMA((pieces * heads,)),
        ],
        input_output_aliases=aliases,
        cost_estimate=pl.CostEstimate(flops=10 * E * work, transcendentals=work, bytes_accessed=6 * work),
        compiler_params=pltpu.CompilerParams(
            vmem_limit_bytes=8 * work + 16 * heads * rows * 128 * 4 + SPARE
        ),
    )(*args)


def fused(body, shapes, scalars, *arrays, scratch=(), flops=0):
    shapes = [jax.ShapeDtypeStruct(shape, kind) for shape, kind in shapes]
    scratch = [pltpu.VMEM(shape, kind) for shape, kind in scratch]
    return pl.pallas_call(
        body,
        out_shape=shapes,
        in_specs=[pl.BlockSpec(memory_space=pltpu.SMEM)]
        + [pl.BlockSpec(memory_space=pltpu.VMEM)] * len(arrays),
        out_specs=[pl.BlockSpec(memory_space=pltpu.VMEM)] * len(shapes),
        scratch_shapes=scratch,
        cost_estimate=pl.CostEstimate(flops=flops, transcendentals=0, bytes_accessed=1 << 20),
        compiler_params=pltpu.CompilerParams(vmem_limit_bytes=size_of(*arrays, *shapes, *scratch) + SPARE),
    )(scalars, *arrays)


def rows_at(index, count):
    return pl.ds(pl.multiple_of(index * count, count), count)


def normalize(values):
    center = values - jnp.mean(values, axis=-1, keepdims=True)
    r = lax.rsqrt(jnp.mean(center * center, axis=-1, keepdims=True) + EPSILON)
    return center * r, r


def pull_norm(n, r, gain, cotangent):
    dn = cotangent * gain
    return r * (dn - jnp.mean(dn, axis=-1, keepdims=True) - n * jnp.mean(dn * n, axis=-1, keepdims=True))


def project_kernel(pieces, s_ref, *refs):
    w_refs, x_refs = refs[: pieces + 1], refs[pieces + 1 : pieces + 5]
    rows_ref, turned_ref, q_ref, natural_ref, kv_ref, w_s = refs[pieces + 5 :]
    share, own = w_refs[0].shape[0], x_refs[0].shape[0]
    width = q_ref.shape[0]
    if pieces == 1:
        share *= 2
    for i in range(pieces - 1):
        w_s[rows_at(s_ref[1 + i], share), :] = w_refs[i][...]
    last = s_ref[pieces] * share
    half = share // 2
    w_s[pl.ds(pl.multiple_of(last, half), half), :] = w_refs[pieces - 1][...]
    w_s[pl.ds(pl.multiple_of(last + half, half), half), :] = w_refs[pieces][...]
    for i in range(4):
        rows_ref[rows_at(s_ref[0] ^ i, own), :] = x_refs[i][...]
    turned_ref[...] = w_s[...].astype(F32).T.astype(BF)
    projected = contract(turned_ref[: 3 * width, :], rows_ref[...], 1, 1)
    q_ref[...] = (projected[:width] * (E ** (-0.5))).astype(BF)
    for h in range(width // E):
        natural_ref[h] = (projected[h * E : (h + 1) * E] * (E ** (-0.5))).T.astype(BF)
    kv_ref[0] = projected[width : 2 * width].astype(BF)
    kv_ref[1] = projected[2 * width :].astype(BF)


def feed_kernel(s_ref, mixed_ref, x_ref, o0, o1, o2, o3, pack_ref, out_ref, gains_ref, low_ref, active_ref, slope_ref, n_ref, r_ref, mine_ref, other_ref, o_s, part_s, n_s, r_s):
    index = s_ref[0]
    near = index % 2
    rows, model = x_ref.shape
    own, width = rows // 4, o0.shape[0]
    for i, ref in enumerate((o0, o1, o2, o3)):
        o_s[rows_at(index ^ i, width), :] = ref[...]
    bias = pack_ref[:, model:].astype(F32).T
    chunk = min(256, rows)
    for r0 in range(0, rows, chunk):
        rs = slice(r0, r0 + chunk)
        attended = contract(mixed_ref[:, rs].astype(F32).T.astype(BF), o_s[...], 1, 0)
        n, r = normalize(x_ref[rs, :].astype(F32) + attended)
        n_s[rs, :] = n
        r_s[rs, :] = jnp.broadcast_to(r, (chunk, 128))
        low = (n * gains_ref[0:1, :] + gains_ref[1:2, :]).astype(BF)
        low_ref[rs, :] = low
        inner = contract(low, pack_ref[:, :model], 1, 0) + bias
        below = 0.5 + 0.5 * lax.erf(inner * (0.5**0.5))
        density = jnp.exp(-0.5 * inner * inner) * 0.3989422804014327
        slope_ref[rs, :] = below + inner * density
        active = (inner * below).astype(BF)
        active_ref[rs, :] = active
        part_s[rs, :] = contract(active, out_ref[...], 1, 0)
    for f in range(2):
        here = slice(f * own, (f + 1) * own)
        n_ref[here, :] = n_s[rows_at(2 * f + near, own), :]
        r_ref[here, :] = r_s[rows_at(2 * f + near, own), :]
        mine_ref[here, :] = part_s[rows_at(2 * f + near, own), :].astype(BF)
        other_ref[here, :] = part_s[rows_at(2 * f + 1 - near, own), :].astype(BF)


def second_kernel(s_ref, a_ref, b_ref, n_ref, cot_own, cot_far, gains_ref, result_ref, second_ref, low_ref, sums_ref):
    far = s_ref[0] // 2
    own = cot_own.shape[0]
    gain1, shift1, gain2, shift2 = (gains_ref[i : i + 1, :] for i in range(4))
    sums = [jnp.zeros(gain2.shape, F32), jnp.zeros(gain2.shape, F32)]
    for f in range(2):
        here = slice(f * own, (f + 1) * own)
        hidden = n_ref[here, :] * gain1 + shift1
        n, r = normalize(hidden + (a_ref[here, :].astype(F32) + b_ref[here, :].astype(F32)))
        cot = jnp.where(far == f, cot_own[...].astype(F32), cot_far[...].astype(F32))

        @pl.when(far == f)
        def _():
            result_ref[...] = (n * gain2 + shift2).astype(BF)

        second = pull_norm(n, r, gain2, cot)
        second_ref[here, :] = second
        low_ref[here, :] = second.astype(BF)
        sums[0] += jnp.sum(cot * n, axis=0, keepdims=True)
        sums[1] += jnp.sum(cot, axis=0, keepdims=True)
    sums_ref[0:1, :] = sums[0]
    sums_ref[1:2, :] = sums[1]


def back_kernel(s_ref, low_ref, near_ref, slope_ref, pack_ref, out_ref, all_ref, inner_ref, bias_ref, mine_ref, other_ref, part_s):
    near = s_ref[0] % 2
    rows, model = slope_ref.shape
    own = rows // 4
    for f in range(2):
        here = slice(f * own, (f + 1) * own)
        all_ref[rows_at(2 * f + near, own), :] = low_ref[here, :]
        all_ref[rows_at(2 * f + 1 - near, own), :] = near_ref[here, :]
    chunk = min(256, rows)
    bias = jnp.zeros((1, model), F32)
    for r0 in range(0, rows, chunk):
        rs = slice(r0, r0 + chunk)
        grad = contract(all_ref[rs, :], out_ref[...], 1, 1).astype(BF).astype(F32)
        inner = (grad * slope_ref[rs, :]).astype(BF)
        inner_ref[rs, :] = inner
        bias += jnp.sum(inner.astype(F32), axis=0, keepdims=True)
        part_s[rs, :] = contract(inner, pack_ref[:, :model], 1, 1)
    bias_ref[...] = bias
    for f in range(2):
        here = slice(f * own, (f + 1) * own)
        mine_ref[here, :] = part_s[rows_at(2 * f + near, own), :].astype(BF)
        other_ref[here, :] = part_s[rows_at(2 * f + 1 - near, own), :].astype(BF)


def first_kernel(s_ref, a_ref, b_ref, second_ref, n_ref, r_ref, sums_ref, gains_ref, sent_ref, grad_ref):
    far = s_ref[0] // 2
    own = grad_ref.shape[0]
    gain = gains_ref[0:1, :]
    sums = [jnp.zeros(gain.shape, F32), jnp.zeros(gain.shape, F32)]
    for f in range(2):
        here = slice(f * own, (f + 1) * own)
        cot = second_ref[here, :] + (a_ref[here, :].astype(F32) + b_ref[here, :].astype(F32))
        n = n_ref[here, :]
        grad = pull_norm(n, r_ref[here, :1], gain, cot)

        @pl.when(far == f)
        def _():
            grad_ref[...] = grad

        sent_ref[here, :] = grad.astype(BF)
        sums[0] += jnp.sum(cot * n, axis=0, keepdims=True)
        sums[1] += jnp.sum(cot, axis=0, keepdims=True)
    sums = jnp.concatenate(sums + [sums_ref[...]], axis=0)
    high = sums.astype(BF).astype(F32)
    tail = jnp.concatenate([high, sums - high, jnp.zeros((8, sums.shape[1]), F32)], axis=0)
    sent_ref[2 * own :, :] = tail.astype(BF)


def mixed_kernel(s_ref, sent_ref, near_ref, mixed_ref, o_ref, bias_ref, aux_ref, do_ref, natural_ref, line_ref, grad_w_ref, sums_ref, all_s):
    near = s_ref[0] % 2
    rows, model = all_s.shape
    own = rows // 4
    for f in range(2):
        here = slice(f * own, (f + 1) * own)
        all_s[rows_at(2 * f + near, own), :] = sent_ref[here, :]
        all_s[rows_at(2 * f + 1 - near, own), :] = near_ref[here, :]
    grad = contract(o_ref[...], all_s[...], 1, 1).astype(BF)
    do_ref[...] = grad
    for h in range(natural_ref.shape[0]):
        do = grad[h * E : (h + 1) * E].astype(F32).T
        natural_ref[h] = do.astype(BF)
        line_ref[h, :, :E] = jnp.broadcast_to(jnp.sum(do * aux_ref[h, :, :E], axis=1, keepdims=True), (rows, E))
        line_ref[h, :, E:] = aux_ref[h, :, E:]
    grad_w_ref[...] = contract(mixed_ref[...], all_s[...], 1, 0)
    tail = sent_ref[2 * own :, :].astype(F32) + near_ref[2 * own :, :].astype(F32)
    rest = jnp.zeros((sums_ref.shape[0] - 5, model), F32)
    sums_ref[...] = jnp.concatenate([tail[:4] + tail[4:8], bias_ref[...], rest], axis=0)


def weight_kernel(s_ref, active_ref, second_ref, low_ref, inner_ref, out_ref):
    model = low_ref.shape[1]
    out_ref[:, :model] = contract(active_ref[...].astype(F32).T.astype(BF), second_ref[...], 1, 0).astype(BF)
    out_ref[:, model:] = contract(low_ref[...].astype(F32).T.astype(BF), inner_ref[...], 1, 0).astype(BF)


def join_kernel(half, s_ref, behind_ref, ahead_ref, up_ref, down_ref, up_out, down_out):
    if half:
        middle = up_ref.shape[0]
        up_out[:middle] = add(ahead_ref[:middle], up_ref[...])
        up_out[middle:] = ahead_ref[middle:]
        down_out[:middle] = behind_ref[:middle]
        down_out[middle:] = add(behind_ref[middle:], down_ref[...])
    else:
        up_out[...] = add(ahead_ref[...], up_ref[...])
        down_out[...] = add(behind_ref[...], down_ref[...])


def close_kernel(s_ref, part_ref, up_ref, down_ref, gq_ref, rows_ref, attn_ref, *refs):
    outs, project_ref, total_s = refs[:-2], refs[-2], refs[-1]
    width = gq_ref.shape[0]
    project_ref[:width] = gq_ref[...]
    for w in range(2):
        total = part_ref[w].astype(F32) + up_ref[w].astype(F32) + down_ref[w].astype(F32)
        project_ref[(1 + w) * width : (2 + w) * width] = total.astype(BF)
    total_s[...] = jnp.concatenate([contract(project_ref[...], rows_ref[...], 1, 0), attn_ref[...]], axis=0).T
    count = len(outs) - 1
    if count == 0:
        outs[0][...] = total_s[...].astype(BF)
        return
    half = outs[0].shape[0]
    for i in range(2):
        at = pl.multiple_of(s_ref[count] * 2 * half + i * half, half)
        outs[i][...] = total_s[pl.ds(at, half), :].astype(BF)
    for i in range(1, count):
        outs[1 + i][...] = total_s[rows_at(s_ref[count - i], 2 * half), :].astype(BF)


def input_kernel(s_ref, project_ref, turned_ref, mine_ref, other_ref, part_s):
    near = s_ref[0] % 2
    rows = part_s.shape[0]
    own = rows // 4
    cols = project_ref.shape[0]
    part_s[...] = contract(project_ref[...].astype(F32).T.astype(BF), turned_ref[:cols], 1, 0)
    for f in range(2):
        here = slice(f * own, (f + 1) * own)
        mine_ref[here, :] = part_s[rows_at(2 * f + near, own), :].astype(BF)
        other_ref[here, :] = part_s[rows_at(2 * f + 1 - near, own), :].astype(BF)


class Ring:
    def __init__(self, axis, total, size):
        self.axis, self.size = axis, size
        local = list(range(0, size, 2)) + list(range(size - 1 - size % 2, 0, -2))
        self.local = local
        self.up, self.down = [], []
        for base in range(0, total, size):
            for i in range(size):
                a, b = base + local[i], base + local[(i + 1) % size]
                self.up.append((a, b))
                self.down.append((b, a))

    def members(self, index, offsets):
        n = self.size
        mine = jnp.where(index % 2 == 0, index // 2, n - 1 - index // 2)
        place = (mine + jnp.array(offsets, jnp.int32)) % n
        return jnp.where(place < (n + 1) // 2, 2 * place, 2 * (n - 1 - place) + 1)

    def groups(self):
        if self.size == 1:
            return [[0]]
        half = self.size // 2
        return [[0]] + [[-k, k] for k in range(1, half)] + [[half]]

    def gather(self, x):
        pieces = [x]
        up = down = x
        for group in self.groups()[1:-1]:
            up, down = self.send_up(up), self.send_down(down)
            pieces += [up, down]
        return pieces + [self.send_up(halves(up, 0)[0]), self.send_down(halves(down, 0)[1])]

    def send_up(self, x):
        return lax.ppermute(x, self.axis, self.up)

    def send_down(self, x):
        return lax.ppermute(x, self.axis, self.down)


class RingSum:
    def __init__(self, ring):
        self.ring = ring

    def first(self, a, b):
        self.up, self.down, self.half = self.ring.send_up(a), self.ring.send_down(b), True

    def step(self, scalars, behind, ahead):
        kind = (behind.shape, BF)
        up, down = fused(
            functools.partial(join_kernel, self.half), [kind, kind], scalars, behind, ahead, self.up, self.down
        )
        self.up, self.down, self.half = self.ring.send_up(up), self.ring.send_down(down), False
        return up, down


def halves(x, axis):
    middle = x.shape[axis] // 2
    return lax.slice_in_dim(x, 0, middle, axis=axis), lax.slice_in_dim(x, middle, x.shape[axis], axis=axis)


def add(a, b):
    return (a.astype(F32) + b.astype(F32)).astype(BF)


def after(x, *earlier):
    return lax.optimization_barrier((x, *earlier))[0]


def spread_gather(x, axis, n):
    return lax.all_to_all(jnp.broadcast_to(x[None], (n,) + x.shape), axis, 0, 0, tiled=True)


def group_sum(x, axis, n):
    parts = lax.all_to_all(x.reshape(n, x.shape[0] // n, x.shape[1]), axis, 0, 0, tiled=True)
    return jnp.sum(parts.astype(F32), axis=0)


def high_low(x):
    high = x.astype(BF)
    return high, (x - high.astype(F32)).astype(BF)


class Quad:
    def __init__(self, axis):
        self.axis = axis
        index = lax.axis_index(axis)
        self.near, self.far = index % 2, index // 2
        self.flip_near = [(i, i ^ 1) for i in range(4)]
        self.flip_far = [(i, i ^ 2) for i in range(4)]

    def send_near(self, x):
        return lax.ppermute(x, self.axis, self.flip_near)

    def send_far(self, x):
        return lax.ppermute(x, self.axis, self.flip_far)


def shards(
    inputs,
    prev_logits,
    w_query,
    w_key,
    w_value,
    w_attn_out,
    w_ffn_in,
    ffn_bias,
    w_ffn_out,
    norm1_gain,
    norm1_shift,
    norm2_gain,
    norm2_shift,
    token_segment,
    segment_parent,
    out_grad,
    logit_grad,
):
    rows, heads, length = prev_logits.shape
    width = heads * E
    own, model = inputs.shape
    spread = length // rows
    nd = lax.axis_size("dp")
    share = model // nd
    data_index, tensor_index = lax.axis_index("dp"), lax.axis_index("tensor")
    tree_index, local_index = data_index // spread, data_index % spread
    nb = rows // BLOCK
    quad = Quad("tensor")
    ring, all_ring = Ring("dp", nd, spread), Ring("dp", nd, nd)
    by_ring = share % 32 == 0
    place = tensor_index.astype(jnp.int32).reshape(1)
    gains = jnp.stack([norm1_gain, norm1_shift, norm2_gain, norm2_shift])

    seg = lax.dynamic_slice_in_dim(token_segment, tree_index * length, length, 0)[::BLOCK]
    parents = lax.dynamic_slice_in_dim(segment_parent, tree_index, 1, 0)[0]
    seg_rows = lax.dynamic_slice_in_dim(seg, local_index * nb, nb, 0)
    labels = jnp.arange(parents.shape[0], dtype=jnp.int32)
    one = jnp.sum(jnp.where(seg_rows[:, None] == labels[None, :], parents[None, :], 0), axis=1)
    two = jnp.sum(jnp.where(one[:, None] == labels[None, :], parents[None, :], 0), axis=1)
    act = (
        (seg[None, :] == seg_rows[:, None])
        | (seg[None, :] == one[:, None])
        | (seg[None, :] == two[:, None])
    )
    act = act.astype(jnp.int32).reshape(-1)
    groups = ring.groups()
    order = [o for group in groups for o in group]
    sid = ring.members(local_index, order)

    pack_in = jnp.concatenate([w_ffn_in, ffn_bias[:, None]], axis=1)
    w_out = lax.all_gather(w_ffn_out, "dp", axis=0, tiled=True)
    pack = jnp.concatenate([w_query, w_key, w_value, w_attn_out.T], axis=1)
    if by_ring:
        pieces = all_ring.gather(pack)
        pieces[2], pack_in = lax.optimization_barrier((pieces[2], pack_in))
        owners = [o for group in all_ring.groups() for o in group]
        owners = all_ring.members(data_index, owners)
    else:
        pieces = list(spread_gather(pack, "dp", nd).reshape(2, model // 2, 4 * width))
        owners = jnp.zeros((1,), jnp.int32)
    hidden_units = w_ffn_in.shape[1]
    pack_in = lax.all_gather(pack_in, "dp", axis=0, tiled=True)
    place = jnp.concatenate([place, owners])
    place, act, sid, gains = lax.optimization_barrier((place, act, sid, gains))
    near = quad.send_near(inputs)
    rows_of_four = [inputs, near, quad.send_far(inputs), quad.send_far(near)]
    rows_all, turned, q_t, q_n, kv_own = fused(
        functools.partial(project_kernel, len(pieces) - 1),
        [((rows, model), BF), ((4 * width, model), BF), ((width, rows), BF), ((heads, rows, E), BF), ((2, width, rows), BF)],
        place,
        *map(apart, pieces),
        *map(apart, rows_of_four),
        scratch=[((model, 4 * width), BF)],
    )
    out_own = turned[3 * width :]

    prev = apart(jnp.transpose(prev_logits, (1, 0, 2)))
    up_grad = apart(jnp.transpose(logit_grad, (1, 0, 2)))
    held = [[kv_own]]
    going_up = going_down = kv_own
    state = None
    for step, group in enumerate(groups):
        last = step + 1 == len(groups)
        if not last:
            if state is not None:
                going_up, going_down = lax.optimization_barrier((going_up, going_down, state[1]))[:2]
            if step + 2 == len(groups):
                held.append([ring.send_up(going_up[:1]), ring.send_down(going_down[1:])])
            else:
                going_up, going_down = ring.send_up(going_up), ring.send_down(going_down)
                held.append([going_up, going_down])
        result = attend_forward(
            sid, order.index(group[0]), act, q_n, held[step], prev, state, last, 512
        )
        state = (result[0], result[-1])
        if step == 0:
            out_grad_far = quad.send_far(after(out_grad, q_t))
            state = (state[0], after(state[1], out_grad_far))
            near = quad.send_near(out_own)
            outs = [out_own, near, quad.send_far(out_own), quad.send_far(near)]
    logits, mixed, aux = result
    pack_in, w_out, *outs = (apart(after(w, mixed)) for w in (pack_in, w_out, *outs))

    pair = (2 * own, model)
    mixed_all = lax.all_gather(mixed, "tensor", axis=0, tiled=True)
    low, active, slope, first_n, first_r, mine, other = fused(
        feed_kernel,
        [((rows, model), BF), ((rows, model), BF), ((rows, model), F32), (pair, F32), ((2 * own, 128), F32)]
        + [(pair, BF)] * 2,
        place,
        mixed_all,
        rows_all,
        *outs,
        pack_in,
        w_out,
        gains,
        scratch=[((4 * width, model), BF), ((rows, model), F32), ((rows, model), F32), ((rows, 128), F32)],
    )
    mine = add(mine, quad.send_near(other))
    output, second, second_low, sums = fused(
        second_kernel,
        [((own, model), BF), (pair, F32), (pair, BF), ((2, model), F32)],
        place,
        mine,
        quad.send_far(mine),
        apart(first_n),
        apart(out_grad),
        apart(out_grad_far),
        gains,
    )
    second_all, inner, grad_bias, mine, other = fused(
        back_kernel,
        [((rows, model), BF), ((rows, model), BF), ((1, model), F32), (pair, BF), (pair, BF)],
        place,
        second_low,
        quad.send_near(second_low),
        slope,
        pack_in,
        w_out,
        scratch=[((rows, model), F32)],
    )
    mine = add(mine, quad.send_near(other))
    far = quad.send_far(mine)
    (weight_grads,) = fused(
        weight_kernel,
        [((model, 2 * model), BF)],
        place,
        active,
        second_all,
        low,
        inner,
    )
    far = after(far, weight_grads)
    weight_grads = lax.psum_scatter(weight_grads, "dp", scatter_dimension=0, tiled=True)

    sent, grad_first = fused(
        first_kernel,
        [((2 * own + 16, model), BF), ((own, model), F32)],
        place,
        mine,
        far,
        second,
        apart(first_n),
        apart(first_r),
        sums,
        gains,
    )
    received = quad.send_near(sent)
    grad_mixed, grad_mixed_n, aux, grad_w_attn, sums = fused(
        mixed_kernel,
        [
            ((width, rows), BF),
            ((heads, rows, E), BF),
            ((heads, rows, 128), F32),
            ((width, model), F32),
            ((8, model), F32),
        ],
        place,
        sent,
        received,
        apart(mixed),
        apart(out_own),
        grad_bias,
        apart(aux),
        scratch=[((rows, model), BF)],
    )

    doublings = iter([1 << i for i in range((nd - 1).bit_length())])

    def sums_step(sums):
        bit = next(doublings, None)
        if bit is None:
            return sums
        return sums + lax.ppermute(sums, "dp", [(i, i ^ bit) for i in range(nd)])

    state = None
    total_kv = RingSum(ring)
    steps = list(reversed(range(1, len(groups))))
    steps.append(0)
    for turn, step in enumerate(steps):
        result = attend_backward(
            sid,
            order.index(groups[step][0]),
            act,
            q_t,
            grad_mixed,
            q_n,
            grad_mixed_n,
            aux,
            [apart(kv) for kv in held[step]],
            prev,
            up_grad,
            state,
            turn + 1 == len(steps),
            512,
        )
        state = (result[0], result[-1])
        if step == 0:
            part = result[1]
        elif step + 1 == len(groups):
            total_kv.first(*result[1:-1])
        else:
            sums = sums_step(sums)
            total_kv.step(after(place, sums), *result[1:-1])
    prev_grad, grad_query = result[0], result[-1]
    for _ in range(nd):
        sums = sums_step(sums)
    grad_w_out, grad_w_in = weight_grads[:, :model].astype(F32), weight_grads[:, model:].astype(F32)

    if by_ring:
        shapes = [((share // 2, 4 * width), BF)] * 2 + [((share, 4 * width), BF)] * (nd - 1)
    else:
        shapes = [((model, 4 * width), BF)]
    *parts, grad_project = fused(
        close_kernel,
        shapes + [((3 * width, rows), BF)],
        place,
        part,
        total_kv.up,
        total_kv.down,
        grad_query,
        rows_all,
        apart(grad_w_attn),
        scratch=[((model, 4 * width), F32)],
    )
    if by_ring:
        last_sum = RingSum(all_ring)
        last_sum.first(parts[0], parts[1])
        grad_project = after(grad_project, last_sum.up, last_sum.down)
    mine, other = fused(
        input_kernel,
        [(pair, BF), (pair, BF)],
        place,
        grad_project,
        apart(turned),
        scratch=[((rows, model), F32)],
    )
    mine = add(mine, quad.send_near(other)).reshape(2, own, model)
    far = quad.send_far(lax.dynamic_index_in_dim(mine, 1 - quad.far, 0, keepdims=False))
    kept = lax.dynamic_index_in_dim(mine, quad.far, 0, keepdims=False)
    grad_inputs = grad_first + (kept.astype(F32) + far.astype(F32))
    if by_ring:
        parts[3] = after(parts[3], grad_w_out, grad_w_in)
        for i in range(2, nd, 2):
            if i == 4:
                parts = lax.optimization_barrier((*parts, far))[:-1]
            last_sum.step(place, apart(parts[i + 1]), apart(parts[i]))
        grads = parts[-1].astype(F32) + (last_sum.up.astype(F32) + last_sum.down.astype(F32))
    else:
        grads = group_sum(parts[0], "dp", nd)
    grad_bias = lax.dynamic_slice_in_dim(sums[4], data_index * (hidden_units // nd), hidden_units // nd, 0)
    return (
        output,
        jnp.transpose(logits, (1, 0, 2)),
        grad_inputs,
        jnp.transpose(prev_grad, (1, 0, 2)),
        grads[:, :width],
        grads[:, width : 2 * width],
        grads[:, 2 * width : 3 * width],
        grads[:, 3 * width :].T,
        grad_w_in,
        grad_bias,
        grad_w_out,
        sums[0],
        sums[1],
        sums[2],
        sums[3],
    )


def solution(mesh):
    placed = (
        P(("dp", "tensor"), None),
        P("dp", "tensor", None),
        P("dp", "tensor"),
        P("dp", "tensor"),
        P("dp", "tensor"),
        P("tensor", "dp"),
        P("dp", "tensor"),
        P(("tensor", "dp")),
        P(("tensor", "dp"), None),
        P(),
        P(),
        P(),
        P(),
        P(),
        P(),
        P(("dp", "tensor"), None),
        P("dp", "tensor", None),
    )
    return jax.shard_map(
        shards,
        mesh=mesh,
        in_specs=placed,
        out_specs=(
            P(("dp", "tensor"), None),
            P("dp", "tensor", None),
            P(("dp", "tensor"), None),
            P("dp", "tensor", None),
            P("dp", "tensor"),
            P("dp", "tensor"),
            P("dp", "tensor"),
            P("tensor", "dp"),
            P("dp", "tensor"),
            P(("tensor", "dp")),
            P(("tensor", "dp"), None),
            P(),
            P(),
            P(),
            P(),
        ),
        check_vma=False,
    )
```

```python
import functools
import math

import jax
import jax.numpy as jnp
from jax import lax
from jax.experimental import pallas as pl
from jax.experimental.pallas import tpu as pltpu
from jax.sharding import PartitionSpec as P

E = 64
SPARE = 6 << 20
TRUNK = 2048
BLOCK = 128
EPSILON = 1e-12
LOW = -1e30

BF = jnp.bfloat16
F32 = jnp.float32


def layer_norm(values, norm_gain, norm_shift):
    center = values - jnp.mean(values, axis=-1, keepdims=True)
    spread = jnp.mean(center * center, axis=-1, keepdims=True)
    return center * lax.rsqrt(spread + EPSILON) * norm_gain + norm_shift


def size_of(*arrays):
    return sum(math.prod(a.shape) * jnp.dtype(a.dtype).itemsize for a in arrays)


def apart(x):
    return pltpu.with_memory_space_constraint(x, pltpu.HBM)


def contract(a, b, da, db):
    return lax.dot_general(a, b, (((da,), (db,)), ((), ())), preferred_element_type=F32)


def block_mask(shard, rows, act_ref, q_blocks):
    nb = rows // BLOCK
    total_blocks = act_ref.shape[0] // nb
    parts = []
    for qi in q_blocks:
        flags = [act_ref[qi * total_blocks + shard * nb + ki].astype(F32) for ki in range(nb)]
        line = jnp.concatenate([jnp.full((1, BLOCK), f, F32) for f in flags], axis=1)
        parts.append(jnp.broadcast_to(line, (BLOCK, rows)))
    return jnp.concatenate(parts, axis=0)


def in_use(shard, rows, act_ref):
    nb = rows // BLOCK
    total_blocks = act_ref.shape[0] // nb
    flags = [act_ref[qi * total_blocks + shard * nb + ki] for qi in range(nb) for ki in range(nb)]
    return functools.reduce(jnp.maximum, flags) == 1


def tile_of(ref, head, shard, rows):
    return ref.at[head, :, pl.ds(pl.multiple_of(shard * rows, BLOCK), rows)]


def read_pieces(pieces, parted, refs):
    if parted:
        return [(lambda rs: refs[0][0, rs, :], lambda rs: refs[1][0, rs, :])], refs[2:]
    return [
        (lambda rs, ref=ref: ref[0, rs, :], lambda rs, ref=ref: ref[1, rs, :]) for ref in refs[:pieces]
    ], refs[pieces:]


def forward_kernel(first, last, pieces, parted, base, rc, *refs):
    sid_ref, act_ref, q_ref = refs[:3]
    readers, refs = read_pieces(pieces, parted, refs[3:])
    prev_ref, refs = refs[0], refs[1:]
    if not first:
        carry_in, refs = refs[1], refs[2:]
    logit_ref, refs = refs[0], refs[1:]
    if last:
        mix_ref, refs = refs[0], refs[1:]
    out_ref, m_s, acc_s, kv_s, prev_s, logit_s, in_sem, out_sem = refs
    heads, rows, _ = prev_ref.shape
    count = pieces * heads

    def incoming(i):
        tile = tile_of(prev_ref, i % heads, sid_ref[base + i // heads], rows)
        return pltpu.make_async_copy(tile, prev_s.at[i], in_sem.at[i])

    def outgoing(i):
        tile = tile_of(logit_ref, i % heads, sid_ref[base + i // heads], rows)
        return pltpu.make_async_copy(logit_s.at[i], tile, out_sem.at[i])

    def used(i):
        return in_use(sid_ref[base + i // heads], rows, act_ref)

    @pl.loop(0, count)
    def _(i):
        @pl.when(used(i))
        def _():
            incoming(i).start()

    for h in range(heads):
        feature = slice(h * E, (h + 1) * E)
        for p, (keys, values) in enumerate(readers):
            kv_s[p * heads + h, :E, :] = values(feature)
            kv_s[p * heads + h, E : 2 * E, :] = jnp.ones((E, rows), BF)
            kv_s[p * heads + h, 2 * E :, :] = keys(feature)
        if first:
            m_s[h] = jnp.full((rows, 1), LOW, F32)
            acc_s[h] = jnp.zeros((rows, 2 * E), F32)
        else:
            m_s[h] = carry_in[h, :, 96:97]
            acc_s[h] = carry_in[h]

    @pl.loop(0, count)
    def _(i):
        shard, h, here = sid_ref[base + i // heads], i % heads, used(i)

        @pl.when(here)
        def _():
            incoming(i).wait()

            for r0 in range(0, rows, min(rc, rows)):
                rs = slice(r0, r0 + min(rc, rows))
                on = block_mask(shard, rows, act_ref, range(r0 // BLOCK, rs.stop // BLOCK))
                s = contract(q_ref[h, rs, :], kv_s[i, 2 * E :, :], 1, 0) + prev_s[i, rs, :].astype(F32)
                logit_s[i, rs, :] = (s * on).astype(BF)
                s = s + (on - 1.0) * (-LOW)
                m_old = m_s[h, rs, :]
                m_new = jnp.maximum(m_old, jnp.max(s, axis=1, keepdims=True))
                weight = jnp.exp(s - m_new).astype(BF)
                fix = jnp.exp(m_old - m_new)
                m_s[h, rs, :] = m_new
                acc_s[h, rs, :] = acc_s[h, rs, :] * fix + contract(weight, kv_s[i, : 2 * E, :], 1, 1)

        @pl.when(jnp.logical_not(here))
        def _():
            logit_s[i] = jnp.zeros((rows, rows), BF)

        outgoing(i).start()

    for h in range(heads):
        if last:
            total = acc_s[h, :, E : E + 1]
            out = acc_s[h, :, :E] / total
            mix_ref[h * E : (h + 1) * E, :] = out.T.astype(BF)
            out_ref[h, :, :E] = out
            out_ref[h, :, E:] = jnp.broadcast_to(m_s[h] + jnp.log(total), (rows, 128 - E))
        else:
            out_ref[h, :, :96] = acc_s[h, :, :96]
            out_ref[h, :, 96:] = jnp.broadcast_to(m_s[h], (rows, 32))

    @pl.loop(0, count)
    def _(i):
        outgoing(i).wait()


def attend_forward(sid, base, act, q_n, kvs, prev, carry, last, rc=256):
    heads, rows, length = prev.shape
    first, parted = carry is None, kvs[0].shape[0] == 1
    pieces = 1 if parted else len(kvs)
    scalars = pl.BlockSpec(memory_space=pltpu.SMEM)
    whole = pl.BlockSpec(memory_space=pltpu.VMEM)
    left = pl.BlockSpec(memory_space=pltpu.HBM)
    in_specs = [scalars, scalars, whole] + [whole] * len(kvs) + [left]
    args = [sid, act, q_n, *kvs, prev]
    aliases = {}
    if not first:
        aliases = {len(args): 0}
        in_specs += [left, whole]
        args += list(carry)
    out_shape = [jax.ShapeDtypeStruct((heads, rows, length), BF)]
    if last:
        out_shape.append(jax.ShapeDtypeStruct((heads * E, rows), BF))
    out_shape.append(jax.ShapeDtypeStruct((heads, rows, 128), F32))
    work = heads * pieces * rows * rows
    return pl.pallas_call(
        functools.partial(forward_kernel, first, last, pieces, parted, base, rc),
        out_shape=out_shape,
        in_specs=in_specs,
        out_specs=[left] + [whole] * (len(out_shape) - 1),
        scratch_shapes=[
            pltpu.VMEM((heads, rows, 1), F32),
            pltpu.VMEM((heads, rows, 128), F32),
            pltpu.VMEM((pieces * heads, 3 * E, rows), BF),
            pltpu.VMEM((pieces * heads, rows, rows), BF),
            pltpu.VMEM((pieces * heads, rows, rows), BF),
            pltpu.SemaphoreType.DMA((pieces * heads,)),
            pltpu.SemaphoreType.DMA((pieces * heads,)),
        ],
        input_output_aliases=aliases,
        cost_estimate=pl.CostEstimate(flops=4 * E * work, transcendentals=work, bytes_accessed=4 * work),
        compiler_params=pltpu.CompilerParams(
            vmem_limit_bytes=6 * work + 16 * heads * rows * 128 * 4 + SPARE
        ),
    )(*args)


def backward_kernel(first, last, pieces, parted, base, rc, *refs):
    sid_ref, act_ref, q_ref, do_ref, q_s, do_s, aux_ref = refs[:7]
    readers, refs = read_pieces(pieces, parted, refs[7:])
    prev_ref, up_ref, refs = refs[0], refs[1], refs[2:]
    if not first:
        gq_in, refs = refs[1], refs[2:]
    outputs = 2 if parted else pieces
    pg_ref, gkv_refs = refs[0], refs[1 : 1 + outputs]
    gq_ref, gq_s, p_s, kv_s, gkv_s, prev_s, up_s, pg_s, prev_sem, up_sem, out_sem = refs[1 + outputs :]
    heads, rows, _ = prev_ref.shape
    count = pieces * heads

    def incoming(i):
        at = i % heads, sid_ref[base + i // heads], rows
        return (
            pltpu.make_async_copy(tile_of(prev_ref, *at), prev_s.at[i], prev_sem.at[i]),
            pltpu.make_async_copy(tile_of(up_ref, *at), up_s.at[i], up_sem.at[i]),
        )

    def outgoing(i):
        tile = tile_of(pg_ref, i % heads, sid_ref[base + i // heads], rows)
        return pltpu.make_async_copy(pg_s.at[i], tile, out_sem.at[i])

    def used(i):
        return in_use(sid_ref[base + i // heads], rows, act_ref)

    @pl.loop(0, count)
    def _(i):
        @pl.when(used(i))
        def _():
            for copy in incoming(i):
                copy.start()

    for h in range(heads):
        feature = slice(h * E, (h + 1) * E)
        gq_s[h] = jnp.zeros((rows, E), F32) if first else gq_in[h]
        for p, (keys, values) in enumerate(readers):
            kv_s[p * heads + h, :E, :] = keys(feature)
            kv_s[p * heads + h, E:, :] = values(feature)

    @pl.loop(0, count)
    def _(i):
        shard, h, here = sid_ref[base + i // heads], i % heads, used(i)
        feature = pl.ds(pl.multiple_of(h * E, E), E)

        @pl.when(here)
        def _():
            for copy in incoming(i):
                copy.wait()
            chunk = min(rc, rows)

            @pl.loop(0, rows // chunk)
            def _(r):
                rs = pl.ds(pl.multiple_of(r * chunk, chunk), chunk)
                blocks = chunk // BLOCK
                on = block_mask(shard, rows, act_ref, [r * blocks + b for b in range(blocks)])
                s = contract(q_s[h, rs, :], kv_s[i, :E, :], 1, 0) + prev_s[i, rs, :].astype(F32)
                weight = jnp.exp(s - aux_ref[h, rs, E : E + 1] + (on - 1.0) * (-LOW))
                dp = contract(do_s[h, rs, :], kv_s[i, E:, :], 1, 0)
                upper = up_s[i, rs, :].astype(F32) * on
                pg_s[i, rs, :] = (weight * (dp - aux_ref[h, rs, :1]) + upper).astype(BF)
                p_s[rs, :] = weight.astype(BF)

            gkv_s[i, :E, :] = contract(q_ref[feature, :], pg_s[i], 1, 0).astype(BF)
            gkv_s[i, E:, :] = contract(do_ref[feature, :], p_s[...], 1, 0).astype(BF)
            gq_s[h] += contract(pg_s[i], kv_s[i, :E, :], 1, 1)

        @pl.when(jnp.logical_not(here))
        def _():
            pg_s[i] = jnp.zeros((rows, rows), BF)
            gkv_s[i] = jnp.zeros((2 * E, rows), BF)

        outgoing(i).start()

    for h in range(heads):
        feature = slice(h * E, (h + 1) * E)
        for p in range(pieces):
            for w in range(2):
                part = gkv_s[p * heads + h, w * E : (w + 1) * E, :]
                if parted:
                    gkv_refs[w][0, feature, :] = part
                else:
                    gkv_refs[p][w, feature, :] = part
        if last:
            gq_ref[feature, :] = (gq_s[h] * (E ** (-0.5))).T.astype(BF)
        else:
            gq_ref[h] = gq_s[h]

    @pl.loop(0, count)
    def _(i):
        outgoing(i).wait()


def attend_backward(sid, base, act, q_t, do_t, q_n, do_n, aux, kvs, prev, up, carry, last, rc=256):
    heads, rows, length = prev.shape
    first, parted = carry is None, kvs[0].shape[0] == 1
    pieces = 1 if parted else len(kvs)
    scalars = pl.BlockSpec(memory_space=pltpu.SMEM)
    whole = pl.BlockSpec(memory_space=pltpu.VMEM)
    left = pl.BlockSpec(memory_space=pltpu.HBM)
    in_specs = [scalars, scalars] + [whole] * (5 + len(kvs)) + [left, left]
    args = [sid, act, q_t, do_t, q_n, do_n, aux, *kvs, prev, up]
    aliases = {}
    if not first:
        aliases = {len(args): 0}
        in_specs += [left, whole]
        args += list(carry)
    out_shape = [jax.ShapeDtypeStruct((heads, rows, length), BF)]
    out_shape += [jax.ShapeDtypeStruct(kv.shape, BF) for kv in kvs]
    if last:
        out_shape.append(jax.ShapeDtypeStruct((heads * E, rows), BF))
    else:
        out_shape.append(jax.ShapeDtypeStruct((heads, rows, E), F32))
    work = heads * pieces * rows * rows
    return pl.pallas_call(
        functools.partial(backward_kernel, first, last, pieces, parted, base, rc),
        out_shape=out_shape,
        in_specs=in_specs,
        out_specs=[left] + [whole] * (len(kvs) + 1),
        scratch_shapes=[
            pltpu.VMEM((heads, rows, E), F32),
            pltpu.VMEM((rows, rows), BF),
            pltpu.VMEM((pieces * heads, 2 * E, rows), BF),
            pltpu.VMEM((pieces * heads, 2 * E, rows), BF),
            pltpu.VMEM((pieces * heads, rows, rows), BF),
            pltpu.VMEM((pieces * heads, rows, rows), BF),
            pltpu.VMEM((pieces * heads, rows, rows), BF),
            pltpu.SemaphoreType.DMA((pieces * heads,)),
            pltpu.SemaphoreType.DMA((pieces * heads,)),
            pltpu.SemaphoreType.DMA((pieces * heads,)),
        ],
        input_output_aliases=aliases,
        cost_estimate=pl.CostEstimate(flops=10 * E * work, transcendentals=work, bytes_accessed=6 * work),
        compiler_params=pltpu.CompilerParams(
            vmem_limit_bytes=8 * work + 16 * heads * rows * 128 * 4 + SPARE
        ),
    )(*args)


def fused(body, shapes, scalars, *arrays, scratch=(), flops=0):
    shapes = [jax.ShapeDtypeStruct(shape, kind) for shape, kind in shapes]
    scratch = [pltpu.VMEM(shape, kind) for shape, kind in scratch]
    return pl.pallas_call(
        body,
        out_shape=shapes,
        in_specs=[pl.BlockSpec(memory_space=pltpu.SMEM)]
        + [pl.BlockSpec(memory_space=pltpu.VMEM)] * len(arrays),
        out_specs=[pl.BlockSpec(memory_space=pltpu.VMEM)] * len(shapes),
        scratch_shapes=scratch,
        cost_estimate=pl.CostEstimate(flops=flops, transcendentals=0, bytes_accessed=1 << 20),
        compiler_params=pltpu.CompilerParams(vmem_limit_bytes=size_of(*arrays, *shapes, *scratch) + SPARE),
    )(scalars, *arrays)


def rows_at(index, count):
    return pl.ds(pl.multiple_of(index * count, count), count)


def normalize(values):
    center = values - jnp.mean(values, axis=-1, keepdims=True)
    r = lax.rsqrt(jnp.mean(center * center, axis=-1, keepdims=True) + EPSILON)
    return center * r, r


def pull_norm(n, r, gain, cotangent):
    dn = cotangent * gain
    return r * (dn - jnp.mean(dn, axis=-1, keepdims=True) - n * jnp.mean(dn * n, axis=-1, keepdims=True))


def project_kernel(pieces, s_ref, *refs):
    w_refs, x_refs = refs[: pieces + 1], refs[pieces + 1 : pieces + 5]
    rows_ref, turned_ref, q_ref, natural_ref, kv_ref, w_s = refs[pieces + 5 :]
    share, own = w_refs[0].shape[0], x_refs[0].shape[0]
    width = q_ref.shape[0]
    if pieces == 1:
        share *= 2
    for i in range(pieces - 1):
        w_s[rows_at(s_ref[1 + i], share), :] = w_refs[i][...]
    last = s_ref[pieces] * share
    half = share // 2
    w_s[pl.ds(pl.multiple_of(last, half), half), :] = w_refs[pieces - 1][...]
    w_s[pl.ds(pl.multiple_of(last + half, half), half), :] = w_refs[pieces][...]
    for i in range(4):
        rows_ref[rows_at(s_ref[0] ^ i, own), :] = x_refs[i][...]
    turned_ref[...] = w_s[...].astype(F32).T.astype(BF)
    projected = contract(turned_ref[: 3 * width, :], rows_ref[...], 1, 1)
    q_ref[...] = (projected[:width] * (E ** (-0.5))).astype(BF)
    for h in range(width // E):
        natural_ref[h] = (projected[h * E : (h + 1) * E] * (E ** (-0.5))).T.astype(BF)
    kv_ref[0] = projected[width : 2 * width].astype(BF)
    kv_ref[1] = projected[2 * width :].astype(BF)


def feed_kernel(s_ref, mixed_ref, x_ref, o0, o1, o2, o3, pack_ref, out_ref, gains_ref, low_ref, active_ref, slope_ref, n_ref, r_ref, mine_ref, other_ref, o_s, part_s, n_s, r_s):
    index = s_ref[0]
    near = index % 2
    rows, model = x_ref.shape
    own, width = rows // 4, o0.shape[0]
    for i, ref in enumerate((o0, o1, o2, o3)):
        o_s[rows_at(index ^ i, width), :] = ref[...]
    bias = pack_ref[:, model:].astype(F32).T
    chunk = min(256, rows)
    for r0 in range(0, rows, chunk):
        rs = slice(r0, r0 + chunk)
        attended = contract(mixed_ref[:, rs].astype(F32).T.astype(BF), o_s[...], 1, 0)
        n, r = normalize(x_ref[rs, :].astype(F32) + attended)
        n_s[rs, :] = n
        r_s[rs, :] = jnp.broadcast_to(r, (chunk, 128))
        low = (n * gains_ref[0:1, :] + gains_ref[1:2, :]).astype(BF)
        low_ref[rs, :] = low
        inner = contract(low, pack_ref[:, :model], 1, 0) + bias
        below = 0.5 + 0.5 * lax.erf(inner * (0.5**0.5))
        density = jnp.exp(-0.5 * inner * inner) * 0.3989422804014327
        slope_ref[rs, :] = below + inner * density
        active = (inner * below).astype(BF)
        active_ref[rs, :] = active
        part_s[rs, :] = contract(active, out_ref[...], 1, 0)
    for f in range(2):
        here = slice(f * own, (f + 1) * own)
        n_ref[here, :] = n_s[rows_at(2 * f + near, own), :]
        r_ref[here, :] = r_s[rows_at(2 * f + near, own), :]
        mine_ref[here, :] = part_s[rows_at(2 * f + near, own), :].astype(BF)
        other_ref[here, :] = part_s[rows_at(2 * f + 1 - near, own), :].astype(BF)


def second_kernel(s_ref, a_ref, b_ref, n_ref, cot_own, cot_far, gains_ref, result_ref, second_ref, low_ref, sums_ref):
    far = s_ref[0] // 2
    own = cot_own.shape[0]
    gain1, shift1, gain2, shift2 = (gains_ref[i : i + 1, :] for i in range(4))
    sums = [jnp.zeros(gain2.shape, F32), jnp.zeros(gain2.shape, F32)]
    for f in range(2):
        here = slice(f * own, (f + 1) * own)
        hidden = n_ref[here, :] * gain1 + shift1
        n, r = normalize(hidden + (a_ref[here, :].astype(F32) + b_ref[here, :].astype(F32)))
        cot = jnp.where(far == f, cot_own[...].astype(F32), cot_far[...].astype(F32))

        @pl.when(far == f)
        def _():
            result_ref[...] = (n * gain2 + shift2).astype(BF)

        second = pull_norm(n, r, gain2, cot)
        second_ref[here, :] = second
        low_ref[here, :] = second.astype(BF)
        sums[0] += jnp.sum(cot * n, axis=0, keepdims=True)
        sums[1] += jnp.sum(cot, axis=0, keepdims=True)
    sums_ref[0:1, :] = sums[0]
    sums_ref[1:2, :] = sums[1]


def back_kernel(s_ref, low_ref, near_ref, slope_ref, pack_ref, out_ref, all_ref, inner_ref, bias_ref, mine_ref, other_ref, part_s):
    near = s_ref[0] % 2
    rows, model = slope_ref.shape
    own = rows // 4
    for f in range(2):
        here = slice(f * own, (f + 1) * own)
        all_ref[rows_at(2 * f + near, own), :] = low_ref[here, :]
        all_ref[rows_at(2 * f + 1 - near, own), :] = near_ref[here, :]
    chunk = min(256, rows)
    bias = jnp.zeros((1, model), F32)
    for r0 in range(0, rows, chunk):
        rs = slice(r0, r0 + chunk)
        grad = contract(all_ref[rs, :], out_ref[...], 1, 1).astype(BF).astype(F32)
        inner = (grad * slope_ref[rs, :]).astype(BF)
        inner_ref[rs, :] = inner
        bias += jnp.sum(inner.astype(F32), axis=0, keepdims=True)
        part_s[rs, :] = contract(inner, pack_ref[:, :model], 1, 1)
    bias_ref[...] = bias
    for f in range(2):
        here = slice(f * own, (f + 1) * own)
        mine_ref[here, :] = part_s[rows_at(2 * f + near, own), :].astype(BF)
        other_ref[here, :] = part_s[rows_at(2 * f + 1 - near, own), :].astype(BF)


def first_kernel(s_ref, a_ref, b_ref, second_ref, n_ref, r_ref, sums_ref, gains_ref, sent_ref, grad_ref):
    far = s_ref[0] // 2
    own = grad_ref.shape[0]
    gain = gains_ref[0:1, :]
    sums = [jnp.zeros(gain.shape, F32), jnp.zeros(gain.shape, F32)]
    for f in range(2):
        here = slice(f * own, (f + 1) * own)
        cot = second_ref[here, :] + (a_ref[here, :].astype(F32) + b_ref[here, :].astype(F32))
        n = n_ref[here, :]
        grad = pull_norm(n, r_ref[here, :1], gain, cot)

        @pl.when(far == f)
        def _():
            grad_ref[...] = grad

        sent_ref[here, :] = grad.astype(BF)
        sums[0] += jnp.sum(cot * n, axis=0, keepdims=True)
        sums[1] += jnp.sum(cot, axis=0, keepdims=True)
    sums = jnp.concatenate(sums + [sums_ref[...]], axis=0)
    high = sums.astype(BF).astype(F32)
    tail = jnp.concatenate([high, sums - high, jnp.zeros((8, sums.shape[1]), F32)], axis=0)
    sent_ref[2 * own :, :] = tail.astype(BF)


def mixed_kernel(s_ref, sent_ref, near_ref, mixed_ref, o_ref, bias_ref, aux_ref, do_ref, natural_ref, line_ref, grad_w_ref, sums_ref, all_s):
    near = s_ref[0] % 2
    rows, model = all_s.shape
    own = rows // 4
    for f in range(2):
        here = slice(f * own, (f + 1) * own)
        all_s[rows_at(2 * f + near, own), :] = sent_ref[here, :]
        all_s[rows_at(2 * f + 1 - near, own), :] = near_ref[here, :]
    grad = contract(o_ref[...], all_s[...], 1, 1).astype(BF)
    do_ref[...] = grad
    for h in range(natural_ref.shape[0]):
        do = grad[h * E : (h + 1) * E].astype(F32).T
        natural_ref[h] = do.astype(BF)
        line_ref[h, :, :E] = jnp.broadcast_to(jnp.sum(do * aux_ref[h, :, :E], axis=1, keepdims=True), (rows, E))
        line_ref[h, :, E:] = aux_ref[h, :, E:]
    grad_w_ref[...] = contract(mixed_ref[...], all_s[...], 1, 0)
    tail = sent_ref[2 * own :, :].astype(F32) + near_ref[2 * own :, :].astype(F32)
    rest = jnp.zeros((sums_ref.shape[0] - 5, model), F32)
    sums_ref[...] = jnp.concatenate([tail[:4] + tail[4:8], bias_ref[...], rest], axis=0)


def weight_kernel(s_ref, active_ref, second_ref, low_ref, inner_ref, out_ref):
    model = low_ref.shape[1]
    out_ref[:, :model] = contract(active_ref[...].astype(F32).T.astype(BF), second_ref[...], 1, 0).astype(BF)
    out_ref[:, model:] = contract(low_ref[...].astype(F32).T.astype(BF), inner_ref[...], 1, 0).astype(BF)


def join_kernel(half, s_ref, behind_ref, ahead_ref, up_ref, down_ref, up_out, down_out):
    if half:
        middle = up_ref.shape[0]
        up_out[:middle] = add(ahead_ref[:middle], up_ref[...])
        up_out[middle:] = ahead_ref[middle:]
        down_out[:middle] = behind_ref[:middle]
        down_out[middle:] = add(behind_ref[middle:], down_ref[...])
    else:
        up_out[...] = add(ahead_ref[...], up_ref[...])
        down_out[...] = add(behind_ref[...], down_ref[...])


def close_kernel(s_ref, part_ref, up_ref, down_ref, gq_ref, rows_ref, attn_ref, turned_ref, *refs):
    outs, (mine_ref, other_ref, project_ref, total_s, part_s) = refs[:-5], refs[-5:]
    near = s_ref[0] % 2
    rows, cols = part_s.shape[0], project_ref.shape[0]
    own = rows // 4
    width = gq_ref.shape[0]
    project_ref[:width] = gq_ref[...]
    for w in range(2):
        total = part_ref[w].astype(F32) + up_ref[w].astype(F32) + down_ref[w].astype(F32)
        project_ref[(1 + w) * width : (2 + w) * width] = total.astype(BF)
    total_s[...] = jnp.concatenate([contract(project_ref[...], rows_ref[...], 1, 0), attn_ref[...]], axis=0).T
    count = len(outs) - 1
    if count == 0:
        outs[0][...] = total_s[...].astype(BF)
    else:
        half = outs[0].shape[0]
        for i in range(2):
            at = pl.multiple_of(s_ref[count] * 2 * half + i * half, half)
            outs[i][...] = total_s[pl.ds(at, half), :].astype(BF)
        for i in range(1, count):
            outs[1 + i][...] = total_s[rows_at(s_ref[count - i], 2 * half), :].astype(BF)
    part_s[...] = contract(project_ref[...].astype(F32).T.astype(BF), turned_ref[:cols], 1, 0)
    for f in range(2):
        here = slice(f * own, (f + 1) * own)
        mine_ref[here, :] = part_s[rows_at(2 * f + near, own), :].astype(BF)
        other_ref[here, :] = part_s[rows_at(2 * f + 1 - near, own), :].astype(BF)


class Ring:
    def __init__(self, axis, total, size):
        self.axis, self.size = axis, size
        local = list(range(0, size, 2)) + list(range(size - 1 - size % 2, 0, -2))
        self.local = local
        self.up, self.down = [], []
        for base in range(0, total, size):
            for i in range(size):
                a, b = base + local[i], base + local[(i + 1) % size]
                self.up.append((a, b))
                self.down.append((b, a))

    def members(self, index, offsets):
        n = self.size
        mine = jnp.where(index % 2 == 0, index // 2, n - 1 - index // 2)
        place = (mine + jnp.array(offsets, jnp.int32)) % n
        return jnp.where(place < (n + 1) // 2, 2 * place, 2 * (n - 1 - place) + 1)

    def groups(self):
        if self.size == 1:
            return [[0]]
        half = self.size // 2
        return [[0]] + [[-k, k] for k in range(1, half)] + [[half]]

    def gather(self, x):
        pieces = [x]
        up = down = x
        for group in self.groups()[1:-1]:
            up, down = self.send_up(up), self.send_down(down)
            pieces += [up, down]
        return pieces + [self.send_up(halves(up, 0)[0]), self.send_down(halves(down, 0)[1])]

    def send_up(self, x):
        return lax.ppermute(x, self.axis, self.up)

    def send_down(self, x):
        return lax.ppermute(x, self.axis, self.down)


class RingSum:
    def __init__(self, ring):
        self.ring = ring

    def first(self, a, b):
        self.up, self.down, self.half = self.ring.send_up(a), self.ring.send_down(b), True

    def step(self, scalars, behind, ahead):
        kind = (behind.shape, BF)
        up, down = fused(
            functools.partial(join_kernel, self.half), [kind, kind], scalars, behind, ahead, self.up, self.down
        )
        self.up, self.down, self.half = self.ring.send_up(up), self.ring.send_down(down), False
        return up, down


def halves(x, axis):
    middle = x.shape[axis] // 2
    return lax.slice_in_dim(x, 0, middle, axis=axis), lax.slice_in_dim(x, middle, x.shape[axis], axis=axis)


def add(a, b):
    return (a.astype(F32) + b.astype(F32)).astype(BF)


def after(x, *earlier):
    return lax.optimization_barrier((x, *earlier))[0]


def spread_gather(x, axis, n):
    return lax.all_to_all(jnp.broadcast_to(x[None], (n,) + x.shape), axis, 0, 0, tiled=True)


def group_sum(x, axis, n):
    parts = lax.all_to_all(x.reshape(n, x.shape[0] // n, x.shape[1]), axis, 0, 0, tiled=True)
    return jnp.sum(parts.astype(F32), axis=0)


def high_low(x):
    high = x.astype(BF)
    return high, (x - high.astype(F32)).astype(BF)


class Quad:
    def __init__(self, axis):
        self.axis = axis
        index = lax.axis_index(axis)
        self.near, self.far = index % 2, index // 2
        self.flip_near = [(i, i ^ 1) for i in range(4)]
        self.flip_far = [(i, i ^ 2) for i in range(4)]

    def send_near(self, x):
        return lax.ppermute(x, self.axis, self.flip_near)

    def send_far(self, x):
        return lax.ppermute(x, self.axis, self.flip_far)


def shards(
    inputs,
    prev_logits,
    w_query,
    w_key,
    w_value,
    w_attn_out,
    w_ffn_in,
    ffn_bias,
    w_ffn_out,
    norm1_gain,
    norm1_shift,
    norm2_gain,
    norm2_shift,
    token_segment,
    segment_parent,
    out_grad,
    logit_grad,
):
    rows, heads, length = prev_logits.shape
    width = heads * E
    own, model = inputs.shape
    spread = length // rows
    nd = lax.axis_size("dp")
    share = model // nd
    data_index, tensor_index = lax.axis_index("dp"), lax.axis_index("tensor")
    tree_index, local_index = data_index // spread, data_index % spread
    nb = rows // BLOCK
    quad = Quad("tensor")
    ring, all_ring = Ring("dp", nd, spread), Ring("dp", nd, nd)
    by_ring = share % 32 == 0
    place = tensor_index.astype(jnp.int32).reshape(1)
    gains = jnp.stack([norm1_gain, norm1_shift, norm2_gain, norm2_shift])

    seg = lax.dynamic_slice_in_dim(token_segment, tree_index * length, length, 0)[::BLOCK]
    parents = lax.dynamic_slice_in_dim(segment_parent, tree_index, 1, 0)[0]
    seg_rows = lax.dynamic_slice_in_dim(seg, local_index * nb, nb, 0)
    labels = jnp.arange(parents.shape[0], dtype=jnp.int32)
    one = jnp.sum(jnp.where(seg_rows[:, None] == labels[None, :], parents[None, :], 0), axis=1)
    two = jnp.sum(jnp.where(one[:, None] == labels[None, :], parents[None, :], 0), axis=1)
    act = (
        (seg[None, :] == seg_rows[:, None])
        | (seg[None, :] == one[:, None])
        | (seg[None, :] == two[:, None])
    )
    act = act.astype(jnp.int32).reshape(-1)
    groups = ring.groups()
    order = [o for group in groups for o in group]
    sid = ring.members(local_index, order)

    pack_in = jnp.concatenate([w_ffn_in, ffn_bias[:, None]], axis=1)
    w_out = lax.all_gather(w_ffn_out, "dp", axis=0, tiled=True)
    pack = jnp.concatenate([w_query, w_key, w_value, w_attn_out.T], axis=1)
    if by_ring:
        pieces = all_ring.gather(pack)
        pieces[2], pack_in = lax.optimization_barrier((pieces[2], pack_in))
        owners = [o for group in all_ring.groups() for o in group]
        owners = all_ring.members(data_index, owners)
    else:
        pieces = list(spread_gather(pack, "dp", nd).reshape(2, model // 2, 4 * width))
        owners = jnp.zeros((1,), jnp.int32)
    hidden_units = w_ffn_in.shape[1]
    pack_in = lax.all_gather(pack_in, "dp", axis=0, tiled=True)
    place = jnp.concatenate([place, owners])
    place, act, sid, gains = lax.optimization_barrier((place, act, sid, gains))
    near = quad.send_near(inputs)
    rows_of_four = [inputs, near, quad.send_far(inputs), quad.send_far(near)]
    rows_all, turned, q_t, q_n, kv_own = fused(
        functools.partial(project_kernel, len(pieces) - 1),
        [((rows, model), BF), ((4 * width, model), BF), ((width, rows), BF), ((heads, rows, E), BF), ((2, width, rows), BF)],
        place,
        *map(apart, pieces),
        *map(apart, rows_of_four),
        scratch=[((model, 4 * width), BF)],
    )
    out_own = turned[3 * width :]

    prev = apart(jnp.transpose(prev_logits, (1, 0, 2)))
    up_grad = apart(jnp.transpose(logit_grad, (1, 0, 2)))
    held = [[kv_own]]
    going_up = going_down = kv_own
    state = None
    for step, group in enumerate(groups):
        last = step + 1 == len(groups)
        if not last:
            if state is not None:
                going_up, going_down = lax.optimization_barrier((going_up, going_down, state[1]))[:2]
            if step + 2 == len(groups):
                held.append([ring.send_up(going_up[:1]), ring.send_down(going_down[1:])])
            else:
                going_up, going_down = ring.send_up(going_up), ring.send_down(going_down)
                held.append([going_up, going_down])
        result = attend_forward(
            sid, order.index(group[0]), act, q_n, held[step], prev, state, last, 512
        )
        state = (result[0], result[-1])
        if step == 0:
            out_grad_far = quad.send_far(after(out_grad, q_t))
            state = (state[0], after(state[1], out_grad_far))
            near = quad.send_near(out_own)
            outs = [out_own, near, quad.send_far(out_own), quad.send_far(near)]
    logits, mixed, aux = result
    pack_in, w_out, *outs = (apart(after(w, mixed)) for w in (pack_in, w_out, *outs))

    pair = (2 * own, model)
    mixed_all = lax.all_gather(mixed, "tensor", axis=0, tiled=True)
    low, active, slope, first_n, first_r, mine, other = fused(
        feed_kernel,
        [((rows, model), BF), ((rows, model), BF), ((rows, model), F32), (pair, F32), ((2 * own, 128), F32)]
        + [(pair, BF)] * 2,
        place,
        mixed_all,
        rows_all,
        *outs,
        pack_in,
        w_out,
        gains,
        scratch=[((4 * width, model), BF), ((rows, model), F32), ((rows, model), F32), ((rows, 128), F32)],
    )
    mine = add(mine, quad.send_near(other))
    output, second, second_low, sums = fused(
        second_kernel,
        [((own, model), BF), (pair, F32), (pair, BF), ((2, model), F32)],
        place,
        mine,
        quad.send_far(mine),
        apart(first_n),
        apart(out_grad),
        apart(out_grad_far),
        gains,
    )
    second_all, inner, grad_bias, mine, other = fused(
        back_kernel,
        [((rows, model), BF), ((rows, model), BF), ((1, model), F32), (pair, BF), (pair, BF)],
        place,
        second_low,
        quad.send_near(second_low),
        slope,
        pack_in,
        w_out,
        scratch=[((rows, model), F32)],
    )
    mine = add(mine, quad.send_near(other))
    far = quad.send_far(mine)
    (weight_grads,) = fused(
        weight_kernel,
        [((model, 2 * model), BF)],
        place,
        active,
        second_all,
        low,
        inner,
    )
    far = after(far, weight_grads)
    weight_grads = lax.psum_scatter(weight_grads, "dp", scatter_dimension=0, tiled=True)

    sent, grad_first = fused(
        first_kernel,
        [((2 * own + 16, model), BF), ((own, model), F32)],
        place,
        mine,
        far,
        second,
        apart(first_n),
        apart(first_r),
        sums,
        gains,
    )
    received = quad.send_near(sent)
    grad_mixed, grad_mixed_n, aux, grad_w_attn, sums = fused(
        mixed_kernel,
        [
            ((width, rows), BF),
            ((heads, rows, E), BF),
            ((heads, rows, 128), F32),
            ((width, model), F32),
            ((8, model), F32),
        ],
        place,
        sent,
        received,
        apart(mixed),
        apart(out_own),
        grad_bias,
        apart(aux),
        scratch=[((rows, model), BF)],
    )

    doublings = iter([1 << i for i in range((nd - 1).bit_length())])

    def sums_step(sums):
        bit = next(doublings, None)
        if bit is None:
            return sums
        return sums + lax.ppermute(sums, "dp", [(i, i ^ bit) for i in range(nd)])

    state = None
    total_kv = RingSum(ring)
    steps = list(reversed(range(1, len(groups))))
    steps.append(0)
    for turn, step in enumerate(steps):
        result = attend_backward(
            sid,
            order.index(groups[step][0]),
            act,
            q_t,
            grad_mixed,
            q_n,
            grad_mixed_n,
            aux,
            [apart(kv) for kv in held[step]],
            prev,
            up_grad,
            state,
            turn + 1 == len(steps),
            512,
        )
        state = (result[0], result[-1])
        if step == 0:
            part = result[1]
        elif step + 1 == len(groups):
            total_kv.first(*result[1:-1])
        else:
            sums = sums_step(sums)
            total_kv.step(after(place, sums), *result[1:-1])
    prev_grad, grad_query = result[0], result[-1]
    for _ in range(nd):
        sums = sums_step(sums)
    grad_w_out, grad_w_in = weight_grads[:, :model].astype(F32), weight_grads[:, model:].astype(F32)

    if by_ring:
        shapes = [((share // 2, 4 * width), BF)] * 2 + [((share, 4 * width), BF)] * (nd - 1)
    else:
        shapes = [((model, 4 * width), BF)]
    *parts, mine, other = fused(
        close_kernel,
        shapes + [(pair, BF), (pair, BF)],
        place,
        part,
        total_kv.up,
        total_kv.down,
        grad_query,
        rows_all,
        apart(grad_w_attn),
        apart(turned),
        scratch=[((3 * width, rows), BF), ((model, 4 * width), F32), ((rows, model), F32)],
    )
    if by_ring:
        last_sum = RingSum(all_ring)
        last_sum.first(parts[0], parts[1])
    mine = add(mine, quad.send_near(other)).reshape(2, own, model)
    far = quad.send_far(lax.dynamic_index_in_dim(mine, 1 - quad.far, 0, keepdims=False))
    kept = lax.dynamic_index_in_dim(mine, quad.far, 0, keepdims=False)
    grad_inputs = grad_first + (kept.astype(F32) + far.astype(F32))
    if by_ring:
        for i in range(2, nd, 2):
            scalars = after(place, *((far,) if i == 4 else (grad_w_out, grad_w_in) if i == 6 else ()))
            last_sum.step(scalars, parts[i + 1], parts[i])
        grads = parts[-1].astype(F32) + (last_sum.up.astype(F32) + last_sum.down.astype(F32))
    else:
        grads = group_sum(parts[0], "dp", nd)
    grad_bias = lax.dynamic_slice_in_dim(sums[4], data_index * (hidden_units // nd), hidden_units // nd, 0)
    return (
        output,
        jnp.transpose(logits, (1, 0, 2)),
        grad_inputs,
        jnp.transpose(prev_grad, (1, 0, 2)),
        grads[:, :width],
        grads[:, width : 2 * width],
        grads[:, 2 * width : 3 * width],
        grads[:, 3 * width :].T,
        grad_w_in,
        grad_bias,
        grad_w_out,
        sums[0],
        sums[1],
        sums[2],
        sums[3],
    )


def solution(mesh):
    placed = (
        P(("dp", "tensor"), None),
        P("dp", "tensor", None),
        P("dp", "tensor"),
        P("dp", "tensor"),
        P("dp", "tensor"),
        P("tensor", "dp"),
        P("dp", "tensor"),
        P(("tensor", "dp")),
        P(("tensor", "dp"), None),
        P(),
        P(),
        P(),
        P(),
        P(),
        P(),
        P(("dp", "tensor"), None),
        P("dp", "tensor", None),
    )
    return jax.shard_map(
        shards,
        mesh=mesh,
        in_specs=placed,
        out_specs=(
            P(("dp", "tensor"), None),
            P("dp", "tensor", None),
            P(("dp", "tensor"), None),
            P("dp", "tensor", None),
            P("dp", "tensor"),
            P("dp", "tensor"),
            P("dp", "tensor"),
            P("tensor", "dp"),
            P("dp", "tensor"),
            P(("tensor", "dp")),
            P(("tensor", "dp"), None),
            P(),
            P(),
            P(),
            P(),
        ),
        check_vma=False,
    )
```

```python
import functools
import math

import jax
import jax.numpy as jnp
from jax import lax
from jax.experimental import pallas as pl
from jax.experimental.pallas import tpu as pltpu
from jax.sharding import PartitionSpec as P

E = 64
SPARE = 6 << 20
TRUNK = 2048
BLOCK = 128
EPSILON = 1e-12
LOW = -1e30

BF = jnp.bfloat16
F32 = jnp.float32


def layer_norm(values, norm_gain, norm_shift):
    center = values - jnp.mean(values, axis=-1, keepdims=True)
    spread = jnp.mean(center * center, axis=-1, keepdims=True)
    return center * lax.rsqrt(spread + EPSILON) * norm_gain + norm_shift


def size_of(*arrays):
    return sum(math.prod(a.shape) * jnp.dtype(a.dtype).itemsize for a in arrays)


def apart(x):
    return pltpu.with_memory_space_constraint(x, pltpu.HBM)


def contract(a, b, da, db):
    return lax.dot_general(a, b, (((da,), (db,)), ((), ())), preferred_element_type=F32)


def block_mask(shard, rows, act_ref, q_blocks):
    nb = rows // BLOCK
    total_blocks = act_ref.shape[0] // nb
    parts = []
    for qi in q_blocks:
        flags = [act_ref[qi * total_blocks + shard * nb + ki].astype(F32) for ki in range(nb)]
        line = jnp.concatenate([jnp.full((1, BLOCK), f, F32) for f in flags], axis=1)
        parts.append(jnp.broadcast_to(line, (BLOCK, rows)))
    return jnp.concatenate(parts, axis=0)


def in_use(shard, rows, act_ref):
    nb = rows // BLOCK
    total_blocks = act_ref.shape[0] // nb
    flags = [act_ref[qi * total_blocks + shard * nb + ki] for qi in range(nb) for ki in range(nb)]
    return functools.reduce(jnp.maximum, flags) == 1


def tile_of(ref, head, shard, rows):
    return ref.at[head, :, pl.ds(pl.multiple_of(shard * rows, BLOCK), rows)]


def read_pieces(pieces, parted, refs):
    if parted:
        return [(lambda rs: refs[0][0, rs, :], lambda rs: refs[1][0, rs, :])], refs[2:]
    return [
        (lambda rs, ref=ref: ref[0, rs, :], lambda rs, ref=ref: ref[1, rs, :]) for ref in refs[:pieces]
    ], refs[pieces:]


def forward_kernel(first, last, pieces, parted, base, rc, *refs):
    sid_ref, act_ref, q_ref = refs[:3]
    readers, refs = read_pieces(pieces, parted, refs[3:])
    prev_ref, refs = refs[0], refs[1:]
    if not first:
        carry_in, refs = refs[1], refs[2:]
    logit_ref, refs = refs[0], refs[1:]
    if last:
        mix_ref, refs = refs[0], refs[1:]
    out_ref, m_s, acc_s, kv_s, prev_s, logit_s, in_sem, out_sem = refs
    heads, rows, _ = prev_ref.shape
    count = pieces * heads

    def incoming(i):
        tile = tile_of(prev_ref, i % heads, sid_ref[base + i // heads], rows)
        return pltpu.make_async_copy(tile, prev_s.at[i], in_sem.at[i])

    def outgoing(i):
        tile = tile_of(logit_ref, i % heads, sid_ref[base + i // heads], rows)
        return pltpu.make_async_copy(logit_s.at[i], tile, out_sem.at[i])

    def used(i):
        return in_use(sid_ref[base + i // heads], rows, act_ref)

    @pl.loop(0, count)
    def _(i):
        @pl.when(used(i))
        def _():
            incoming(i).start()

    for h in range(heads):
        feature = slice(h * E, (h + 1) * E)
        for p, (keys, values) in enumerate(readers):
            kv_s[p * heads + h, :E, :] = values(feature)
            kv_s[p * heads + h, E : 2 * E, :] = jnp.ones((E, rows), BF)
            kv_s[p * heads + h, 2 * E :, :] = keys(feature)
        if first:
            m_s[h] = jnp.full((rows, 1), LOW, F32)
            acc_s[h] = jnp.zeros((rows, 2 * E), F32)
        else:
            m_s[h] = carry_in[h, :, 96:97]
            acc_s[h] = carry_in[h]

    @pl.loop(0, count)
    def _(i):
        shard, h, here = sid_ref[base + i // heads], i % heads, used(i)

        @pl.when(here)
        def _():
            incoming(i).wait()

            for r0 in range(0, rows, min(rc, rows)):
                rs = slice(r0, r0 + min(rc, rows))
                on = block_mask(shard, rows, act_ref, range(r0 // BLOCK, rs.stop // BLOCK))
                s = contract(q_ref[h, rs, :], kv_s[i, 2 * E :, :], 1, 0) + prev_s[i, rs, :].astype(F32)
                logit_s[i, rs, :] = (s * on).astype(BF)
                s = s + (on - 1.0) * (-LOW)
                m_old = m_s[h, rs, :]
                m_new = jnp.maximum(m_old, jnp.max(s, axis=1, keepdims=True))
                weight = jnp.exp(s - m_new).astype(BF)
                fix = jnp.exp(m_old - m_new)
                m_s[h, rs, :] = m_new
                acc_s[h, rs, :] = acc_s[h, rs, :] * fix + contract(weight, kv_s[i, : 2 * E, :], 1, 1)

        @pl.when(jnp.logical_not(here))
        def _():
            logit_s[i] = jnp.zeros((rows, rows), BF)

        outgoing(i).start()

    for h in range(heads):
        if last:
            total = acc_s[h, :, E : E + 1]
            out = acc_s[h, :, :E] / total
            mix_ref[h * E : (h + 1) * E, :] = out.T.astype(BF)
            out_ref[h, :, :E] = out
            out_ref[h, :, E:] = jnp.broadcast_to(m_s[h] + jnp.log(total), (rows, 128 - E))
        else:
            out_ref[h, :, :96] = acc_s[h, :, :96]
            out_ref[h, :, 96:] = jnp.broadcast_to(m_s[h], (rows, 32))

    @pl.loop(0, count)
    def _(i):
        outgoing(i).wait()


def attend_forward(sid, base, act, q_n, kvs, prev, carry, last, rc=256):
    heads, rows, length = prev.shape
    first, parted = carry is None, kvs[0].shape[0] == 1
    pieces = 1 if parted else len(kvs)
    scalars = pl.BlockSpec(memory_space=pltpu.SMEM)
    whole = pl.BlockSpec(memory_space=pltpu.VMEM)
    left = pl.BlockSpec(memory_space=pltpu.HBM)
    in_specs = [scalars, scalars, whole] + [whole] * len(kvs) + [left]
    args = [sid, act, q_n, *kvs, prev]
    aliases = {}
    if not first:
        aliases = {len(args): 0}
        in_specs += [left, whole]
        args += list(carry)
    out_shape = [jax.ShapeDtypeStruct((heads, rows, length), BF)]
    if last:
        out_shape.append(jax.ShapeDtypeStruct((heads * E, rows), BF))
    out_shape.append(jax.ShapeDtypeStruct((heads, rows, 128), F32))
    work = heads * pieces * rows * rows
    return pl.pallas_call(
        functools.partial(forward_kernel, first, last, pieces, parted, base, rc),
        out_shape=out_shape,
        in_specs=in_specs,
        out_specs=[left] + [whole] * (len(out_shape) - 1),
        scratch_shapes=[
            pltpu.VMEM((heads, rows, 1), F32),
            pltpu.VMEM((heads, rows, 128), F32),
            pltpu.VMEM((pieces * heads, 3 * E, rows), BF),
            pltpu.VMEM((pieces * heads, rows, rows), BF),
            pltpu.VMEM((pieces * heads, rows, rows), BF),
            pltpu.SemaphoreType.DMA((pieces * heads,)),
            pltpu.SemaphoreType.DMA((pieces * heads,)),
        ],
        input_output_aliases=aliases,
        cost_estimate=pl.CostEstimate(flops=4 * E * work, transcendentals=work, bytes_accessed=4 * work),
        compiler_params=pltpu.CompilerParams(
            vmem_limit_bytes=6 * work + 16 * heads * rows * 128 * 4 + SPARE
        ),
    )(*args)


def backward_kernel(first, last, pieces, parted, base, rc, *refs):
    sid_ref, act_ref, q_ref, do_ref, q_s, do_s, aux_ref = refs[:7]
    readers, refs = read_pieces(pieces, parted, refs[7:])
    prev_ref, up_ref, refs = refs[0], refs[1], refs[2:]
    if not first:
        gq_in, refs = refs[1], refs[2:]
    outputs = 2 if parted else pieces
    pg_ref, gkv_refs = refs[0], refs[1 : 1 + outputs]
    gq_ref, gq_s, p_s, kv_s, gkv_s, prev_s, up_s, pg_s, prev_sem, up_sem, out_sem = refs[1 + outputs :]
    heads, rows, _ = prev_ref.shape
    count = pieces * heads

    def incoming(i):
        at = i % heads, sid_ref[base + i // heads], rows
        return (
            pltpu.make_async_copy(tile_of(prev_ref, *at), prev_s.at[i], prev_sem.at[i]),
            pltpu.make_async_copy(tile_of(up_ref, *at), up_s.at[i], up_sem.at[i]),
        )

    def outgoing(i):
        tile = tile_of(pg_ref, i % heads, sid_ref[base + i // heads], rows)
        return pltpu.make_async_copy(pg_s.at[i], tile, out_sem.at[i])

    def used(i):
        return in_use(sid_ref[base + i // heads], rows, act_ref)

    @pl.loop(0, count)
    def _(i):
        @pl.when(used(i))
        def _():
            for copy in incoming(i):
                copy.start()

    for h in range(heads):
        feature = slice(h * E, (h + 1) * E)
        gq_s[h] = jnp.zeros((rows, E), F32) if first else gq_in[h]
        for p, (keys, values) in enumerate(readers):
            kv_s[p * heads + h, :E, :] = keys(feature)
            kv_s[p * heads + h, E:, :] = values(feature)

    @pl.loop(0, count)
    def _(i):
        shard, h, here = sid_ref[base + i // heads], i % heads, used(i)
        feature = pl.ds(pl.multiple_of(h * E, E), E)

        @pl.when(here)
        def _():
            for copy in incoming(i):
                copy.wait()
            chunk = min(rc, rows)

            @pl.loop(0, rows // chunk)
            def _(r):
                rs = pl.ds(pl.multiple_of(r * chunk, chunk), chunk)
                blocks = chunk // BLOCK
                on = block_mask(shard, rows, act_ref, [r * blocks + b for b in range(blocks)])
                s = contract(q_s[h, rs, :], kv_s[i, :E, :], 1, 0) + prev_s[i, rs, :].astype(F32)
                weight = jnp.exp(s - aux_ref[h, rs, E : E + 1] + (on - 1.0) * (-LOW))
                dp = contract(do_s[h, rs, :], kv_s[i, E:, :], 1, 0)
                upper = up_s[i, rs, :].astype(F32) * on
                pg_s[i, rs, :] = (weight * (dp - aux_ref[h, rs, :1]) + upper).astype(BF)
                p_s[rs, :] = weight.astype(BF)

            gkv_s[i, :E, :] = contract(q_ref[feature, :], pg_s[i], 1, 0).astype(BF)
            gkv_s[i, E:, :] = contract(do_ref[feature, :], p_s[...], 1, 0).astype(BF)
            gq_s[h] += contract(pg_s[i], kv_s[i, :E, :], 1, 1)

        @pl.when(jnp.logical_not(here))
        def _():
            pg_s[i] = jnp.zeros((rows, rows), BF)
            gkv_s[i] = jnp.zeros((2 * E, rows), BF)

        outgoing(i).start()

    for h in range(heads):
        feature = slice(h * E, (h + 1) * E)
        for p in range(pieces):
            for w in range(2):
                part = gkv_s[p * heads + h, w * E : (w + 1) * E, :]
                if parted:
                    gkv_refs[w][0, feature, :] = part
                else:
                    gkv_refs[p][w, feature, :] = part
        if last:
            gq_ref[feature, :] = (gq_s[h] * (E ** (-0.5))).T.astype(BF)
        else:
            gq_ref[h] = gq_s[h]

    @pl.loop(0, count)
    def _(i):
        outgoing(i).wait()


def attend_backward(sid, base, act, q_t, do_t, q_n, do_n, aux, kvs, prev, up, carry, last, rc=256):
    heads, rows, length = prev.shape
    first, parted = carry is None, kvs[0].shape[0] == 1
    pieces = 1 if parted else len(kvs)
    scalars = pl.BlockSpec(memory_space=pltpu.SMEM)
    whole = pl.BlockSpec(memory_space=pltpu.VMEM)
    left = pl.BlockSpec(memory_space=pltpu.HBM)
    in_specs = [scalars, scalars] + [whole] * (5 + len(kvs)) + [left, left]
    args = [sid, act, q_t, do_t, q_n, do_n, aux, *kvs, prev, up]
    aliases = {}
    if not first:
        aliases = {len(args): 0}
        in_specs += [left, whole]
        args += list(carry)
    out_shape = [jax.ShapeDtypeStruct((heads, rows, length), BF)]
    out_shape += [jax.ShapeDtypeStruct(kv.shape, BF) for kv in kvs]
    if last:
        out_shape.append(jax.ShapeDtypeStruct((heads * E, rows), BF))
    else:
        out_shape.append(jax.ShapeDtypeStruct((heads, rows, E), F32))
    work = heads * pieces * rows * rows
    return pl.pallas_call(
        functools.partial(backward_kernel, first, last, pieces, parted, base, rc),
        out_shape=out_shape,
        in_specs=in_specs,
        out_specs=[left] + [whole] * (len(kvs) + 1),
        scratch_shapes=[
            pltpu.VMEM((heads, rows, E), F32),
            pltpu.VMEM((rows, rows), BF),
            pltpu.VMEM((pieces * heads, 2 * E, rows), BF),
            pltpu.VMEM((pieces * heads, 2 * E, rows), BF),
            pltpu.VMEM((pieces * heads, rows, rows), BF),
            pltpu.VMEM((pieces * heads, rows, rows), BF),
            pltpu.VMEM((pieces * heads, rows, rows), BF),
            pltpu.SemaphoreType.DMA((pieces * heads,)),
            pltpu.SemaphoreType.DMA((pieces * heads,)),
            pltpu.SemaphoreType.DMA((pieces * heads,)),
        ],
        input_output_aliases=aliases,
        cost_estimate=pl.CostEstimate(flops=10 * E * work, transcendentals=work, bytes_accessed=6 * work),
        compiler_params=pltpu.CompilerParams(
            vmem_limit_bytes=8 * work + 16 * heads * rows * 128 * 4 + SPARE
        ),
    )(*args)


def fused(body, shapes, scalars, *arrays, scratch=(), flops=0):
    shapes = [jax.ShapeDtypeStruct(shape, kind) for shape, kind in shapes]
    scratch = [pltpu.VMEM(shape, kind) for shape, kind in scratch]
    return pl.pallas_call(
        body,
        out_shape=shapes,
        in_specs=[pl.BlockSpec(memory_space=pltpu.SMEM)]
        + [pl.BlockSpec(memory_space=pltpu.VMEM)] * len(arrays),
        out_specs=[pl.BlockSpec(memory_space=pltpu.VMEM)] * len(shapes),
        scratch_shapes=scratch,
        cost_estimate=pl.CostEstimate(flops=flops, transcendentals=0, bytes_accessed=1 << 20),
        compiler_params=pltpu.CompilerParams(vmem_limit_bytes=size_of(*arrays, *shapes, *scratch) + SPARE),
    )(scalars, *arrays)


def rows_at(index, count):
    return pl.ds(pl.multiple_of(index * count, count), count)


def normalize(values):
    center = values - jnp.mean(values, axis=-1, keepdims=True)
    r = lax.rsqrt(jnp.mean(center * center, axis=-1, keepdims=True) + EPSILON)
    return center * r, r


def pull_norm(n, r, gain, cotangent):
    dn = cotangent * gain
    return r * (dn - jnp.mean(dn, axis=-1, keepdims=True) - n * jnp.mean(dn * n, axis=-1, keepdims=True))


def pack_kernel(s_ref, query_ref, key_ref, value_ref, out_ref, pack_ref):
    turned = out_ref[...].astype(F32).T
    parts = [ref[...].astype(F32) for ref in (query_ref, key_ref, value_ref)]
    pack_ref[...] = jnp.concatenate([*parts, turned], axis=1).astype(BF)


def finish_kernel(s_ref, part_ref, up_ref, down_ref, query_ref, key_ref, value_ref, out_ref):
    width = query_ref.shape[1]
    total = part_ref[...].astype(F32) + (up_ref[...].astype(F32) + down_ref[...].astype(F32))
    for i, ref in enumerate((query_ref, key_ref, value_ref)):
        ref[...] = total[:, i * width : (i + 1) * width]
    out_ref[...] = total[:, 3 * width :].T


def project_kernel(pieces, s_ref, *refs):
    w_refs, x_refs = refs[: pieces + 1], refs[pieces + 1 : pieces + 5]
    rows_ref, turned_ref, q_ref, natural_ref, kv_ref, w_s = refs[pieces + 5 :]
    share, own = w_refs[0].shape[0], x_refs[0].shape[0]
    width = q_ref.shape[0]
    if pieces == 1:
        share *= 2
    for i in range(pieces - 1):
        w_s[rows_at(s_ref[1 + i], share), :] = w_refs[i][...]
    last = s_ref[pieces] * share
    half = share // 2
    w_s[pl.ds(pl.multiple_of(last, half), half), :] = w_refs[pieces - 1][...]
    w_s[pl.ds(pl.multiple_of(last + half, half), half), :] = w_refs[pieces][...]
    for i in range(4):
        rows_ref[rows_at(s_ref[0] ^ i, own), :] = x_refs[i][...]
    turned_ref[...] = w_s[...].astype(F32).T.astype(BF)
    projected = contract(turned_ref[: 3 * width, :], rows_ref[...], 1, 1)
    q_ref[...] = (projected[:width] * (E ** (-0.5))).astype(BF)
    for h in range(width // E):
        natural_ref[h] = (projected[h * E : (h + 1) * E] * (E ** (-0.5))).T.astype(BF)
    kv_ref[0] = projected[width : 2 * width].astype(BF)
    kv_ref[1] = projected[2 * width :].astype(BF)


def feed_kernel(s_ref, mixed_ref, x_ref, o0, o1, o2, o3, pack_ref, out_ref, gains_ref, low_ref, active_ref, slope_ref, n_ref, r_ref, mine_ref, other_ref, o_s, part_s, n_s, r_s):
    index = s_ref[0]
    near = index % 2
    rows, model = x_ref.shape
    own, width = rows // 4, o0.shape[0]
    for i, ref in enumerate((o0, o1, o2, o3)):
        o_s[rows_at(index ^ i, width), :] = ref[...]
    bias = pack_ref[:, model:].astype(F32).T
    chunk = min(256, rows)
    for r0 in range(0, rows, chunk):
        rs = slice(r0, r0 + chunk)
        attended = contract(mixed_ref[:, rs].astype(F32).T.astype(BF), o_s[...], 1, 0)
        n, r = normalize(x_ref[rs, :].astype(F32) + attended)
        n_s[rs, :] = n
        r_s[rs, :] = jnp.broadcast_to(r, (chunk, 128))
        low = (n * gains_ref[0:1, :] + gains_ref[1:2, :]).astype(BF)
        low_ref[rs, :] = low
        inner = contract(low, pack_ref[:, :model], 1, 0) + bias
        below = 0.5 + 0.5 * lax.erf(inner * (0.5**0.5))
        density = jnp.exp(-0.5 * inner * inner) * 0.3989422804014327
        slope_ref[rs, :] = below + inner * density
        active = (inner * below).astype(BF)
        active_ref[rs, :] = active
        part_s[rs, :] = contract(active, out_ref[...], 1, 0)
    for f in range(2):
        here = slice(f * own, (f + 1) * own)
        n_ref[here, :] = n_s[rows_at(2 * f + near, own), :]
        r_ref[here, :] = r_s[rows_at(2 * f + near, own), :]
        mine_ref[here, :] = part_s[rows_at(2 * f + near, own), :].astype(BF)
        other_ref[here, :] = part_s[rows_at(2 * f + 1 - near, own), :].astype(BF)


def second_kernel(s_ref, a_ref, b_ref, n_ref, cot_own, cot_far, gains_ref, result_ref, second_ref, low_ref, sums_ref):
    far = s_ref[0] // 2
    own = cot_own.shape[0]
    gain1, shift1, gain2, shift2 = (gains_ref[i : i + 1, :] for i in range(4))
    sums = [jnp.zeros(gain2.shape, F32), jnp.zeros(gain2.shape, F32)]
    for f in range(2):
        here = slice(f * own, (f + 1) * own)
        hidden = n_ref[here, :] * gain1 + shift1
        n, r = normalize(hidden + (a_ref[here, :].astype(F32) + b_ref[here, :].astype(F32)))
        cot = jnp.where(far == f, cot_own[...].astype(F32), cot_far[...].astype(F32))

        @pl.when(far == f)
        def _():
            result_ref[...] = (n * gain2 + shift2).astype(BF)

        second = pull_norm(n, r, gain2, cot)
        second_ref[here, :] = second
        low_ref[here, :] = second.astype(BF)
        sums[0] += jnp.sum(cot * n, axis=0, keepdims=True)
        sums[1] += jnp.sum(cot, axis=0, keepdims=True)
    sums_ref[0:1, :] = sums[0]
    sums_ref[1:2, :] = sums[1]


def back_kernel(s_ref, low_ref, near_ref, slope_ref, pack_ref, out_ref, all_ref, inner_ref, bias_ref, mine_ref, other_ref, part_s):
    near = s_ref[0] % 2
    rows, model = slope_ref.shape
    own = rows // 4
    for f in range(2):
        here = slice(f * own, (f + 1) * own)
        all_ref[rows_at(2 * f + near, own), :] = low_ref[here, :]
        all_ref[rows_at(2 * f + 1 - near, own), :] = near_ref[here, :]
    chunk = min(256, rows)
    bias = jnp.zeros((1, model), F32)
    for r0 in range(0, rows, chunk):
        rs = slice(r0, r0 + chunk)
        grad = contract(all_ref[rs, :], out_ref[...], 1, 1).astype(BF).astype(F32)
        inner = (grad * slope_ref[rs, :]).astype(BF)
        inner_ref[rs, :] = inner
        bias += jnp.sum(inner.astype(F32), axis=0, keepdims=True)
        part_s[rs, :] = contract(inner, pack_ref[:, :model], 1, 1)
    bias_ref[...] = bias
    for f in range(2):
        here = slice(f * own, (f + 1) * own)
        mine_ref[here, :] = part_s[rows_at(2 * f + near, own), :].astype(BF)
        other_ref[here, :] = part_s[rows_at(2 * f + 1 - near, own), :].astype(BF)


def first_kernel(s_ref, a_ref, b_ref, second_ref, n_ref, r_ref, sums_ref, gains_ref, sent_ref, grad_ref):
    far = s_ref[0] // 2
    own = grad_ref.shape[0]
    gain = gains_ref[0:1, :]
    sums = [jnp.zeros(gain.shape, F32), jnp.zeros(gain.shape, F32)]
    for f in range(2):
        here = slice(f * own, (f + 1) * own)
        cot = second_ref[here, :] + (a_ref[here, :].astype(F32) + b_ref[here, :].astype(F32))
        n = n_ref[here, :]
        grad = pull_norm(n, r_ref[here, :1], gain, cot)

        @pl.when(far == f)
        def _():
            grad_ref[...] = grad

        sent_ref[here, :] = grad.astype(BF)
        sums[0] += jnp.sum(cot * n, axis=0, keepdims=True)
        sums[1] += jnp.sum(cot, axis=0, keepdims=True)
    sums = jnp.concatenate(sums + [sums_ref[...]], axis=0)
    high = sums.astype(BF).astype(F32)
    tail = jnp.concatenate([high, sums - high, jnp.zeros((8, sums.shape[1]), F32)], axis=0)
    sent_ref[2 * own :, :] = tail.astype(BF)


def mixed_kernel(s_ref, sent_ref, near_ref, mixed_ref, o_ref, bias_ref, aux_ref, do_ref, natural_ref, line_ref, grad_w_ref, sums_ref, all_s):
    near = s_ref[0] % 2
    rows, model = all_s.shape
    own = rows // 4
    for f in range(2):
        here = slice(f * own, (f + 1) * own)
        all_s[rows_at(2 * f + near, own), :] = sent_ref[here, :]
        all_s[rows_at(2 * f + 1 - near, own), :] = near_ref[here, :]
    grad = contract(o_ref[...], all_s[...], 1, 1).astype(BF)
    do_ref[...] = grad
    for h in range(natural_ref.shape[0]):
        do = grad[h * E : (h + 1) * E].astype(F32).T
        natural_ref[h] = do.astype(BF)
        line_ref[h, :, :E] = jnp.broadcast_to(jnp.sum(do * aux_ref[h, :, :E], axis=1, keepdims=True), (rows, E))
        line_ref[h, :, E:] = aux_ref[h, :, E:]
    grad_w_ref[...] = contract(mixed_ref[...], all_s[...], 1, 0)
    tail = sent_ref[2 * own :, :].astype(F32) + near_ref[2 * own :, :].astype(F32)
    rest = jnp.zeros((sums_ref.shape[0] - 5, model), F32)
    sums_ref[...] = jnp.concatenate([tail[:4] + tail[4:8], bias_ref[...], rest], axis=0)


def weight_kernel(s_ref, active_ref, second_ref, low_ref, inner_ref, out_ref):
    model = low_ref.shape[1]
    out_ref[:, :model] = contract(active_ref[...].astype(F32).T.astype(BF), second_ref[...], 1, 0).astype(BF)
    out_ref[:, model:] = contract(low_ref[...].astype(F32).T.astype(BF), inner_ref[...], 1, 0).astype(BF)


def join_kernel(half, s_ref, behind_ref, ahead_ref, up_ref, down_ref, up_out, down_out):
    if half:
        middle = up_ref.shape[0]
        up_out[:middle] = add(ahead_ref[:middle], up_ref[...])
        up_out[middle:] = ahead_ref[middle:]
        down_out[:middle] = behind_ref[:middle]
        down_out[middle:] = add(behind_ref[middle:], down_ref[...])
    else:
        up_out[...] = add(ahead_ref[...], up_ref[...])
        down_out[...] = add(behind_ref[...], down_ref[...])


def close_kernel(s_ref, part_ref, up_ref, down_ref, gq_ref, rows_ref, attn_ref, turned_ref, *refs):
    outs, (mine_ref, other_ref, project_ref, total_s, part_s) = refs[:-5], refs[-5:]
    near = s_ref[0] % 2
    rows, cols = part_s.shape[0], project_ref.shape[0]
    own = rows // 4
    width = gq_ref.shape[0]
    project_ref[:width] = gq_ref[...]
    for w in range(2):
        total = part_ref[w].astype(F32) + up_ref[w].astype(F32) + down_ref[w].astype(F32)
        project_ref[(1 + w) * width : (2 + w) * width] = total.astype(BF)
    total_s[...] = jnp.concatenate([contract(project_ref[...], rows_ref[...], 1, 0), attn_ref[...]], axis=0).T
    count = len(outs) - 1
    if count == 0:
        outs[0][...] = total_s[...].astype(BF)
    else:
        half = outs[0].shape[0]
        for i in range(2):
            at = pl.multiple_of(s_ref[count] * 2 * half + i * half, half)
            outs[i][...] = total_s[pl.ds(at, half), :].astype(BF)
        for i in range(1, count):
            outs[1 + i][...] = total_s[rows_at(s_ref[count - i], 2 * half), :].astype(BF)
    part_s[...] = contract(project_ref[...].astype(F32).T.astype(BF), turned_ref[:cols], 1, 0)
    for f in range(2):
        here = slice(f * own, (f + 1) * own)
        mine_ref[here, :] = part_s[rows_at(2 * f + near, own), :].astype(BF)
        other_ref[here, :] = part_s[rows_at(2 * f + 1 - near, own), :].astype(BF)


class Ring:
    def __init__(self, axis, total, size):
        self.axis, self.size = axis, size
        local = list(range(0, size, 2)) + list(range(size - 1 - size % 2, 0, -2))
        self.local = local
        self.up, self.down = [], []
        for base in range(0, total, size):
            for i in range(size):
                a, b = base + local[i], base + local[(i + 1) % size]
                self.up.append((a, b))
                self.down.append((b, a))

    def members(self, index, offsets):
        n = self.size
        mine = jnp.where(index % 2 == 0, index // 2, n - 1 - index // 2)
        place = (mine + jnp.array(offsets, jnp.int32)) % n
        return jnp.where(place < (n + 1) // 2, 2 * place, 2 * (n - 1 - place) + 1)

    def groups(self):
        if self.size == 1:
            return [[0]]
        half = self.size // 2
        return [[0]] + [[-k, k] for k in range(1, half)] + [[half]]

    def gather(self, x):
        pieces = [x]
        up = down = x
        for group in self.groups()[1:-1]:
            up, down = self.send_up(up), self.send_down(down)
            pieces += [up, down]
        return pieces + [self.send_up(halves(up, 0)[0]), self.send_down(halves(down, 0)[1])]

    def send_up(self, x):
        return lax.ppermute(x, self.axis, self.up)

    def send_down(self, x):
        return lax.ppermute(x, self.axis, self.down)


class RingSum:
    def __init__(self, ring):
        self.ring = ring

    def first(self, a, b):
        self.up, self.down, self.half = self.ring.send_up(a), self.ring.send_down(b), True

    def step(self, scalars, behind, ahead):
        kind = (behind.shape, BF)
        up, down = fused(
            functools.partial(join_kernel, self.half), [kind, kind], scalars, behind, ahead, self.up, self.down
        )
        self.up, self.down, self.half = self.ring.send_up(up), self.ring.send_down(down), False
        return up, down


def halves(x, axis):
    middle = x.shape[axis] // 2
    return lax.slice_in_dim(x, 0, middle, axis=axis), lax.slice_in_dim(x, middle, x.shape[axis], axis=axis)


def add(a, b):
    return (a.astype(F32) + b.astype(F32)).astype(BF)


def after(x, *earlier):
    return lax.optimization_barrier((x, *earlier))[0]


def spread_gather(x, axis, n):
    return lax.all_to_all(jnp.broadcast_to(x[None], (n,) + x.shape), axis, 0, 0, tiled=True)


def group_sum(x, axis, n):
    parts = lax.all_to_all(x.reshape(n, x.shape[0] // n, x.shape[1]), axis, 0, 0, tiled=True)
    return jnp.sum(parts.astype(F32), axis=0)


def high_low(x):
    high = x.astype(BF)
    return high, (x - high.astype(F32)).astype(BF)


class Quad:
    def __init__(self, axis):
        self.axis = axis
        index = lax.axis_index(axis)
        self.near, self.far = index % 2, index // 2
        self.flip_near = [(i, i ^ 1) for i in range(4)]
        self.flip_far = [(i, i ^ 2) for i in range(4)]

    def send_near(self, x):
        return lax.ppermute(x, self.axis, self.flip_near)

    def send_far(self, x):
        return lax.ppermute(x, self.axis, self.flip_far)


def shards(
    inputs,
    prev_logits,
    w_query,
    w_key,
    w_value,
    w_attn_out,
    w_ffn_in,
    ffn_bias,
    w_ffn_out,
    norm1_gain,
    norm1_shift,
    norm2_gain,
    norm2_shift,
    token_segment,
    segment_parent,
    out_grad,
    logit_grad,
):
    rows, heads, length = prev_logits.shape
    width = heads * E
    own, model = inputs.shape
    spread = length // rows
    nd = lax.axis_size("dp")
    share = model // nd
    data_index, tensor_index = lax.axis_index("dp"), lax.axis_index("tensor")
    tree_index, local_index = data_index // spread, data_index % spread
    nb = rows // BLOCK
    quad = Quad("tensor")
    ring, all_ring = Ring("dp", nd, spread), Ring("dp", nd, nd)
    by_ring = share % 32 == 0
    place = tensor_index.astype(jnp.int32).reshape(1)
    gains = jnp.stack([norm1_gain, norm1_shift, norm2_gain, norm2_shift])

    seg = lax.dynamic_slice_in_dim(token_segment, tree_index * length, length, 0)[::BLOCK]
    parents = lax.dynamic_slice_in_dim(segment_parent, tree_index, 1, 0)[0]
    seg_rows = lax.dynamic_slice_in_dim(seg, local_index * nb, nb, 0)
    labels = jnp.arange(parents.shape[0], dtype=jnp.int32)
    one = jnp.sum(jnp.where(seg_rows[:, None] == labels[None, :], parents[None, :], 0), axis=1)
    two = jnp.sum(jnp.where(one[:, None] == labels[None, :], parents[None, :], 0), axis=1)
    act = (
        (seg[None, :] == seg_rows[:, None])
        | (seg[None, :] == one[:, None])
        | (seg[None, :] == two[:, None])
    )
    act = act.astype(jnp.int32).reshape(-1)
    groups = ring.groups()
    order = [o for group in groups for o in group]
    sid = ring.members(local_index, order)

    pack_in = jnp.concatenate([w_ffn_in, ffn_bias[:, None]], axis=1)
    w_out = lax.all_gather(w_ffn_out, "dp", axis=0, tiled=True)
    if by_ring:
        (pack,) = fused(
            pack_kernel, [((share, 4 * width), BF)], place, *map(apart, (w_query, w_key, w_value, w_attn_out))
        )
        pieces = all_ring.gather(pack)
        pieces[2], pack_in = lax.optimization_barrier((pieces[2], pack_in))
        owners = [o for group in all_ring.groups() for o in group]
        owners = all_ring.members(data_index, owners)
    else:
        pack = jnp.concatenate([w_query, w_key, w_value, w_attn_out.T], axis=1)
        pieces = list(spread_gather(pack, "dp", nd).reshape(2, model // 2, 4 * width))
        owners = jnp.zeros((1,), jnp.int32)
    hidden_units = w_ffn_in.shape[1]
    pack_in = lax.all_gather(pack_in, "dp", axis=0, tiled=True)
    place = jnp.concatenate([place, owners])
    place, act, sid, gains = lax.optimization_barrier((place, act, sid, gains))
    near = quad.send_near(inputs)
    rows_of_four = [inputs, near, quad.send_far(inputs), quad.send_far(near)]
    rows_all, turned, q_t, q_n, kv_own = fused(
        functools.partial(project_kernel, len(pieces) - 1),
        [((rows, model), BF), ((4 * width, model), BF), ((width, rows), BF), ((heads, rows, E), BF), ((2, width, rows), BF)],
        place,
        *map(apart, pieces),
        *map(apart, rows_of_four),
        scratch=[((model, 4 * width), BF)],
    )
    out_own = turned[3 * width :]

    prev = apart(jnp.transpose(prev_logits, (1, 0, 2)))
    up_grad = apart(jnp.transpose(logit_grad, (1, 0, 2)))
    held = [[kv_own]]
    going_up = going_down = kv_own
    state = None
    for step, group in enumerate(groups):
        last = step + 1 == len(groups)
        if not last:
            if state is not None:
                going_up, going_down = lax.optimization_barrier((going_up, going_down, state[1]))[:2]
            if step + 2 == len(groups):
                held.append([apart(ring.send_up(going_up[:1])), apart(ring.send_down(going_down[1:]))])
            else:
                going_up, going_down = ring.send_up(going_up), ring.send_down(going_down)
                held.append([going_up, going_down])
        result = attend_forward(
            sid, order.index(group[0]), act, q_n, held[step], prev, state, last, 512
        )
        state = (result[0], result[-1])
        if step == 0:
            out_grad_far = quad.send_far(after(out_grad, q_t))
            state = (state[0], after(state[1], out_grad_far))
            near = quad.send_near(out_own)
            outs = [out_own, near, quad.send_far(out_own), quad.send_far(near)]
    logits, mixed, aux = result
    pack_in, w_out, *outs = (apart(after(w, mixed)) for w in (pack_in, w_out, *outs))

    pair = (2 * own, model)
    mixed_all = lax.all_gather(mixed, "tensor", axis=0, tiled=True)
    low, active, slope, first_n, first_r, mine, other = fused(
        feed_kernel,
        [((rows, model), BF), ((rows, model), BF), ((rows, model), F32), (pair, F32), ((2 * own, 128), F32)]
        + [(pair, BF)] * 2,
        place,
        mixed_all,
        rows_all,
        *outs,
        pack_in,
        w_out,
        gains,
        scratch=[((4 * width, model), BF), ((rows, model), F32), ((rows, model), F32), ((rows, 128), F32)],
    )
    mine = add(mine, quad.send_near(other))
    output, second, second_low, sums = fused(
        second_kernel,
        [((own, model), BF), (pair, F32), (pair, BF), ((2, model), F32)],
        place,
        mine,
        quad.send_far(mine),
        apart(first_n),
        apart(out_grad),
        apart(out_grad_far),
        gains,
    )
    second_all, inner, grad_bias, mine, other = fused(
        back_kernel,
        [((rows, model), BF), ((rows, model), BF), ((1, model), F32), (pair, BF), (pair, BF)],
        place,
        second_low,
        quad.send_near(second_low),
        slope,
        pack_in,
        w_out,
        scratch=[((rows, model), F32)],
    )
    mine = add(mine, quad.send_near(other))
    far = quad.send_far(mine)
    (weight_grads,) = fused(
        weight_kernel,
        [((model, 2 * model), BF)],
        place,
        active,
        second_all,
        low,
        inner,
    )
    far = after(far, weight_grads)
    weight_grads = lax.psum_scatter(weight_grads, "dp", scatter_dimension=0, tiled=True)

    sent, grad_first = fused(
        first_kernel,
        [((2 * own + 16, model), BF), ((own, model), F32)],
        place,
        mine,
        far,
        second,
        apart(first_n),
        apart(first_r),
        sums,
        gains,
    )
    received = quad.send_near(sent)
    grad_mixed, grad_mixed_n, aux, grad_w_attn, sums = fused(
        mixed_kernel,
        [
            ((width, rows), BF),
            ((heads, rows, E), BF),
            ((heads, rows, 128), F32),
            ((width, model), F32),
            ((8, model), F32),
        ],
        place,
        sent,
        received,
        apart(mixed),
        apart(out_own),
        grad_bias,
        apart(aux),
        scratch=[((rows, model), BF)],
    )

    doublings = iter([1 << i for i in range((nd - 1).bit_length())])

    def sums_step(sums):
        bit = next(doublings, None)
        if bit is None:
            return sums
        return sums + lax.ppermute(sums, "dp", [(i, i ^ bit) for i in range(nd)])

    state = None
    total_kv = RingSum(ring)
    steps = list(reversed(range(1, len(groups))))
    steps.append(0)
    for turn, step in enumerate(steps):
        result = attend_backward(
            sid,
            order.index(groups[step][0]),
            act,
            q_t,
            grad_mixed,
            q_n,
            grad_mixed_n,
            aux,
            held[step] if step + 1 == len(groups) else [apart(kv) for kv in held[step]],
            prev,
            up_grad,
            state,
            turn + 1 == len(steps),
            512,
        )
        state = (result[0], result[-1])
        if step == 0:
            part = result[1]
        elif step + 1 == len(groups):
            total_kv.first(*result[1:-1])
        else:
            sums = sums_step(sums)
            total_kv.step(after(place, sums), *result[1:-1])
    prev_grad, grad_query = result[0], result[-1]
    for _ in range(nd):
        sums = sums_step(sums)
    grad_w_out, grad_w_in = weight_grads[:, :model].astype(F32), weight_grads[:, model:].astype(F32)

    if by_ring:
        shapes = [((share // 2, 4 * width), BF)] * 2 + [((share, 4 * width), BF)] * (nd - 1)
    else:
        shapes = [((model, 4 * width), BF)]
    *parts, mine, other = fused(
        close_kernel,
        shapes + [(pair, BF), (pair, BF)],
        place,
        part,
        total_kv.up,
        total_kv.down,
        grad_query,
        rows_all,
        grad_w_attn,
        apart(turned),
        scratch=[((3 * width, rows), BF), ((model, 4 * width), F32), ((rows, model), F32)],
    )
    if by_ring:
        last_sum = RingSum(all_ring)
        last_sum.first(parts[0], parts[1])
    mine = add(mine, quad.send_near(other)).reshape(2, own, model)
    far = quad.send_far(lax.dynamic_index_in_dim(mine, 1 - quad.far, 0, keepdims=False))
    kept = lax.dynamic_index_in_dim(mine, quad.far, 0, keepdims=False)
    grad_inputs = grad_first + (kept.astype(F32) + far.astype(F32))
    if by_ring:
        for i in range(2, nd, 2):
            scalars = after(place, *((far,) if i == 4 else (grad_w_out, grad_w_in) if i == 6 else ()))
            last_sum.step(scalars, parts[i + 1], parts[i])
        grads = fused(
            finish_kernel,
            [((share, width), F32)] * 3 + [((width, share), F32)],
            place,
            parts[-1],
            last_sum.up,
            last_sum.down,
        )
    else:
        grads = group_sum(parts[0], "dp", nd)
        grads = [grads[:, i * width : (i + 1) * width] for i in range(4)]
        grads[3] = grads[3].T
    grad_bias = lax.dynamic_slice_in_dim(sums[4], data_index * (hidden_units // nd), hidden_units // nd, 0)
    return (
        output,
        jnp.transpose(logits, (1, 0, 2)),
        grad_inputs,
        jnp.transpose(prev_grad, (1, 0, 2)),
        *grads,
        grad_w_in,
        grad_bias,
        grad_w_out,
        sums[0],
        sums[1],
        sums[2],
        sums[3],
    )


def solution(mesh):
    placed = (
        P(("dp", "tensor"), None),
        P("dp", "tensor", None),
        P("dp", "tensor"),
        P("dp", "tensor"),
        P("dp", "tensor"),
        P("tensor", "dp"),
        P("dp", "tensor"),
        P(("tensor", "dp")),
        P(("tensor", "dp"), None),
        P(),
        P(),
        P(),
        P(),
        P(),
        P(),
        P(("dp", "tensor"), None),
        P("dp", "tensor", None),
    )
    return jax.shard_map(
        shards,
        mesh=mesh,
        in_specs=placed,
        out_specs=(
            P(("dp", "tensor"), None),
            P("dp", "tensor", None),
            P(("dp", "tensor"), None),
            P("dp", "tensor", None),
            P("dp", "tensor"),
            P("dp", "tensor"),
            P("dp", "tensor"),
            P("tensor", "dp"),
            P("dp", "tensor"),
            P(("tensor", "dp")),
            P(("tensor", "dp"), None),
            P(),
            P(),
            P(),
            P(),
        ),
        check_vma=False,
    )
```

```python
import functools
import math

import jax
import jax.numpy as jnp
from jax import lax
from jax.experimental import pallas as pl
from jax.experimental.pallas import tpu as pltpu
from jax.sharding import PartitionSpec as P

E = 64
SPARE = 6 << 20
TRUNK = 2048
BLOCK = 128
EPSILON = 1e-12
LOW = -1e30

BF = jnp.bfloat16
F32 = jnp.float32


def layer_norm(values, norm_gain, norm_shift):
    center = values - jnp.mean(values, axis=-1, keepdims=True)
    spread = jnp.mean(center * center, axis=-1, keepdims=True)
    return center * lax.rsqrt(spread + EPSILON) * norm_gain + norm_shift


def size_of(*arrays):
    return sum(math.prod(a.shape) * jnp.dtype(a.dtype).itemsize for a in arrays)


def apart(x):
    return pltpu.with_memory_space_constraint(x, pltpu.HBM)


def contract(a, b, da, db):
    return lax.dot_general(a, b, (((da,), (db,)), ((), ())), preferred_element_type=F32)


def block_mask(shard, rows, act_ref, q_blocks):
    nb = rows // BLOCK
    total_blocks = act_ref.shape[0] // nb
    parts = []
    for qi in q_blocks:
        flags = [act_ref[qi * total_blocks + shard * nb + ki].astype(F32) for ki in range(nb)]
        line = jnp.concatenate([jnp.full((1, BLOCK), f, F32) for f in flags], axis=1)
        parts.append(jnp.broadcast_to(line, (BLOCK, rows)))
    return jnp.concatenate(parts, axis=0)


def in_use(shard, rows, act_ref):
    nb = rows // BLOCK
    total_blocks = act_ref.shape[0] // nb
    flags = [act_ref[qi * total_blocks + shard * nb + ki] for qi in range(nb) for ki in range(nb)]
    return functools.reduce(jnp.maximum, flags) == 1


def tile_of(ref, head, shard, rows):
    return ref.at[head, :, pl.ds(pl.multiple_of(shard * rows, BLOCK), rows)]


def read_pieces(pieces, parted, refs):
    if parted:
        return [(lambda rs: refs[0][0, rs, :], lambda rs: refs[1][0, rs, :])], refs[2:]
    return [
        (lambda rs, ref=ref: ref[0, rs, :], lambda rs, ref=ref: ref[1, rs, :]) for ref in refs[:pieces]
    ], refs[pieces:]


def forward_kernel(first, last, pieces, parted, base, rc, *refs):
    sid_ref, act_ref, q_ref = refs[:3]
    readers, refs = read_pieces(pieces, parted, refs[3:])
    prev_ref, refs = refs[0], refs[1:]
    if not first:
        carry_in, refs = refs[1], refs[2:]
    logit_ref, refs = refs[0], refs[1:]
    if last:
        mix_ref, refs = refs[0], refs[1:]
    out_ref, m_s, acc_s, kv_s, prev_s, logit_s, in_sem, out_sem = refs
    heads, rows, _ = prev_ref.shape
    count = pieces * heads

    def incoming(i):
        tile = tile_of(prev_ref, i % heads, sid_ref[base + i // heads], rows)
        return pltpu.make_async_copy(tile, prev_s.at[i], in_sem.at[i])

    def outgoing(i):
        tile = tile_of(logit_ref, i % heads, sid_ref[base + i // heads], rows)
        return pltpu.make_async_copy(logit_s.at[i], tile, out_sem.at[i])

    def used(i):
        return in_use(sid_ref[base + i // heads], rows, act_ref)

    @pl.loop(0, count)
    def _(i):
        @pl.when(used(i))
        def _():
            incoming(i).start()

    for h in range(heads):
        feature = slice(h * E, (h + 1) * E)
        for p, (keys, values) in enumerate(readers):
            kv_s[p * heads + h, :E, :] = values(feature)
            kv_s[p * heads + h, E : 2 * E, :] = jnp.ones((E, rows), BF)
            kv_s[p * heads + h, 2 * E :, :] = keys(feature)
        if first:
            m_s[h] = jnp.full((rows, 1), LOW, F32)
            acc_s[h] = jnp.zeros((rows, 2 * E), F32)
        else:
            m_s[h] = carry_in[h, :, 96:97]
            acc_s[h] = carry_in[h]

    @pl.loop(0, count)
    def _(i):
        shard, h, here = sid_ref[base + i // heads], i % heads, used(i)

        @pl.when(here)
        def _():
            incoming(i).wait()

            for r0 in range(0, rows, min(rc, rows)):
                rs = slice(r0, r0 + min(rc, rows))
                on = block_mask(shard, rows, act_ref, range(r0 // BLOCK, rs.stop // BLOCK))
                s = contract(q_ref[h, rs, :], kv_s[i, 2 * E :, :], 1, 0) + prev_s[i, rs, :].astype(F32)
                logit_s[i, rs, :] = (s * on).astype(BF)
                s = s + (on - 1.0) * (-LOW)
                m_old = m_s[h, rs, :]
                m_new = jnp.maximum(m_old, jnp.max(s, axis=1, keepdims=True))
                weight = jnp.exp(s - m_new).astype(BF)
                fix = jnp.exp(m_old - m_new)
                m_s[h, rs, :] = m_new
                acc_s[h, rs, :] = acc_s[h, rs, :] * fix + contract(weight, kv_s[i, : 2 * E, :], 1, 1)

        @pl.when(jnp.logical_not(here))
        def _():
            logit_s[i] = jnp.zeros((rows, rows), BF)

        outgoing(i).start()

    for h in range(heads):
        if last:
            total = acc_s[h, :, E : E + 1]
            out = acc_s[h, :, :E] / total
            mix_ref[h * E : (h + 1) * E, :] = out.T.astype(BF)
            out_ref[h, :, :E] = out
            out_ref[h, :, E:] = jnp.broadcast_to(m_s[h] + jnp.log(total), (rows, 128 - E))
        else:
            out_ref[h, :, :96] = acc_s[h, :, :96]
            out_ref[h, :, 96:] = jnp.broadcast_to(m_s[h], (rows, 32))

    @pl.loop(0, count)
    def _(i):
        outgoing(i).wait()


def attend_forward(sid, base, act, q_n, kvs, prev, carry, last, rc=256):
    heads, rows, length = prev.shape
    first, parted = carry is None, kvs[0].shape[0] == 1
    pieces = 1 if parted else len(kvs)
    scalars = pl.BlockSpec(memory_space=pltpu.SMEM)
    whole = pl.BlockSpec(memory_space=pltpu.VMEM)
    left = pl.BlockSpec(memory_space=pltpu.HBM)
    in_specs = [scalars, scalars, whole] + [whole] * len(kvs) + [left]
    args = [sid, act, q_n, *kvs, prev]
    aliases = {}
    if not first:
        aliases = {len(args): 0}
        in_specs += [left, whole]
        args += list(carry)
    out_shape = [jax.ShapeDtypeStruct((heads, rows, length), BF)]
    if last:
        out_shape.append(jax.ShapeDtypeStruct((heads * E, rows), BF))
    out_shape.append(jax.ShapeDtypeStruct((heads, rows, 128), F32))
    work = heads * pieces * rows * rows
    return pl.pallas_call(
        functools.partial(forward_kernel, first, last, pieces, parted, base, rc),
        out_shape=out_shape,
        in_specs=in_specs,
        out_specs=[left] + [whole] * (len(out_shape) - 1),
        scratch_shapes=[
            pltpu.VMEM((heads, rows, 1), F32),
            pltpu.VMEM((heads, rows, 128), F32),
            pltpu.VMEM((pieces * heads, 3 * E, rows), BF),
            pltpu.VMEM((pieces * heads, rows, rows), BF),
            pltpu.VMEM((pieces * heads, rows, rows), BF),
            pltpu.SemaphoreType.DMA((pieces * heads,)),
            pltpu.SemaphoreType.DMA((pieces * heads,)),
        ],
        input_output_aliases=aliases,
        cost_estimate=pl.CostEstimate(flops=4 * E * work, transcendentals=work, bytes_accessed=4 * work),
        compiler_params=pltpu.CompilerParams(
            vmem_limit_bytes=6 * work + 16 * heads * rows * 128 * 4 + SPARE
        ),
    )(*args)


def backward_kernel(first, last, pieces, parted, base, rc, *refs):
    sid_ref, act_ref, q_ref, do_ref, q_s, do_s, aux_ref = refs[:7]
    readers, refs = read_pieces(pieces, parted, refs[7:])
    prev_ref, up_ref, refs = refs[0], refs[1], refs[2:]
    if not first:
        gq_in, refs = refs[1], refs[2:]
    outputs = 2 if parted else pieces
    pg_ref, gkv_refs = refs[0], refs[1 : 1 + outputs]
    gq_ref, gq_s, p_s, kv_s, gkv_s, prev_s, up_s, pg_s, prev_sem, up_sem, out_sem = refs[1 + outputs :]
    heads, rows, _ = prev_ref.shape
    count = pieces * heads

    def incoming(i):
        at = i % heads, sid_ref[base + i // heads], rows
        return (
            pltpu.make_async_copy(tile_of(prev_ref, *at), prev_s.at[i], prev_sem.at[i]),
            pltpu.make_async_copy(tile_of(up_ref, *at), up_s.at[i], up_sem.at[i]),
        )

    def outgoing(i):
        tile = tile_of(pg_ref, i % heads, sid_ref[base + i // heads], rows)
        return pltpu.make_async_copy(pg_s.at[i], tile, out_sem.at[i])

    def used(i):
        return in_use(sid_ref[base + i // heads], rows, act_ref)

    @pl.loop(0, count)
    def _(i):
        @pl.when(used(i))
        def _():
            for copy in incoming(i):
                copy.start()

    for h in range(heads):
        feature = slice(h * E, (h + 1) * E)
        gq_s[h] = jnp.zeros((rows, E), F32) if first else gq_in[h]
        for p, (keys, values) in enumerate(readers):
            kv_s[p * heads + h, :E, :] = keys(feature)
            kv_s[p * heads + h, E:, :] = values(feature)

    @pl.loop(0, count)
    def _(i):
        shard, h, here = sid_ref[base + i // heads], i % heads, used(i)
        feature = pl.ds(pl.multiple_of(h * E, E), E)

        @pl.when(here)
        def _():
            for copy in incoming(i):
                copy.wait()
            chunk = min(rc, rows)

            @pl.loop(0, rows // chunk)
            def _(r):
                rs = pl.ds(pl.multiple_of(r * chunk, chunk), chunk)
                blocks = chunk // BLOCK
                on = block_mask(shard, rows, act_ref, [r * blocks + b for b in range(blocks)])
                s = contract(q_s[h, rs, :], kv_s[i, :E, :], 1, 0) + prev_s[i, rs, :].astype(F32)
                weight = jnp.exp(s - aux_ref[h, rs, E : E + 1] + (on - 1.0) * (-LOW))
                dp = contract(do_s[h, rs, :], kv_s[i, E:, :], 1, 0)
                upper = up_s[i, rs, :].astype(F32) * on
                pg_s[i, rs, :] = (weight * (dp - aux_ref[h, rs, :1]) + upper).astype(BF)
                p_s[rs, :] = weight.astype(BF)

            gkv_s[i, :E, :] = contract(q_ref[feature, :], pg_s[i], 1, 0).astype(BF)
            gkv_s[i, E:, :] = contract(do_ref[feature, :], p_s[...], 1, 0).astype(BF)
            gq_s[h] += contract(pg_s[i], kv_s[i, :E, :], 1, 1)

        @pl.when(jnp.logical_not(here))
        def _():
            pg_s[i] = jnp.zeros((rows, rows), BF)
            gkv_s[i] = jnp.zeros((2 * E, rows), BF)

        outgoing(i).start()

    for h in range(heads):
        feature = slice(h * E, (h + 1) * E)
        for p in range(pieces):
            for w in range(2):
                part = gkv_s[p * heads + h, w * E : (w + 1) * E, :]
                if parted:
                    gkv_refs[w][0, feature, :] = part
                else:
                    gkv_refs[p][w, feature, :] = part
        if last:
            gq_ref[feature, :] = (gq_s[h] * (E ** (-0.5))).T.astype(BF)
        else:
            gq_ref[h] = gq_s[h]

    @pl.loop(0, count)
    def _(i):
        outgoing(i).wait()


def attend_backward(sid, base, act, q_t, do_t, q_n, do_n, aux, kvs, prev, up, carry, last, rc=256):
    heads, rows, length = prev.shape
    first, parted = carry is None, kvs[0].shape[0] == 1
    pieces = 1 if parted else len(kvs)
    scalars = pl.BlockSpec(memory_space=pltpu.SMEM)
    whole = pl.BlockSpec(memory_space=pltpu.VMEM)
    left = pl.BlockSpec(memory_space=pltpu.HBM)
    in_specs = [scalars, scalars] + [whole] * (5 + len(kvs)) + [left, left]
    args = [sid, act, q_t, do_t, q_n, do_n, aux, *kvs, prev, up]
    aliases = {}
    if not first:
        aliases = {len(args): 0}
        in_specs += [left, whole]
        args += list(carry)
    out_shape = [jax.ShapeDtypeStruct((heads, rows, length), BF)]
    out_shape += [jax.ShapeDtypeStruct(kv.shape, BF) for kv in kvs]
    if last:
        out_shape.append(jax.ShapeDtypeStruct((heads * E, rows), BF))
    else:
        out_shape.append(jax.ShapeDtypeStruct((heads, rows, E), F32))
    work = heads * pieces * rows * rows
    return pl.pallas_call(
        functools.partial(backward_kernel, first, last, pieces, parted, base, rc),
        out_shape=out_shape,
        in_specs=in_specs,
        out_specs=[left] + [whole] * (len(kvs) + 1),
        scratch_shapes=[
            pltpu.VMEM((heads, rows, E), F32),
            pltpu.VMEM((rows, rows), BF),
            pltpu.VMEM((pieces * heads, 2 * E, rows), BF),
            pltpu.VMEM((pieces * heads, 2 * E, rows), BF),
            pltpu.VMEM((pieces * heads, rows, rows), BF),
            pltpu.VMEM((pieces * heads, rows, rows), BF),
            pltpu.VMEM((pieces * heads, rows, rows), BF),
            pltpu.SemaphoreType.DMA((pieces * heads,)),
            pltpu.SemaphoreType.DMA((pieces * heads,)),
            pltpu.SemaphoreType.DMA((pieces * heads,)),
        ],
        input_output_aliases=aliases,
        cost_estimate=pl.CostEstimate(flops=10 * E * work, transcendentals=work, bytes_accessed=6 * work),
        compiler_params=pltpu.CompilerParams(
            vmem_limit_bytes=8 * work + 16 * heads * rows * 128 * 4 + SPARE
        ),
    )(*args)


def fused(body, shapes, scalars, *arrays, scratch=(), flops=0):
    shapes = [jax.ShapeDtypeStruct(shape, kind) for shape, kind in shapes]
    scratch = [pltpu.VMEM(shape, kind) for shape, kind in scratch]
    return pl.pallas_call(
        body,
        out_shape=shapes,
        in_specs=[pl.BlockSpec(memory_space=pltpu.SMEM)]
        + [pl.BlockSpec(memory_space=pltpu.VMEM)] * len(arrays),
        out_specs=[pl.BlockSpec(memory_space=pltpu.VMEM)] * len(shapes),
        scratch_shapes=scratch,
        cost_estimate=pl.CostEstimate(flops=flops, transcendentals=0, bytes_accessed=1 << 20),
        compiler_params=pltpu.CompilerParams(vmem_limit_bytes=size_of(*arrays, *shapes, *scratch) + SPARE),
    )(scalars, *arrays)


def rows_at(index, count):
    return pl.ds(pl.multiple_of(index * count, count), count)


def normalize(values):
    center = values - jnp.mean(values, axis=-1, keepdims=True)
    r = lax.rsqrt(jnp.mean(center * center, axis=-1, keepdims=True) + EPSILON)
    return center * r, r


def pull_norm(n, r, gain, cotangent):
    dn = cotangent * gain
    return r * (dn - jnp.mean(dn, axis=-1, keepdims=True) - n * jnp.mean(dn * n, axis=-1, keepdims=True))


def pack_kernel(s_ref, query_ref, key_ref, value_ref, out_ref, pack_ref):
    turned = out_ref[...].astype(F32).T
    parts = [ref[...].astype(F32) for ref in (query_ref, key_ref, value_ref)]
    pack_ref[...] = jnp.concatenate([*parts, turned], axis=1).astype(BF)


def finish_kernel(s_ref, part_ref, up_ref, down_ref, query_ref, key_ref, value_ref, out_ref):
    width = query_ref.shape[1]
    total = part_ref[...].astype(F32) + (up_ref[...].astype(F32) + down_ref[...].astype(F32))
    for i, ref in enumerate((query_ref, key_ref, value_ref)):
        ref[...] = total[:, i * width : (i + 1) * width]
    out_ref[...] = total[:, 3 * width :].T


def project_kernel(pieces, s_ref, *refs):
    w_refs, x_refs = refs[: pieces + 1], refs[pieces + 1 : pieces + 5]
    rows_ref, turned_ref, q_ref, natural_ref, kv_ref, w_s = refs[pieces + 5 :]
    share, own = w_refs[0].shape[0], x_refs[0].shape[0]
    width = q_ref.shape[0]
    if pieces == 1:
        share *= 2
    for i in range(pieces - 1):
        w_s[rows_at(s_ref[1 + i], share), :] = w_refs[i][...]
    last = s_ref[pieces] * share
    half = share // 2
    w_s[pl.ds(pl.multiple_of(last, half), half), :] = w_refs[pieces - 1][...]
    w_s[pl.ds(pl.multiple_of(last + half, half), half), :] = w_refs[pieces][...]
    for i in range(4):
        rows_ref[rows_at(s_ref[0] ^ i, own), :] = x_refs[i][...]
    turned_ref[...] = w_s[...].astype(F32).T.astype(BF)
    projected = contract(turned_ref[: 3 * width, :], rows_ref[...], 1, 1)
    q_ref[...] = (projected[:width] * (E ** (-0.5))).astype(BF)
    for h in range(width // E):
        natural_ref[h] = (projected[h * E : (h + 1) * E] * (E ** (-0.5))).T.astype(BF)
    kv_ref[0] = projected[width : 2 * width].astype(BF)
    kv_ref[1] = projected[2 * width :].astype(BF)


def feed_kernel(s_ref, mixed_ref, x_ref, o0, o1, o2, o3, pack_ref, out_ref, gains_ref, low_ref, active_ref, slope_ref, n_ref, r_ref, mine_ref, other_ref, o_s, part_s, n_s, r_s):
    index = s_ref[0]
    near = index % 2
    rows, model = x_ref.shape
    own, width = rows // 4, o0.shape[0]
    for i, ref in enumerate((o0, o1, o2, o3)):
        o_s[rows_at(index ^ i, width), :] = ref[...]
    bias = pack_ref[:, model:].astype(F32).T
    chunk = min(256, rows)
    for r0 in range(0, rows, chunk):
        rs = slice(r0, r0 + chunk)
        attended = contract(mixed_ref[:, rs].astype(F32).T.astype(BF), o_s[...], 1, 0)
        n, r = normalize(x_ref[rs, :].astype(F32) + attended)
        n_s[rs, :] = n
        r_s[rs, :] = jnp.broadcast_to(r, (chunk, 128))
        low = (n * gains_ref[0:1, :] + gains_ref[1:2, :]).astype(BF)
        low_ref[rs, :] = low
        inner = contract(low, pack_ref[:, :model], 1, 0) + bias
        below = 0.5 + 0.5 * lax.erf(inner * (0.5**0.5))
        density = jnp.exp(-0.5 * inner * inner) * 0.3989422804014327
        slope_ref[rs, :] = below + inner * density
        active = (inner * below).astype(BF)
        active_ref[rs, :] = active
        part_s[rs, :] = contract(active, out_ref[...], 1, 0)
    for f in range(2):
        here = slice(f * own, (f + 1) * own)
        n_ref[here, :] = n_s[rows_at(2 * f + near, own), :]
        r_ref[here, :] = r_s[rows_at(2 * f + near, own), :]
        mine_ref[here, :] = part_s[rows_at(2 * f + near, own), :].astype(BF)
        other_ref[here, :] = part_s[rows_at(2 * f + 1 - near, own), :].astype(BF)


def second_kernel(s_ref, a_ref, b_ref, n_ref, cot_own, cot_far, gains_ref, result_ref, second_ref, low_ref, sums_ref):
    far = s_ref[0] // 2
    own = cot_own.shape[0]
    gain1, shift1, gain2, shift2 = (gains_ref[i : i + 1, :] for i in range(4))
    sums = [jnp.zeros(gain2.shape, F32), jnp.zeros(gain2.shape, F32)]
    for f in range(2):
        here = slice(f * own, (f + 1) * own)
        hidden = n_ref[here, :] * gain1 + shift1
        n, r = normalize(hidden + (a_ref[here, :].astype(F32) + b_ref[here, :].astype(F32)))
        cot = jnp.where(far == f, cot_own[...].astype(F32), cot_far[...].astype(F32))

        @pl.when(far == f)
        def _():
            result_ref[...] = (n * gain2 + shift2).astype(BF)

        second = pull_norm(n, r, gain2, cot)
        second_ref[here, :] = second
        low_ref[here, :] = second.astype(BF)
        sums[0] += jnp.sum(cot * n, axis=0, keepdims=True)
        sums[1] += jnp.sum(cot, axis=0, keepdims=True)
    sums_ref[0:1, :] = sums[0]
    sums_ref[1:2, :] = sums[1]


def back_kernel(s_ref, low_ref, near_ref, slope_ref, pack_ref, out_ref, all_ref, inner_ref, bias_ref, mine_ref, other_ref, part_s):
    near = s_ref[0] % 2
    rows, model = slope_ref.shape
    own = rows // 4
    for f in range(2):
        here = slice(f * own, (f + 1) * own)
        all_ref[rows_at(2 * f + near, own), :] = low_ref[here, :]
        all_ref[rows_at(2 * f + 1 - near, own), :] = near_ref[here, :]
    chunk = min(256, rows)
    bias = jnp.zeros((1, model), F32)
    for r0 in range(0, rows, chunk):
        rs = slice(r0, r0 + chunk)
        grad = contract(all_ref[rs, :], out_ref[...], 1, 1).astype(BF).astype(F32)
        inner = (grad * slope_ref[rs, :]).astype(BF)
        inner_ref[rs, :] = inner
        bias += jnp.sum(inner.astype(F32), axis=0, keepdims=True)
        part_s[rs, :] = contract(inner, pack_ref[:, :model], 1, 1)
    bias_ref[...] = bias
    for f in range(2):
        here = slice(f * own, (f + 1) * own)
        mine_ref[here, :] = part_s[rows_at(2 * f + near, own), :].astype(BF)
        other_ref[here, :] = part_s[rows_at(2 * f + 1 - near, own), :].astype(BF)


def first_kernel(s_ref, a_ref, b_ref, second_ref, n_ref, r_ref, sums_ref, gains_ref, sent_ref, grad_ref):
    far = s_ref[0] // 2
    own = grad_ref.shape[0]
    gain = gains_ref[0:1, :]
    sums = [jnp.zeros(gain.shape, F32), jnp.zeros(gain.shape, F32)]
    for f in range(2):
        here = slice(f * own, (f + 1) * own)
        cot = second_ref[here, :] + (a_ref[here, :].astype(F32) + b_ref[here, :].astype(F32))
        n = n_ref[here, :]
        grad = pull_norm(n, r_ref[here, :1], gain, cot)

        @pl.when(far == f)
        def _():
            grad_ref[...] = grad

        sent_ref[here, :] = grad.astype(BF)
        sums[0] += jnp.sum(cot * n, axis=0, keepdims=True)
        sums[1] += jnp.sum(cot, axis=0, keepdims=True)
    sums = jnp.concatenate(sums + [sums_ref[...]], axis=0)
    high = sums.astype(BF).astype(F32)
    tail = jnp.concatenate([high, sums - high, jnp.zeros((8, sums.shape[1]), F32)], axis=0)
    sent_ref[2 * own :, :] = tail.astype(BF)


def mixed_kernel(s_ref, sent_ref, near_ref, mixed_ref, o_ref, bias_ref, aux_ref, do_ref, natural_ref, line_ref, grad_w_ref, sums_ref, all_s):
    near = s_ref[0] % 2
    rows, model = all_s.shape
    own = rows // 4
    for f in range(2):
        here = slice(f * own, (f + 1) * own)
        all_s[rows_at(2 * f + near, own), :] = sent_ref[here, :]
        all_s[rows_at(2 * f + 1 - near, own), :] = near_ref[here, :]
    grad = contract(o_ref[...], all_s[...], 1, 1).astype(BF)
    do_ref[...] = grad
    for h in range(natural_ref.shape[0]):
        do = grad[h * E : (h + 1) * E].astype(F32).T
        natural_ref[h] = do.astype(BF)
        line_ref[h, :, :E] = jnp.broadcast_to(jnp.sum(do * aux_ref[h, :, :E], axis=1, keepdims=True), (rows, E))
        line_ref[h, :, E:] = aux_ref[h, :, E:]
    grad_w_ref[...] = contract(mixed_ref[...], all_s[...], 1, 0)
    tail = sent_ref[2 * own :, :].astype(F32) + near_ref[2 * own :, :].astype(F32)
    rest = jnp.zeros((sums_ref.shape[0] - 5, model), F32)
    sums_ref[...] = jnp.concatenate([tail[:4] + tail[4:8], bias_ref[...], rest], axis=0)


def weight_kernel(s_ref, active_ref, second_ref, low_ref, inner_ref, out_ref):
    model = low_ref.shape[1]
    out_ref[:, :model] = contract(active_ref[...].astype(F32).T.astype(BF), second_ref[...], 1, 0).astype(BF)
    out_ref[:, model:] = contract(low_ref[...].astype(F32).T.astype(BF), inner_ref[...], 1, 0).astype(BF)


def join_kernel(half, s_ref, behind_ref, ahead_ref, up_ref, down_ref, up_out, down_out):
    if half:
        middle = up_ref.shape[0]
        up_out[:middle] = add(ahead_ref[:middle], up_ref[...])
        up_out[middle:] = ahead_ref[middle:]
        down_out[:middle] = behind_ref[:middle]
        down_out[middle:] = add(behind_ref[middle:], down_ref[...])
    else:
        up_out[...] = add(ahead_ref[...], up_ref[...])
        down_out[...] = add(behind_ref[...], down_ref[...])


def close_kernel(s_ref, part_ref, up_ref, down_ref, gq_ref, rows_ref, attn_ref, turned_ref, *refs):
    outs, (mine_ref, other_ref, project_ref, total_s, part_s) = refs[:-5], refs[-5:]
    near = s_ref[0] % 2
    rows, cols = part_s.shape[0], project_ref.shape[0]
    own = rows // 4
    width = gq_ref.shape[0]
    project_ref[:width] = gq_ref[...]
    for w in range(2):
        total = part_ref[w].astype(F32) + up_ref[w].astype(F32) + down_ref[w].astype(F32)
        project_ref[(1 + w) * width : (2 + w) * width] = total.astype(BF)
    total_s[...] = jnp.concatenate([contract(project_ref[...], rows_ref[...], 1, 0), attn_ref[...]], axis=0).T
    count = len(outs) - 1
    if count == 0:
        outs[0][...] = total_s[...].astype(BF)
    else:
        half = outs[0].shape[0]
        for i in range(2):
            at = pl.multiple_of(s_ref[count] * 2 * half + i * half, half)
            outs[i][...] = total_s[pl.ds(at, half), :].astype(BF)
        for i in range(1, count):
            outs[1 + i][...] = total_s[rows_at(s_ref[count - i], 2 * half), :].astype(BF)
    part_s[...] = contract(project_ref[...].astype(F32).T.astype(BF), turned_ref[:cols], 1, 0)
    for f in range(2):
        here = slice(f * own, (f + 1) * own)
        mine_ref[here, :] = part_s[rows_at(2 * f + near, own), :].astype(BF)
        other_ref[here, :] = part_s[rows_at(2 * f + 1 - near, own), :].astype(BF)


class Ring:
    def __init__(self, axis, total, size):
        self.axis, self.size = axis, size
        local = list(range(0, size, 2)) + list(range(size - 1 - size % 2, 0, -2))
        self.local = local
        self.up, self.down = [], []
        for base in range(0, total, size):
            for i in range(size):
                a, b = base + local[i], base + local[(i + 1) % size]
                self.up.append((a, b))
                self.down.append((b, a))

    def members(self, index, offsets):
        n = self.size
        mine = jnp.where(index % 2 == 0, index // 2, n - 1 - index // 2)
        place = (mine + jnp.array(offsets, jnp.int32)) % n
        return jnp.where(place < (n + 1) // 2, 2 * place, 2 * (n - 1 - place) + 1)

    def groups(self):
        if self.size == 1:
            return [[0]]
        half = self.size // 2
        return [[0]] + [[-k, k] for k in range(1, half)] + [[half]]

    def gather(self, x):
        pieces = [x]
        up = down = x
        for group in self.groups()[1:-1]:
            up, down = self.send_up(up), self.send_down(down)
            pieces += [up, down]
        return pieces + [self.send_up(halves(up, 0)[0]), self.send_down(halves(down, 0)[1])]

    def send_up(self, x):
        return lax.ppermute(x, self.axis, self.up)

    def send_down(self, x):
        return lax.ppermute(x, self.axis, self.down)


class RingSum:
    def __init__(self, ring):
        self.ring = ring

    def first(self, a, b):
        self.up, self.down, self.half = self.ring.send_up(a), self.ring.send_down(b), True

    def step(self, scalars, behind, ahead):
        kind = (behind.shape, BF)
        up, down = fused(
            functools.partial(join_kernel, self.half), [kind, kind], scalars, behind, ahead, self.up, self.down
        )
        self.up, self.down, self.half = self.ring.send_up(up), self.ring.send_down(down), False
        return up, down


def halves(x, axis):
    middle = x.shape[axis] // 2
    return lax.slice_in_dim(x, 0, middle, axis=axis), lax.slice_in_dim(x, middle, x.shape[axis], axis=axis)


def add(a, b):
    return (a.astype(F32) + b.astype(F32)).astype(BF)


def after(x, *earlier):
    return lax.optimization_barrier((x, *earlier))[0]


def spread_gather(x, axis, n):
    return lax.all_to_all(jnp.broadcast_to(x[None], (n,) + x.shape), axis, 0, 0, tiled=True)


def group_sum(x, axis, n):
    parts = lax.all_to_all(x.reshape(n, x.shape[0] // n, x.shape[1]), axis, 0, 0, tiled=True)
    return jnp.sum(parts.astype(F32), axis=0)


def high_low(x):
    high = x.astype(BF)
    return high, (x - high.astype(F32)).astype(BF)


class Quad:
    def __init__(self, axis):
        self.axis = axis
        index = lax.axis_index(axis)
        self.near, self.far = index % 2, index // 2
        self.flip_near = [(i, i ^ 1) for i in range(4)]
        self.flip_far = [(i, i ^ 2) for i in range(4)]

    def send_near(self, x):
        return lax.ppermute(x, self.axis, self.flip_near)

    def send_far(self, x):
        return lax.ppermute(x, self.axis, self.flip_far)


def shards(
    inputs,
    prev_logits,
    w_query,
    w_key,
    w_value,
    w_attn_out,
    w_ffn_in,
    ffn_bias,
    w_ffn_out,
    norm1_gain,
    norm1_shift,
    norm2_gain,
    norm2_shift,
    token_segment,
    segment_parent,
    out_grad,
    logit_grad,
):
    rows, heads, length = prev_logits.shape
    width = heads * E
    own, model = inputs.shape
    spread = length // rows
    nd = lax.axis_size("dp")
    share = model // nd
    data_index, tensor_index = lax.axis_index("dp"), lax.axis_index("tensor")
    tree_index, local_index = data_index // spread, data_index % spread
    nb = rows // BLOCK
    quad = Quad("tensor")
    ring, all_ring = Ring("dp", nd, spread), Ring("dp", nd, nd)
    by_ring = share % 32 == 0
    place = tensor_index.astype(jnp.int32).reshape(1)
    gains = jnp.stack([norm1_gain, norm1_shift, norm2_gain, norm2_shift])

    seg = lax.dynamic_slice_in_dim(token_segment, tree_index * length, length, 0)[::BLOCK]
    parents = lax.dynamic_slice_in_dim(segment_parent, tree_index, 1, 0)[0]
    seg_rows = lax.dynamic_slice_in_dim(seg, local_index * nb, nb, 0)
    labels = jnp.arange(parents.shape[0], dtype=jnp.int32)
    one = jnp.sum(jnp.where(seg_rows[:, None] == labels[None, :], parents[None, :], 0), axis=1)
    two = jnp.sum(jnp.where(one[:, None] == labels[None, :], parents[None, :], 0), axis=1)
    act = (
        (seg[None, :] == seg_rows[:, None])
        | (seg[None, :] == one[:, None])
        | (seg[None, :] == two[:, None])
    )
    act = act.astype(jnp.int32).reshape(-1)
    groups = ring.groups()
    order = [o for group in groups for o in group]
    sid = ring.members(local_index, order)

    pack_in = jnp.concatenate([w_ffn_in, ffn_bias[:, None]], axis=1)
    w_out = lax.all_gather(w_ffn_out, "dp", axis=0, tiled=True)
    if by_ring:
        (pack,) = fused(
            pack_kernel, [((share, 4 * width), BF)], place, *map(apart, (w_query, w_key, w_value, w_attn_out))
        )
        pieces = all_ring.gather(pack)
        pieces[2], pack_in = lax.optimization_barrier((pieces[2], pack_in))
        owners = [o for group in all_ring.groups() for o in group]
        owners = all_ring.members(data_index, owners)
    else:
        pack = jnp.concatenate([w_query, w_key, w_value, w_attn_out.T], axis=1)
        pieces = list(spread_gather(pack, "dp", nd).reshape(2, model // 2, 4 * width))
        owners = jnp.zeros((1,), jnp.int32)
    hidden_units = w_ffn_in.shape[1]
    pack_in = lax.all_gather(pack_in, "dp", axis=0, tiled=True)
    place = jnp.concatenate([place, owners])
    place, act, sid, gains = lax.optimization_barrier((place, act, sid, gains))
    near = quad.send_near(inputs)
    rows_of_four = [inputs, near, quad.send_far(inputs), quad.send_far(near)]
    rows_all, turned, q_t, q_n, kv_own = fused(
        functools.partial(project_kernel, len(pieces) - 1),
        [((rows, model), BF), ((4 * width, model), BF), ((width, rows), BF), ((heads, rows, E), BF), ((2, width, rows), BF)],
        place,
        *map(apart, pieces),
        *map(apart, rows_of_four),
        scratch=[((model, 4 * width), BF)],
    )
    out_own = turned[3 * width :]

    prev = apart(jnp.transpose(prev_logits, (1, 0, 2)))
    up_grad = apart(jnp.transpose(logit_grad, (1, 0, 2)))
    held = [[kv_own]]
    going_up = going_down = kv_own
    state = None
    for step, group in enumerate(groups):
        last = step + 1 == len(groups)
        if not last:
            if state is not None:
                going_up, going_down = lax.optimization_barrier((going_up, going_down, state[1]))[:2]
            if step + 2 == len(groups):
                held.append([apart(ring.send_up(going_up[:1])), apart(ring.send_down(going_down[1:]))])
            else:
                going_up, going_down = ring.send_up(going_up), ring.send_down(going_down)
                held.append([going_up, going_down])
        result = attend_forward(
            sid, order.index(group[0]), act, q_n, held[step], prev, state, last, 512
        )
        state = (result[0], result[-1])
        if step == 0:
            out_grad_far = quad.send_far(after(out_grad, q_t))
            state = (state[0], after(state[1], out_grad_far))
            near = quad.send_near(out_own)
            outs = [out_own, near, quad.send_far(out_own), quad.send_far(near)]
    logits, mixed, aux = result
    pack_in, w_out, *outs = (apart(after(w, mixed)) for w in (pack_in, w_out, *outs))

    pair = (2 * own, model)
    mixed_all = lax.all_gather(mixed, "tensor", axis=0, tiled=True)
    low, active, slope, first_n, first_r, mine, other = fused(
        feed_kernel,
        [((rows, model), BF), ((rows, model), BF), ((rows, model), F32), (pair, F32), ((2 * own, 128), F32)]
        + [(pair, BF)] * 2,
        place,
        mixed_all,
        rows_all,
        *outs,
        pack_in,
        w_out,
        gains,
        scratch=[((4 * width, model), BF), ((rows, model), F32), ((rows, model), F32), ((rows, 128), F32)],
    )
    mine = add(mine, quad.send_near(other))
    output, second, second_low, sums = fused(
        second_kernel,
        [((own, model), BF), (pair, F32), (pair, BF), ((2, model), F32)],
        place,
        mine,
        quad.send_far(mine),
        apart(first_n),
        apart(out_grad),
        apart(out_grad_far),
        gains,
    )
    second_all, inner, grad_bias, mine, other = fused(
        back_kernel,
        [((rows, model), BF), ((rows, model), BF), ((1, model), F32), (pair, BF), (pair, BF)],
        place,
        second_low,
        quad.send_near(second_low),
        slope,
        pack_in,
        w_out,
        scratch=[((rows, model), F32)],
    )
    mine = add(mine, quad.send_near(other))
    far = quad.send_far(mine)
    (weight_grads,) = fused(
        weight_kernel,
        [((model, 2 * model), BF)],
        place,
        active,
        second_all,
        low,
        inner,
    )
    far = after(far, weight_grads)
    weight_grads = lax.psum_scatter(weight_grads, "dp", scatter_dimension=0, tiled=True)

    sent, grad_first = fused(
        first_kernel,
        [((2 * own + 16, model), BF), ((own, model), F32)],
        place,
        mine,
        far,
        second,
        apart(first_n),
        apart(first_r),
        sums,
        gains,
    )
    received = quad.send_near(sent)
    grad_mixed, grad_mixed_n, aux, grad_w_attn, sums = fused(
        mixed_kernel,
        [
            ((width, rows), BF),
            ((heads, rows, E), BF),
            ((heads, rows, 128), F32),
            ((width, model), F32),
            ((8, model), F32),
        ],
        place,
        sent,
        received,
        apart(mixed),
        apart(out_own),
        grad_bias,
        apart(aux),
        scratch=[((rows, model), BF)],
    )

    doublings = iter([1 << i for i in range((nd - 1).bit_length())])

    def sums_step(sums):
        bit = next(doublings, None)
        if bit is None:
            return sums
        return sums + lax.ppermute(sums, "dp", [(i, i ^ bit) for i in range(nd)])

    state = None
    total_kv = RingSum(ring)
    steps = list(reversed(range(1, len(groups))))
    steps.append(0)
    for turn, step in enumerate(steps):
        result = attend_backward(
            sid,
            order.index(groups[step][0]),
            act,
            q_t,
            grad_mixed,
            q_n,
            grad_mixed_n,
            aux,
            held[step] if step + 1 == len(groups) else [apart(kv) for kv in held[step]],
            prev,
            up_grad,
            state,
            turn + 1 == len(steps),
            512,
        )
        state = (result[0], result[-1])
        if step == 0:
            part = result[1]
        elif step + 1 == len(groups):
            total_kv.first(*result[1:-1])
        else:
            sums = sums_step(sums)
            total_kv.step(after(place, sums), *result[1:-1])
    prev_grad, grad_query = result[0], result[-1]
    for _ in range(nd):
        sums = sums_step(sums)
    grad_w_out, grad_w_in = weight_grads[:, :model].astype(F32), weight_grads[:, model:].astype(F32)

    if by_ring:
        shapes = [((share // 2, 4 * width), BF)] * 2 + [((share, 4 * width), BF)] * (nd - 1)
    else:
        shapes = [((model, 4 * width), BF)]
    *parts, mine, other = fused(
        close_kernel,
        shapes + [(pair, BF), (pair, BF)],
        place,
        part,
        total_kv.up,
        total_kv.down,
        grad_query,
        rows_all,
        grad_w_attn,
        apart(turned),
        scratch=[((3 * width, rows), BF), ((model, 4 * width), F32), ((rows, model), F32)],
    )
    if by_ring:
        last_sum = RingSum(all_ring)
        last_sum.first(parts[0], parts[1])
    mine = add(mine, quad.send_near(other)).reshape(2, own, model)
    far = quad.send_far(lax.dynamic_index_in_dim(mine, 1 - quad.far, 0, keepdims=False))
    kept = lax.dynamic_index_in_dim(mine, quad.far, 0, keepdims=False)
    grad_inputs = grad_first + (kept.astype(F32) + far.astype(F32))
    if by_ring:
        for i in range(2, nd, 2):
            scalars = after(place, *((far, grad_w_out, grad_w_in) if i == 6 else ()))
            last_sum.step(scalars, parts[i + 1], parts[i])
        grads = fused(
            finish_kernel,
            [((share, width), F32)] * 3 + [((width, share), F32)],
            place,
            parts[-1],
            last_sum.up,
            last_sum.down,
        )
    else:
        grads = group_sum(parts[0], "dp", nd)
        grads = [grads[:, i * width : (i + 1) * width] for i in range(4)]
        grads[3] = grads[3].T
    grad_bias = lax.dynamic_slice_in_dim(sums[4], data_index * (hidden_units // nd), hidden_units // nd, 0)
    return (
        output,
        jnp.transpose(logits, (1, 0, 2)),
        grad_inputs,
        jnp.transpose(prev_grad, (1, 0, 2)),
        *grads,
        grad_w_in,
        grad_bias,
        grad_w_out,
        sums[0],
        sums[1],
        sums[2],
        sums[3],
    )


def solution(mesh):
    placed = (
        P(("dp", "tensor"), None),
        P("dp", "tensor", None),
        P("dp", "tensor"),
        P("dp", "tensor"),
        P("dp", "tensor"),
        P("tensor", "dp"),
        P("dp", "tensor"),
        P(("tensor", "dp")),
        P(("tensor", "dp"), None),
        P(),
        P(),
        P(),
        P(),
        P(),
        P(),
        P(("dp", "tensor"), None),
        P("dp", "tensor", None),
    )
    return jax.shard_map(
        shards,
        mesh=mesh,
        in_specs=placed,
        out_specs=(
            P(("dp", "tensor"), None),
            P("dp", "tensor", None),
            P(("dp", "tensor"), None),
            P("dp", "tensor", None),
            P("dp", "tensor"),
            P("dp", "tensor"),
            P("dp", "tensor"),
            P("tensor", "dp"),
            P("dp", "tensor"),
            P(("tensor", "dp")),
            P(("tensor", "dp"), None),
            P(),
            P(),
            P(),
            P(),
        ),
        check_vma=False,
    )
```
